128 devices in a mesh: zone: 4 (over y), blk: 32 (over z, x, core).
Axes of the slice: x: 4, y: 4, z: 4, core: 2. Of those that a mesh axis runs over, the one named last changes fastest.
Arguments:
- flow_state: float32 [4, 8192, 7, 256], P('zone', 'blk'), may hold values from -6 to 6
- right_side: float32 [4, 8192, 7, 256], P('zone', 'blk'), may hold values from -6 to 6
- inv_diag: float32 [4, 8192, 7, 7, 256], P('zone', 'blk'), may hold values from -0.2 to 1, as said below
- face_coef: float32 [4, 8192, 4, 256], P('zone', 'blk'), may hold values from 0.05 to 0.25
- face_jacobian: float32 [4, 7, 7], replicated, may hold values from -2 to 2
- hole_owner: int32 [16384, 1], P(('zone', 'blk')), may hold values from 0 to 127; in each aligned block of 128 rows (0 to 127, 128 to 255, ...) at most 2 rows name the same one
- source_row: int32 [16384], P(('zone', 'blk')), may hold values from 0 to 255
- target_row: int32 [16384], P(('zone', 'blk')), may hold values from 0 to 255
- block_device: int32 [128], replicated, may hold values from 0 to 127, each once
Outputs:
- relaxed: float32 [4, 8192, 7, 256], P('zone', 'blk')
The draws below stay inside these ranges and needn't reach their ends.
Inputs may be any that keep to these rules, and one draw needn't show every extreme that they name: `hole_owner`: among the 128 holes of one device, no block is named more than 2 times, and some block exactly 2 times. `block_device`: each device index appears once. `inv_diag`: diagonal entries lie in 0.5 to 1.0, others in -0.2 to 0.2.
All inputs are finite; a program needn't handle non-finite values.
Results may differ from the reference program's by a relative error of at most 0.0001.
Values sent between devices are 32-bit elements; how exact they have to be, the bound alone decides.
No kernel may reach another device: no remote copies, remote signals or barrier semaphores. Data moves between devices by JAX's collectives and lax.ppermute only.
A program may use at most 128 MiB of HBM per device.

```python
import math
import jax
import jax.numpy as jnp
import numpy as np
from jax import lax

NVAR = 7
SCOLS = 256
SROWS = 256
HOLE_DEV = 128
SWEEPS = 2
CAP = 2
ROWS = 8192
HOLES = 16384
N_ZONE = 4
N_BLK = 32


def draw_inv_diag(key, part):
    first, second = jax.random.split(key)
    shape = (N_ZONE, ROWS, NVAR, NVAR, SCOLS)
    diagonal = jax.random.uniform(first, shape, jnp.float32, 0.5, 1.0)
    others = jnp.clip(0.08 * jax.random.normal(second, shape, jnp.float32), -0.2, 0.2)
    identity = jnp.eye(NVAR, dtype=jnp.float32)[None, None, :, :, None]
    return identity * diagonal + (1.0 - identity) * others


def place_ends(array, own_key, low, high):
    index_at = [jax.random.randint(jax.random.fold_in(own_key, axis), (), 0, length) for axis, length in enumerate(array.shape)]
    main_axis = array.shape.index(max(array.shape))
    next_to = index_at[:main_axis] + [(index_at[main_axis] + 1) % array.shape[main_axis]] + index_at[main_axis + 1:]
    return array.at[tuple(index_at)].set(low).at[tuple(next_to)].set(high)


def block_levels(key, shape, shards, low, top_value):
    loudness, own = 1.0, jax.random.fold_in(key, 6)
    for position, shards_of in shards:
        steps = jnp.exp(jax.random.uniform(jax.random.fold_in(own, position), (shards_of,), jnp.float32, low / len(shards), top_value / len(shards)))
        loudness = loudness * jnp.repeat(steps, shape[position] // shards_of).reshape([-1 if axis == position else 1 for axis in range(len(shape))])
    return loudness


def routed_block(key, own, number, rows, count, top, limit, skew):
    sequence = jax.random.permutation(key, count)
    heavy_load, usual = load_shares(count, rows * top, limit, skew, True), load_shares(count, rows * top, limit, skew, False)
    places = jnp.arange(count)

    def named(tallies, rotation):
        used = int((tallies > 0).sum())
        fixed = max(1, used // 4)
        moved = fixed + (places - fixed + rotation * (used - fixed)) % max(1, count - fixed)
        return jnp.zeros((count,), jnp.int32).at[sequence[jnp.where(places < fixed, places, moved)]].set(jnp.asarray(tallies, jnp.int32))

    tallies = jnp.where(number % 4 == 0, named(heavy_load, number // 4), named(usual, number - number // 4 - 1))
    mixed = jax.random.permutation(jax.random.fold_in(own, 3), count)
    donor, sink = mixed[0:count // 2 * 2:2], mixed[1:count // 2 * 2:2]
    slack = jnp.minimum(tallies[donor] - 1, limit - tallies[sink]) // 2
    slack = jnp.where((donor == sequence[0]) | (sink == sequence[0]) | (tallies[sink] == 0), 0, jnp.maximum(slack, 0))
    moved = jax.random.randint(jax.random.fold_in(own, 4), (count // 2,), 0, 1 << 20) % (slack + 1)
    tallies = tallies.at[donor].add(-moved).at[sink].add(moved)
    members = jnp.searchsorted(jnp.cumsum(tallies), jnp.arange(rows * top), side="right").astype(jnp.int32)
    table = members.reshape(top, rows).T
    table = table[jax.random.permutation(jax.random.fold_in(own, 1), rows)]
    rotation = jax.random.randint(jax.random.fold_in(own, 2), (rows, 1), 0, top)
    return jnp.take_along_axis(table, (jnp.arange(top)[None, :] + rotation) % top, axis=1)


def load_shares(number_of, total, limit, lean, full):
    weights = [(1 << 20) // math.isqrt(rank ** lean) + 1 for rank in range(1, number_of + 1)]
    largest = limit if full else min(limit, max(-(-total // number_of), total * weights[0] // sum(weights)))
    least = 1 if total - largest >= number_of - 1 else 0
    counts, spare = [largest] + [least] * (number_of - 1), total - largest - least * (number_of - 1)
    while spare > 0:
        candidates = [i for i in range(1, number_of) if counts[i] < largest] or [i for i in range(1, number_of) if counts[i] < limit]
        pool, left = sum([weights[i] for i in candidates]), spare
        for i in candidates:
            addition = min(limit - counts[i], max(1, left * weights[i] // pool), spare)
            counts[i] = counts[i] + addition
            spare = spare - addition
    return np.array(counts)


def gaussian(own_key, dims, spread, reach, cuts=(), kind=jnp.bfloat16):
    array = spread * jax.random.normal(own_key, dims, jnp.float32)
    if cuts:
        array = array * block_levels(own_key, dims, cuts, -0.22, 0.18)
    return jnp.clip(array, -reach, reach).astype(kind)


def setup_inputs(seed: int = 0) -> dict:
    splits = jax.random.split(jax.random.key(seed), 10)
    flow_state = gaussian(splits[0], (N_ZONE, ROWS, NVAR, SCOLS), 1.0, 6.0, ((0, 4), (1, 32)), jnp.float32)
    right_side = gaussian(splits[1], (N_ZONE, ROWS, NVAR, SCOLS), 1.0, 6.0, ((0, 4), (1, 32)), jnp.float32)
    inv_diag = draw_inv_diag(jax.random.fold_in(splits[9], 71), 0)
    face_coef = jnp.clip(jnp.exp(math.log(0.25) - 1.609438 * jax.random.uniform(splits[3], (N_ZONE, ROWS, 4, SCOLS), jnp.float32) ** block_levels(splits[3], (N_ZONE, ROWS, 4, SCOLS), ((0, 4), (1, 32)), -0.2, 0.2)), 0.05, 0.25)
    face_jacobian = gaussian(splits[4], (4, NVAR, NVAR), NVAR ** -0.5, 2.0, (), jnp.float32)
    hole_owner_keys = jax.random.split(jax.random.fold_in(splits[5], 1), HOLES // HOLE_DEV)
    hole_owner_turns = jax.random.permutation(jax.random.fold_in(splits[5], 3), HOLES // HOLE_DEV)
    hole_owner = jax.vmap(lambda own, number: routed_block(jax.random.fold_in(splits[5], 2), own, number, HOLE_DEV, N_ZONE * N_BLK, 1, CAP, 2))(hole_owner_keys, hole_owner_turns).reshape((HOLES, 1))
    source_row = place_ends(jax.random.randint(splits[6], (HOLES,), 0, SROWS), jax.random.fold_in(splits[6], 1), 0, SROWS - 1).astype(jnp.int32)
    target_row = place_ends(jax.random.randint(splits[7], (HOLES,), 0, SROWS), jax.random.fold_in(splits[7], 1), 0, SROWS - 1).astype(jnp.int32)
    block_device = jax.random.permutation(splits[8], N_ZONE * N_BLK).astype(jnp.int32)
    return dict(flow_state=flow_state, right_side=right_side, inv_diag=inv_diag, face_coef=face_coef, face_jacobian=face_jacobian, hole_owner=hole_owner, source_row=source_row, target_row=target_row, block_device=block_device)


def neighbour_sum(padded, face_coef, face_jacobian):
    shifted = (padded[:-2, :, 1:-1], padded[2:, :, 1:-1], padded[1:-1, :, :-2], padded[1:-1, :, 2:])
    coupled_sum = None
    for direction in range(4):
        applied = jnp.einsum("ij,rjc->ric", face_jacobian[direction], shifted[direction], precision=lax.Precision.HIGHEST)
        term = face_coef[:, direction][:, None, :] * applied
        coupled_sum = term if coupled_sum is None else coupled_sum + term
    return coupled_sum


def reference(flow_state, right_side, inv_diag, face_coef, face_jacobian, hole_owner, source_row, target_row, block_device):
    devices = N_ZONE * N_BLK
    flat = flow_state.reshape(devices, SROWS, NVAR * SCOLS)
    sender = (jnp.arange(HOLES, dtype=jnp.int32) // HOLE_DEV).astype(jnp.int32)
    target = block_device[hole_owner[:, 0]].astype(jnp.int32)
    source = jnp.zeros_like(flat)
    source = source.at[target, target_row].add(flat[sender, source_row])
    source = source.at[sender, source_row].add(-flat[target, target_row])
    base = right_side + source.reshape(N_ZONE, ROWS, NVAR, SCOLS)

    def zone_sweeps(pieces):
        state_now, zone_base, zone_inv, zone_coef = pieces
        for sweep_index in range(SWEEPS):
            padded = jnp.pad(state_now, ((1, 1), (0, 0), (1, 1)))
            coupled_sum = neighbour_sum(padded, zone_coef, face_jacobian)
            state_now = jnp.sum(zone_inv * (zone_base - coupled_sum)[:, None, :, :], axis=2)
        return state_now

    return lax.map(zone_sweeps, (flow_state, base, inv_diag, face_coef))
```

```python
import functools

import jax
import jax.numpy as jnp
from jax import lax
from jax.experimental import pallas as pl
from jax.experimental.pallas import tpu as pltpu
from jax.sharding import PartitionSpec as P

NV = 7
LANES = 128
AXES = ("zone", "blk")
F32 = jnp.float32
VMEM = pltpu.VMEM
MIB = 1 << 20


def params(mib):
    return pltpu.CompilerParams(vmem_limit_bytes=mib * MIB)


def cost(flops, bytes_accessed):
    return pl.CostEstimate(flops=flops, bytes_accessed=bytes_accessed, transcendentals=0)


def whole(space):
    return pl.BlockSpec(memory_space=space)


def relayout_kernel(flow, right, coef, inv, flow_s, right_s, coef_s, inv_s, scr):
    rows = flow.shape[0]

    def turn(slot, load, count, put):
        for h in range(2):
            for r in range(rows):
                scr[slot + h, pl.ds(8 * r, count), :] = load(r, h)
        for h in range(2):
            for v in range(count):
                put(v, h, scr[slot + h, pl.ds(v, rows, stride=8), :])

    def put_to(ref):
        def put(v, h, val):
            ref[2 * v + h] = val

        return put

    half = lambda h: pl.ds(LANES * h, LANES)
    turn(0, lambda r, h: flow[r, :, half(h)], NV, put_to(flow_s))
    turn(2, lambda r, h: right[r, :, half(h)], NV, put_to(right_s))
    turn(4, lambda r, h: coef[r, :, half(h)], 4, put_to(coef_s))
    for i in range(NV):

        def put_inv(v, h, val, i=i):
            inv_s[0, 2 * (NV * i + v) + h] = val

        turn(6 + 2 * i, lambda r, h, i=i: inv[r, i, :, half(h)], NV, put_inv)


def relayout(flow, right, coef, inv):
    rows = flow.shape[0]
    tiles = rows // 8
    shapes = ((2 * NV, rows, LANES), (2 * NV, rows, LANES), (8, rows, LANES), (tiles, 2 * NV * NV, 8, LANES))
    return pl.pallas_call(
        relayout_kernel,
        grid=(tiles,),
        in_specs=[
            pl.BlockSpec((8, NV, 256), lambda t: (t, 0, 0)),
            pl.BlockSpec((8, NV, 256), lambda t: (t, 0, 0)),
            pl.BlockSpec((8, 4, 256), lambda t: (t, 0, 0)),
            pl.BlockSpec((8, NV, NV, 256), lambda t: (t, 0, 0, 0)),
        ],
        out_specs=[
            pl.BlockSpec((2 * NV, 8, LANES), lambda t: (0, t, 0)),
            pl.BlockSpec((2 * NV, 8, LANES), lambda t: (0, t, 0)),
            pl.BlockSpec((8, 8, LANES), lambda t: (0, t, 0)),
            pl.BlockSpec((1, 2 * NV * NV, 8, LANES), lambda t: (t, 0, 0, 0)),
        ],
        out_shape=[jax.ShapeDtypeStruct(s, F32) for s in shapes],
        scratch_shapes=[VMEM((6 + 2 * NV, 64, LANES), F32)],
        compiler_params=params(16),
        cost_estimate=cost(10_000_000, 38_000_000),
        name="relayout",
    )(flow, right, coef, inv)


def coupled(state, row, coef, jac):
    lane = lax.broadcasted_iota(jnp.int32, (8, LANES), 1)
    out = [[None, None] for _ in range(NV)]
    for direction in range(4):
        cells = []
        for v in range(NV):
            if direction == 0:
                pair = [state[2 * v + h, pl.ds(row - 1, 8), :] for h in range(2)]
            elif direction == 1:
                pair = [state[2 * v + h, pl.ds(row + 1, 8), :] for h in range(2)]
            else:
                mid = [state[2 * v + h, pl.ds(row, 8), :] for h in range(2)]
                if direction == 2:
                    left, right = (pltpu.roll(m, 1, 1) for m in mid)
                    pair = [jnp.where(lane == 0, 0.0, left), jnp.where(lane == 0, left, right)]
                else:
                    left, right = (pltpu.roll(m, LANES - 1, 1) for m in mid)
                    pair = [jnp.where(lane == LANES - 1, right, left), jnp.where(lane == LANES - 1, 0.0, right)]
            cells.append(pair)
        for i in range(NV):
            sums = [None, None]
            for j in range(NV):
                factor = jac[(direction * NV + i) * NV + j]
                for h in range(2):
                    term = factor * cells[j][h]
                    sums[h] = term if j == 0 else sums[h] + term
            for h in range(2):
                term = coef(direction, h) * sums[h]
                out[i][h] = term if direction == 0 else out[i][h] + term
    return out


def apply_inv(inv, cells):
    out = [[None, None] for _ in range(NV)]
    for i in range(NV):
        for h in range(2):
            total = None
            for j in range(NV):
                term = inv(i, j, h) * cells[j][h]
                total = term if j == 0 else total + term
            out[i][h] = total
    return out


def first_kernel(parity, flow_s, right_s, coef_s, jac, halo_a, halo_b, start_s, state):
    tiles = right_s.shape[1] // 8
    even = parity[0] == 0
    for n in range(2 * NV):
        a, b = halo_a[n : n + 1, :], halo_b[n : n + 1, :]
        state[n, 7:8, :] = jnp.where(even, b, a)
        state[n, 8 + 8 * tiles : 9 + 8 * tiles, :] = jnp.where(even, a, b)
        state[n, 8 : 8 + 8 * tiles, :] = flow_s[n]

    def step(t, carry):
        row = pl.multiple_of(8 * t, 8)
        sums = coupled(state, row + 8, lambda d, h: coef_s[2 * d + h, pl.ds(row, 8), :], jac)
        for v in range(NV):
            for h in range(2):
                n = 2 * v + h
                start_s[n, pl.ds(row, 8), :] = right_s[n, pl.ds(row, 8), :] - sums[v][h]
        return carry

    lax.fori_loop(0, tiles, step, 0)


def first_sum(parity, flow_s, right_s, coef_s, jac, halo_a, halo_b):
    rows = flow_s.shape[1]
    return pl.pallas_call(
        first_kernel,
        in_specs=[whole(pltpu.SMEM)] + [whole(VMEM)] * 6,
        out_specs=whole(VMEM),
        out_shape=jax.ShapeDtypeStruct(flow_s.shape, F32),
        scratch_shapes=[VMEM((2 * NV, rows + 16, LANES), F32)],
        compiler_params=params(20),
        cost_estimate=cost(30_000_000, 8_000_000),
        name="first_sum",
    )(parity, flow_s, right_s, coef_s, jac, halo_a, halo_b)


def gather_kernel(sent, asked, flow, message):
    def step(d, carry):
        for part, table in enumerate((sent, asked)):
            for k in range(2):
                row = jnp.maximum(table[2 * d + k] - 1, 0)
                for h in range(2):
                    start = 28 * part + 14 * k + NV * h
                    message[d, start : start + NV, :] = flow[row, :, LANES * h : LANES * (h + 1)]
        return carry

    lax.fori_loop(0, message.shape[0], step, 0, unroll=2)


def gather(sent, asked, flow, devices):
    return pl.pallas_call(
        gather_kernel,
        in_specs=[whole(pltpu.SMEM), whole(pltpu.SMEM), whole(VMEM)],
        out_specs=whole(VMEM),
        out_shape=jax.ShapeDtypeStruct((devices, 8 * NV, LANES), F32),
        compiler_params=params(12),
        cost_estimate=cost(1_000_000, 6_000_000),
        name="gather",
    )(sent, asked, flow)


def scatter_kernel(parity, sent, asked, message, start_lo, start_hi, inv_lo, inv_hi, source, edge_a, edge_b):
    groups = source.shape[1] // 8

    def clear(g, carry):
        for h in range(2):
            source[h, pl.ds(pl.multiple_of(8 * g, 8), 8), :] = jnp.zeros((8, LANES), F32)
        return carry

    lax.fori_loop(0, groups, clear, 0, unroll=8)

    def step(d, carry):
        for part, table in enumerate((asked, sent)):
            for k in range(2):
                row = pl.multiple_of(8 * table[2 * d + k], 8)
                for h in range(2):
                    start = 28 * part + 14 * k + NV * h
                    value = message[d, start : start + NV, :]
                    old = source[h, pl.ds(row, NV), :]
                    source[h, pl.ds(row, NV), :] = old + value if part == 0 else old - value
        return carry

    lax.fori_loop(0, message.shape[0], step, 0, unroll=2)
    even = parity[0] == 0
    edges = []
    for start, inv, tile, sub in ((start_lo, inv_lo, 0, 0), (start_hi, inv_hi, groups // 8 - 2, 7)):
        cells = [
            [start[2 * v + h] + source[h, pl.ds(64 * tile + 8 + v, 8, stride=8), :] for h in range(2)]
            for v in range(NV)
        ]
        relaxed = apply_inv(lambda i, j, h, inv=inv: inv[0, 2 * (NV * i + j) + h], cells)
        edges.append([relaxed[v][h][sub : sub + 1, :] for v in range(NV) for h in range(2)])
    for n in range(2 * NV):
        top, bottom = edges[0][n], edges[1][n]
        edge_a[n : n + 1, :] = jnp.where(even, bottom, top)
        edge_b[n : n + 1, :] = jnp.where(even, top, bottom)


def scatter(parity, sent, asked, message, start_s, inv_s):
    rows = start_s.shape[1]
    last = rows // 8 - 1
    smem = pl.BlockSpec(memory_space=pltpu.SMEM)
    return pl.pallas_call(
        scatter_kernel,
        grid=(1,),
        in_specs=[
            smem,
            smem,
            smem,
            pl.BlockSpec(message.shape, lambda g: (0, 0, 0)),
            pl.BlockSpec((2 * NV, 8, LANES), lambda g: (0, 0, 0)),
            pl.BlockSpec((2 * NV, 8, LANES), lambda g: (0, last, 0)),
            pl.BlockSpec((1, 2 * NV * NV, 8, LANES), lambda g: (0, 0, 0, 0)),
            pl.BlockSpec((1, 2 * NV * NV, 8, LANES), lambda g: (last, 0, 0, 0)),
        ],
        out_specs=[
            pl.BlockSpec((2, 8 * (rows + 8), LANES), lambda g: (0, 0, 0)),
            pl.BlockSpec((2 * NV, LANES), lambda g: (0, 0)),
            pl.BlockSpec((2 * NV, LANES), lambda g: (0, 0)),
        ],
        out_shape=[
            jax.ShapeDtypeStruct((2, 8 * (rows + 8), LANES), F32),
            jax.ShapeDtypeStruct((2 * NV, LANES), F32),
            jax.ShapeDtypeStruct((2 * NV, LANES), F32),
        ],
        compiler_params=params(20),
        cost_estimate=cost(2_000_000, 7_000_000),
        name="scatter",
    )(parity, sent, asked, message, start_s, start_s, inv_s, inv_s)


RING = 4


def sweeps_kernel(source, start_s, right_s, coef_s, jac, inv_s, out, state, turned, ring, sems):
    tiles = start_s.shape[1] // 8

    def fetch(t):
        slot = lax.rem(t, RING)
        return pltpu.make_async_copy(inv_s.at[t], ring.at[slot], sems.at[slot])

    for t in range(RING - 1):
        fetch(t).start()
    for n in range(2 * NV):
        state[n, 0:8, :] = jnp.zeros((8, LANES), F32)
        state[n, 8 + 8 * tiles : 16 + 8 * tiles, :] = jnp.zeros((8, LANES), F32)

    def added(t, v, h):
        return source[h, pl.ds(64 * t + 8 + v, 8, stride=8), :]

    def inverse(t):
        slot = lax.rem(t, RING)
        return lambda i, j, h: ring[slot, 2 * (NV * i + j) + h]

    def sweep_one(t):
        row = pl.multiple_of(8 * t, 8)
        cells = [[start_s[2 * v + h, pl.ds(row, 8), :] + added(t, v, h) for h in range(2)] for v in range(NV)]
        relaxed = apply_inv(inverse(t), cells)
        for v in range(NV):
            for h in range(2):
                state[2 * v + h, pl.ds(row + 8, 8), :] = relaxed[v][h]

    def sweep_two(t):
        row = pl.multiple_of(8 * t, 8)
        sums = coupled(state, row + 8, lambda d, h: coef_s[2 * d + h, pl.ds(row, 8), :], jac)
        cells = [
            [right_s[2 * v + h, pl.ds(row, 8), :] + added(t, v, h) - sums[v][h] for h in range(2)]
            for v in range(NV)
        ]
        relaxed = apply_inv(inverse(t), cells)
        for h in range(2):
            for v in range(NV):
                turned[h, pl.ds(v, 8, stride=8), :] = relaxed[v][h]
            for r in range(8):
                out[row + r, :, LANES * h : LANES * (h + 1)] = turned[h, 8 * r : 8 * r + NV, :]

    fetch(0).wait()
    sweep_one(0)

    def step(t, carry):
        fetch(t).wait()
        sweep_one(t)
        sweep_two(t - 1)

        @pl.when(t + RING - 1 < tiles)
        def _():
            fetch(t + RING - 1).start()

        return carry

    fetch(RING - 1).start()
    lax.fori_loop(1, tiles, step, 0)
    sweep_two(tiles - 1)


def sweeps(source, start_s, right_s, coef_s, jac, inv_s):
    rows = start_s.shape[1]
    return pl.pallas_call(
        sweeps_kernel,
        in_specs=[whole(VMEM)] * 5 + [whole(pl.ANY)],
        out_specs=whole(VMEM),
        out_shape=jax.ShapeDtypeStruct((rows, NV, 2 * LANES), F32),
        scratch_shapes=[
            VMEM((2 * NV, rows + 16, LANES), F32),
            VMEM((2, 64, LANES), F32),
            VMEM((RING, 2 * NV * NV, 8, LANES), F32),
            pltpu.SemaphoreType.DMA((RING,)),
        ],
        compiler_params=params(28),
        cost_estimate=cost(45_000_000, 24_000_000),
        name="sweeps",
    )(source, start_s, right_s, coef_s, jac, inv_s)


def edge_kernel(parity, relaxed, coef, jac, inv, halo_a, halo_b, out, scr):
    low = pl.program_id(0) == 0
    use_a = (parity[0] == 0) != low
    sub = jnp.where(low, 0, 7)
    base = jnp.where(low, 0, NV * NV)
    place = lax.broadcasted_iota(jnp.int32, (8, LANES), 0) == sub
    cells = []
    for v in range(NV):
        pair = []
        for h in range(2):
            n = 2 * v + h
            row = jnp.where(use_a, halo_a[n : n + 1, :], halo_b[n : n + 1, :])
            pair.append(jnp.where(place, jnp.broadcast_to(row, (8, LANES)), 0.0))
        cells.append(pair)
    sums = []
    for i in range(NV):
        pair = []
        for h in range(2):
            total = None
            for j in range(NV):
                term = jac[base + NV * i + j] * cells[j][h]
                total = term if j == 0 else total + term
            factor = jnp.where(low, coef[h], coef[2 + h])
            pair.append(factor * total)
        sums.append(pair)
    change = apply_inv(lambda i, j, h: inv[0, 2 * (NV * i + j) + h], sums)
    for h in range(2):
        for v in range(NV):
            scr[v : v + 1, :] = jnp.sum(change[v][h], axis=0, keepdims=True)
        out[0, :, LANES * h : LANES * (h + 1)] = relaxed[0, :, LANES * h : LANES * (h + 1)] - scr[0:NV, :]


def edge_rows(parity, relaxed, coef_s, jac, inv_s, halo_a, halo_b):
    rows = relaxed.shape[0]
    last = rows // 8 - 1
    return pl.pallas_call(
        edge_kernel,
        grid=(2,),
        in_specs=[
            pl.BlockSpec(memory_space=pltpu.SMEM),
            pl.BlockSpec((1, NV, 2 * LANES), lambda g: (g * (rows - 1), 0, 0)),
            pl.BlockSpec((8, 8, LANES), lambda g: (0, g * last, 0)),
            pl.BlockSpec((4 * NV * NV, 8, LANES), lambda g: (0, 0, 0)),
            pl.BlockSpec((1, 2 * NV * NV, 8, LANES), lambda g: (g * last, 0, 0, 0)),
            pl.BlockSpec((2 * NV, LANES), lambda g: (0, 0)),
            pl.BlockSpec((2 * NV, LANES), lambda g: (0, 0)),
        ],
        out_specs=pl.BlockSpec((1, NV, 2 * LANES), lambda g: (g * (rows - 1), 0, 0)),
        out_shape=jax.ShapeDtypeStruct(relaxed.shape, F32),
        scratch_shapes=[VMEM((8, LANES), F32)],
        input_output_aliases={1: 0},
        compiler_params=params(8),
        cost_estimate=cost(100_000, 900_000),
        name="edge_rows",
    )(parity, relaxed, coef_s, jac, inv_s, halo_a, halo_b)


def exchange(edge_a, edge_b):
    size = lax.axis_size("blk")
    pairs_a = [(i, i ^ 1) for i in range(size)]
    pairs_b = [(i, i - 1 if i % 2 == 0 else i + 1) for i in range(1, size - 1)]
    return lax.ppermute(edge_a, "blk", pairs_a), lax.ppermute(edge_b, "blk", pairs_b)


def slot_tables(hole_owner, source_row, target_row, block_device, devices):
    device_seq = jnp.arange(devices, dtype=jnp.int32)
    target = jnp.sum(jnp.where(hole_owner == device_seq[None, :], block_device[None, :], 0), axis=1)
    hot = (target[:, None] == device_seq[None, :]).astype(jnp.int32)
    rank = jnp.sum((jnp.cumsum(hot, axis=0) - hot) * hot, axis=1)
    slot = 2 * target + rank
    place = (slot[None, :] == jnp.arange(2 * devices, dtype=jnp.int32)[:, None]).astype(jnp.int32)
    return jnp.sum(place * (source_row + 1)[None, :], axis=1), jnp.sum(place * (target_row + 1)[None, :], axis=1)


def body(flow_state, right_side, inv_diag, face_coef, face_jacobian, hole_owner, source_row, target_row, block_device):
    devices = lax.axis_size("zone") * lax.axis_size("blk")
    flow = flow_state[0]
    rows = flow.shape[0]
    parity = (lax.axis_index("blk") % 2).astype(jnp.int32).reshape(1)
    sent, asking = slot_tables(hole_owner, source_row, target_row, block_device, devices)
    asked = lax.all_to_all(asking.reshape(devices, 1, 2), AXES, split_axis=0, concat_axis=0, tiled=True)
    asked = asked.reshape(2 * devices)
    message = gather(sent, asked, flow, devices)
    message = lax.all_to_all(message, AXES, split_axis=0, concat_axis=0, tiled=True)

    jac = jnp.broadcast_to(face_jacobian.reshape(-1, 1, 1), (4 * NV * NV, 8, LANES))
    top, bottom = flow[0].reshape(2 * NV, LANES), flow[rows - 1].reshape(2 * NV, LANES)
    even = parity[0] == 0
    halo_a, halo_b = exchange(jnp.where(even, bottom, top), jnp.where(even, top, bottom))
    flow_s, right_s, coef_s, inv_s = relayout(flow, right_side[0], face_coef[0], inv_diag[0])
    start_s = first_sum(parity, flow_s, right_s, coef_s, jac, halo_a, halo_b)

    source, edge_a, edge_b = scatter(parity, sent, asked, message, start_s, inv_s)
    halo_a, halo_b = exchange(edge_a, edge_b)
    relaxed = sweeps(source, start_s, right_s, coef_s, jac, inv_s)
    relaxed = edge_rows(parity, relaxed, coef_s, jac, inv_s, halo_a, halo_b)
    return relaxed[None]


def solution(mesh):
    placed = (
        P("zone", "blk", None, None),
        P("zone", "blk", None, None),
        P("zone", "blk", None, None, None),
        P("zone", "blk", None, None),
        P(),
        P(("zone", "blk"), None),
        P(("zone", "blk")),
        P(("zone", "blk")),
        P(),
    )
    return jax.shard_map(
        body, mesh=mesh, in_specs=placed, out_specs=P("zone", "blk", None, None), check_vma=False
    )
```

```python
import jax
import jax.numpy as jnp
from jax import lax
from jax.experimental import pallas as pl
from jax.experimental.pallas import tpu as pltpu
from jax.sharding import PartitionSpec as P

NV = 7
LANES = 128
COLS = 2 * LANES
AXES = ("zone", "blk")
F32 = jnp.float32
BF16 = jnp.bfloat16
I32 = jnp.int32
VMEM = pltpu.VMEM
SMEM = pl.BlockSpec(memory_space=pltpu.SMEM)
MIB = 1 << 20
RING = 4


def params(mib):
    return pltpu.CompilerParams(vmem_limit_bytes=mib * MIB)


def cost(flops, bytes_accessed):
    return pl.CostEstimate(flops=flops, bytes_accessed=bytes_accessed, transcendentals=0)


def whole(space=VMEM):
    return pl.BlockSpec(memory_space=space)


def tables_kernel(owner_in, device_in, source_in, target_in, sent, asking, rows, sems):
    n = owner_in.shape[1]
    copies = [
        pltpu.make_async_copy(ref, rows.at[i], sems.at[i])
        for i, ref in enumerate((owner_in, device_in, source_in, target_in))
    ]
    for copy in copies:
        copy.start()
    for copy in copies:
        copy.wait()
    owner, block_device, source_row, target_row = (rows[i].astype(F32) for i in range(4))
    lane = lax.broadcasted_iota(I32, (n, n), 1)
    sub = lax.broadcasted_iota(I32, (n, n), 0)
    eye = lane == sub

    def column(row):
        return jnp.sum(jnp.where(eye, row, 0.0), axis=1, keepdims=True)

    number = lane.astype(F32)
    owner_col = column(owner)
    target = jnp.sum(jnp.where(owner_col == number, block_device, 0.0), axis=1, keepdims=True)
    hot = target == number
    earlier = jnp.where(lane < sub, 1.0, 0.0).astype(BF16)
    prior = jnp.dot(earlier, jnp.where(hot, 1.0, 0.0).astype(BF16), preferred_element_type=F32)
    source_col = column(source_row + 1.0)
    target_col = column(target_row + 1.0)
    picked = jnp.zeros((n, n), F32)
    for k in range(2):
        mine = hot & ((prior > 0.5) if k else (prior < 0.5))
        sent[k : k + 1, :] = jnp.sum(jnp.where(mine, source_col, 0.0), axis=0, keepdims=True).astype(I32)
        asked = column(jnp.sum(jnp.where(mine, target_col, 0.0), axis=0, keepdims=True))
        picked = jnp.where(lane == k, asked, picked)
    asking[...] = picked.astype(I32).reshape(asking.shape)


def slot_tables(owner, block_device, source_row, target_row):
    n = owner.shape[1]
    return pl.pallas_call(
        tables_kernel,
        in_specs=[whole(pltpu.HBM)] * 4,
        out_specs=[whole()] * 2,
        out_shape=[jax.ShapeDtypeStruct((2, n), I32), jax.ShapeDtypeStruct((n, 1, LANES), I32)],
        scratch_shapes=[VMEM((4, 1, n), I32), pltpu.SemaphoreType.DMA((4,))],
        compiler_params=params(60),
        cost_estimate=cost(4_000_000, 100_000),
        name="slot_tables",
    )(owner, block_device, source_row, target_row)


def table_copies(sent_in, asked_in, sent, asked, sems):
    return [
        pltpu.make_async_copy(sent_in, sent, sems.at[0]),
        pltpu.make_async_copy(asked_in, asked, sems.at[1]),
    ]


def table_scratch(devices):
    return [
        pltpu.SMEM((2, devices), I32),
        pltpu.SMEM((devices, 1, LANES), I32),
        pltpu.SemaphoreType.DMA((2,)),
    ]


def gather_kernel(sent_in, asked_in, flow_in, message, asked_out, sent, asked, sems, flow, more):
    count = message.shape[0]
    base = pl.program_id(0) * count

    @pl.when(pl.program_id(0) == 0)
    def _():
        copies = table_copies(sent_in, asked_in, sent, asked, sems) + [
            pltpu.make_async_copy(flow_in, flow, more.at[0]),
            pltpu.make_async_copy(asked_in, asked_out, more.at[1]),
        ]
        for copy in copies:
            copy.start()
        for copy in copies:
            copy.wait()

    def step(d, carry):
        for part in range(2):
            for k in range(2):
                slot = asked[base + d, 0, k] if part else sent[k, base + d]
                row = jnp.maximum(slot - 1, 0)
                for h in range(2):
                    start = 28 * part + 14 * k + NV * h
                    message[d, start : start + NV, :] = flow[row, :, LANES * h : LANES * (h + 1)]
        return carry

    lax.fori_loop(0, count, step, 0, unroll=2)


def gather(sent, asked, flow):
    devices = asked.shape[0]
    return pl.pallas_call(
        gather_kernel,
        grid=(8,),
        in_specs=[whole(pltpu.HBM), whole(), whole(pltpu.HBM)],
        out_specs=[pl.BlockSpec((devices // 8, 8 * NV, LANES), lambda g: (g, 0, 0)), whole(pltpu.HBM)],
        out_shape=[
            jax.ShapeDtypeStruct((devices, 8 * NV, LANES), F32),
            jax.ShapeDtypeStruct(asked.shape, I32),
        ],
        scratch_shapes=table_scratch(devices) + [VMEM(flow.shape, F32), pltpu.SemaphoreType.DMA((2,))],
        compiler_params=params(58),
        cost_estimate=cost(1_000_000, 6_000_000),
        name="gather",
    )(sent, asked, flow)


def coupled(state, row, coef, mix):
    lane = lax.broadcasted_iota(I32, (8, LANES), 1)
    parts = []
    for direction in range(4):
        factor = coef(direction)
        for v in range(NV):
            if direction < 2:
                first = row + 2 * direction - 1
                pair = [state[2 * v + h, pl.ds(first, 8), :] for h in range(2)]
            else:
                mid = [state[2 * v + h, pl.ds(row, 8), :] for h in range(2)]
                if direction == 2:
                    left, right = (pltpu.roll(m, 1, 1) for m in mid)
                    pair = [jnp.where(lane == 0, 0.0, left), jnp.where(lane == 0, left, right)]
                else:
                    left, right = (pltpu.roll(m, LANES - 1, 1) for m in mid)
                    pair = [jnp.where(lane == LANES - 1, right, left), jnp.where(lane == LANES - 1, 0.0, right)]
            parts.append(factor * jnp.concatenate(pair, axis=1))
    cells = jnp.concatenate(parts, axis=0)
    high = cells.astype(BF16)
    low = (cells - high.astype(F32)).astype(BF16)
    dot = lambda a, b: jnp.dot(a, b, preferred_element_type=F32)
    return dot(mix[0], high) + dot(mix[1], high) + dot(mix[0], low)


def apply_inv(inv, cells):
    out = []
    for i in range(NV):
        total = None
        for j in range(NV):
            term = inv(i, j) * cells[j]
            total = term if j == 0 else total + term
        out.append(total)
    return out


def first_kernel(parity, flow, right, coef, mix, halo_a, halo_b, inv, start, start_edges, inv_edges, state, sems):
    tiles = right.shape[1] // 8
    copies = [
        pltpu.make_async_copy(inv.at[:, :, 8 * t : 8 * t + 8, :], inv_edges.at[g], sems.at[g])
        for g, t in enumerate((0, tiles - 1))
    ]
    for copy in copies:
        copy.start()
    even = parity[0] == 0
    for n in range(2 * NV):
        v, h = divmod(n, 2)
        a, b = halo_a[n : n + 1, :], halo_b[n : n + 1, :]
        state[n, 7:8, :] = jnp.where(even, b, a)
        state[n, 8 + 8 * tiles : 9 + 8 * tiles, :] = jnp.where(even, a, b)
        state[n, 8 : 8 + 8 * tiles, :] = flow[v, :, LANES * h : LANES * (h + 1)]

    def step(t, carry):
        row = pl.multiple_of(8 * t, 8)
        sums = coupled(state, row + 8, lambda d: coef[d, pl.ds(row, 8), :], mix)
        for v in range(NV):
            start[v, pl.ds(row, 8), :] = right[v, pl.ds(row, 8), :] - sums[8 * v : 8 * v + 8, :]
        return carry

    lax.fori_loop(0, tiles, step, 0)
    start_edges[0] = start[:, 0:8, :]
    start_edges[1] = start[:, 8 * tiles - 8 : 8 * tiles, :]
    for copy in copies:
        copy.wait()


def first_sum(parity, flow, right, coef, mix, halo_a, halo_b, inv):
    rows = flow.shape[1]
    shapes = (flow.shape, (2, NV, 8, COLS), (2, NV, NV, 8, COLS))
    return pl.pallas_call(
        first_kernel,
        in_specs=[SMEM] + [whole()] * 6 + [whole(pltpu.HBM)],
        out_specs=[whole()] * 3,
        out_shape=[jax.ShapeDtypeStruct(s, F32) for s in shapes],
        scratch_shapes=[VMEM((2 * NV, rows + 16, LANES), F32), pltpu.SemaphoreType.DMA((2,))],
        compiler_params=params(52),
        cost_estimate=cost(30_000_000, 8_000_000),
        name="first_sum",
    )(parity, flow, right, coef, mix, halo_a, halo_b, inv)


def scatter_kernel(
    parity, sent_in, asked_in, message, start_edges, inv_edges, source, edge_a, edge_b, sent, asked, sems
):
    groups = source.shape[1] // 8
    count = message.shape[0]
    base = pl.program_id(0) * count

    @pl.when(pl.program_id(0) == 0)
    def _():
        copies = table_copies(sent_in, asked_in, sent, asked, sems)
        for copy in copies:
            copy.start()

        def clear(g, carry):
            for h in range(2):
                source[h, pl.ds(pl.multiple_of(64 * g, 64), 64), :] = jnp.zeros((64, LANES), F32)
            return carry

        lax.fori_loop(0, groups // 8, clear, 0)
        for copy in copies:
            copy.wait()

    def step(d, carry):
        for part in range(2):
            for k in range(2):
                slot = sent[k, base + d] if part else asked[base + d, 0, k]
                row = pl.multiple_of(8 * slot, 8)
                for h in range(2):
                    start = 28 * part + 14 * k + NV * h
                    value = message[d, start : start + NV, :]
                    old = source[h, pl.ds(row, NV), :]
                    source[h, pl.ds(row, NV), :] = old - value if part else old + value
        return carry

    lax.fori_loop(0, count, step, 0, unroll=2)

    @pl.when(pl.program_id(0) == pl.num_programs(0) - 1)
    def _():
        even = parity[0] == 0
        edges = []
        for g, (tile, sub) in enumerate(((0, 0), (groups // 8 - 2, 7))):
            cells = [start_edges[g, v] + added(source, tile, v) for v in range(NV)]
            relaxed = apply_inv(lambda i, j, g=g: inv_edges[g, i, j], cells)
            edges.append([r[sub : sub + 1, :] for r in relaxed])
        for v in range(NV):
            top, bottom = edges[0][v], edges[1][v]
            out_a, out_b = jnp.where(even, bottom, top), jnp.where(even, top, bottom)
            for h in range(2):
                n = 2 * v + h
                edge_a[n : n + 1, :] = out_a[:, LANES * h : LANES * (h + 1)]
                edge_b[n : n + 1, :] = out_b[:, LANES * h : LANES * (h + 1)]


def added(source, tile, v):
    return jnp.concatenate([source[h, pl.ds(64 * tile + 8 + v, 8, stride=8), :] for h in range(2)], axis=1)


def scatter(parity, sent, asked, message, start_edges, inv_edges, rows):
    devices = message.shape[0]
    steps = 8
    sources = (2, 8 * (rows + 8), LANES)
    edge = (2 * NV, LANES)
    return pl.pallas_call(
        scatter_kernel,
        grid=(steps,),
        in_specs=[
            SMEM,
            whole(pltpu.HBM),
            whole(pltpu.HBM),
            pl.BlockSpec((devices // steps,) + message.shape[1:], lambda g: (g, 0, 0)),
            whole(),
            whole(),
        ],
        out_specs=[whole()] * 3,
        out_shape=[jax.ShapeDtypeStruct(s, F32) for s in (sources, edge, edge)],
        scratch_shapes=table_scratch(devices),
        compiler_params=params(16),
        cost_estimate=cost(2_000_000, 7_000_000),
        name="scatter",
    )(parity, sent, asked, message, start_edges, inv_edges)


def sweeps_kernel(
    source, mix, start_in, right_in, coef_in, inv_in, out, state, done, start, right, coef, inv, sems, out_sems
):
    tiles = start_in.shape[1] // 8
    chunk = 4

    def fetch(t):
        slot = lax.rem(t, RING)
        rows = pl.ds(pl.multiple_of(8 * t, 8), 8)
        streams = ((start_in, start), (right_in, right), (coef_in, coef))
        copies = [
            pltpu.make_async_copy(ref.at[:, rows, :], part.at[slot], sems.at[n, slot])
            for n, (ref, part) in enumerate(streams)
        ]
        return copies + [pltpu.make_async_copy(inv_in.at[:, :, rows, :], inv.at[slot], sems.at[3, slot])]

    def begin(copies):
        for copy in copies:
            copy.start()

    def finish(copies):
        for copy in copies:
            copy.wait()

    def store(c):
        rows = pl.ds(pl.multiple_of(8 * chunk * c, 8), 8 * chunk)
        return pltpu.make_async_copy(done.at[:, rows, :], out.at[:, rows, :], out_sems.at[c])

    for t in range(RING):
        begin(fetch(t))
    for n in range(2 * NV):
        state[n, 0:8, :] = jnp.zeros((8, LANES), F32)
        state[n, 8 + 8 * tiles : 16 + 8 * tiles, :] = jnp.zeros((8, LANES), F32)

    def sweep_one(t):
        slot = lax.rem(t, RING)
        row = pl.multiple_of(8 * t, 8)
        cells = [start[slot, v] + added(source, t, v) for v in range(NV)]
        relaxed = apply_inv(lambda i, j: inv[slot, i, j], cells)
        for v in range(NV):
            for h in range(2):
                state[2 * v + h, pl.ds(row + 8, 8), :] = relaxed[v][:, LANES * h : LANES * (h + 1)]

    def sweep_two(t):
        slot = lax.rem(t, RING)
        row = pl.multiple_of(8 * t, 8)
        sums = coupled(state, row + 8, lambda d: coef[slot, d], mix)
        cells = [right[slot, v] + added(source, t, v) - sums[8 * v : 8 * v + 8, :] for v in range(NV)]
        relaxed = apply_inv(lambda i, j: inv[slot, i, j], cells)
        for v in range(NV):
            done[v, pl.ds(row, 8), :] = relaxed[v]

    finish(fetch(0))
    sweep_one(0)

    def step(t, carry):
        finish(fetch(t))
        sweep_one(t)
        sweep_two(t - 1)

        @pl.when(t + RING - 1 < tiles)
        def _():
            begin(fetch(t + RING - 1))

        @pl.when(lax.rem(t, chunk) == 0)
        def _():
            store(t // chunk - 1).start()

        return carry

    lax.fori_loop(1, tiles, step, 0)
    sweep_two(tiles - 1)
    store(tiles // chunk - 1).start()
    for c in range(tiles // chunk):
        store(c).wait()


def sweeps(source, mix, start, right, coef, inv):
    rows = start.shape[1]
    return pl.pallas_call(
        sweeps_kernel,
        in_specs=[whole()] * 2 + [whole(pltpu.HBM)] * 4,
        out_specs=whole(pltpu.HBM),
        out_shape=jax.ShapeDtypeStruct(start.shape, F32),
        scratch_shapes=[
            VMEM((2 * NV, rows + 16, LANES), F32),
            VMEM(start.shape, F32),
            VMEM((RING, NV, 8, COLS), F32),
            VMEM((RING, NV, 8, COLS), F32),
            VMEM((RING, 4, 8, COLS), F32),
            VMEM((RING, NV, NV, 8, COLS), F32),
            pltpu.SemaphoreType.DMA((4, RING)),
            pltpu.SemaphoreType.DMA((rows // 32,)),
        ],
        compiler_params=params(40),
        cost_estimate=cost(45_000_000, 24_000_000),
        name="sweeps",
    )(source, mix, start, right, coef, inv)


def edge_kernel(parity, relaxed, coef, mix, inv, halo_a, halo_b, out):
    low = pl.program_id(0) == 0
    use_a = (parity[0] == 0) != low
    place = lax.broadcasted_iota(I32, (8, COLS), 0) == jnp.where(low, 0, 7)
    factor = jnp.where(low, coef[0], coef[1])
    parts = []
    for v in range(NV):
        rows = [jnp.where(use_a, halo_a[n : n + 1, :], halo_b[n : n + 1, :]) for n in (2 * v, 2 * v + 1)]
        row = jnp.broadcast_to(jnp.concatenate(rows, axis=1), (8, COLS))
        parts.append(jnp.where(place, factor * row, 0.0))
    cells = jnp.concatenate(parts, axis=0)
    zero = jnp.zeros_like(cells)
    cells = jnp.concatenate([jnp.where(low, cells, zero), jnp.where(low, zero, cells), zero, zero], axis=0)
    high = cells.astype(BF16)
    rest = (cells - high.astype(F32)).astype(BF16)
    dot = lambda a, b: jnp.dot(a, b, preferred_element_type=F32)
    sums = dot(mix[0], high) + dot(mix[1], high) + dot(mix[0], rest)
    change = apply_inv(lambda i, j: inv[i, j], [sums[8 * v : 8 * v + 8, :] for v in range(NV)])
    for v in range(NV):
        out[v] = relaxed[v] - change[v]


def edge_rows(parity, relaxed, coef, mix, inv, halo_a, halo_b):
    last = relaxed.shape[1] // 8 - 1
    slab = pl.BlockSpec((NV, 8, COLS), lambda g: (0, g * last, 0))
    return pl.pallas_call(
        edge_kernel,
        grid=(2,),
        in_specs=[
            SMEM,
            slab,
            pl.BlockSpec((4, 8, COLS), lambda g: (0, g * last, 0)),
            pl.BlockSpec(mix.shape, lambda g: (0, 0, 0)),
            pl.BlockSpec((None, NV, NV, 8, COLS), lambda g: (g, 0, 0, 0, 0)),
            pl.BlockSpec((2 * NV, LANES), lambda g: (0, 0)),
            pl.BlockSpec((2 * NV, LANES), lambda g: (0, 0)),
        ],
        out_specs=slab,
        out_shape=jax.ShapeDtypeStruct(relaxed.shape, F32),
        input_output_aliases={1: 0},
        compiler_params=params(40),
        cost_estimate=cost(100_000, 900_000),
        name="edge_rows",
    )(parity, relaxed, coef, mix, inv, halo_a, halo_b)


def exchange(edge_a, edge_b):
    size = lax.axis_size("blk")
    pairs_a = [(i, i ^ 1) for i in range(size)]
    pairs_b = [(i, i - 1 if i % 2 == 0 else i + 1) for i in range(1, size - 1)]
    return lax.ppermute(edge_a, "blk", pairs_a), lax.ppermute(edge_b, "blk", pairs_b)


def mixing(face_jacobian):
    wide = jnp.transpose(face_jacobian, (1, 0, 2)).reshape(NV, 4 * NV)
    full = (wide[:, None, :, None] * jnp.eye(8, dtype=F32)[None, :, None, :]).reshape(8 * NV, 32 * NV)
    high = lax.reduce_precision(full, exponent_bits=8, mantissa_bits=7)
    return jnp.stack([high.astype(BF16), (full - high).astype(BF16)])


def body(flow_state, right_side, inv_diag, face_coef, face_jacobian, hole_owner, source_row, target_row, block_device):
    flow = jnp.transpose(flow_state[0], (1, 0, 2))
    right = jnp.transpose(right_side[0], (1, 0, 2))
    inv = jnp.transpose(inv_diag[0], (1, 2, 0, 3))
    rows = flow.shape[1]
    parity = (lax.axis_index("blk") % 2).astype(I32).reshape(1)
    as_row = lambda a: a.reshape(1, -1)
    sent, asking = slot_tables(as_row(hole_owner), as_row(block_device), as_row(source_row), as_row(target_row))
    asked = lax.all_to_all(asking, AXES, split_axis=0, concat_axis=0, tiled=True)
    message, asked = gather(sent, asked, flow_state[0])
    message = lax.all_to_all(message, AXES, split_axis=0, concat_axis=0, tiled=True)

    coef = jnp.transpose(face_coef[0], (1, 0, 2))
    mix = mixing(face_jacobian)
    top, bottom = flow[:, 0].reshape(2 * NV, LANES), flow[:, rows - 1].reshape(2 * NV, LANES)
    even = parity[0] == 0
    halo_a, halo_b = exchange(jnp.where(even, bottom, top), jnp.where(even, top, bottom))
    start, start_edges, inv_edges = first_sum(parity, flow, right, coef, mix, halo_a, halo_b, inv)

    source, edge_a, edge_b = scatter(parity, sent, asked, message, start_edges, inv_edges, rows)
    halo_a, halo_b = exchange(edge_a, edge_b)
    relaxed = sweeps(source, mix, start, right, coef, inv)
    relaxed = edge_rows(parity, relaxed, coef, mix, inv_edges, halo_a, halo_b)
    return jnp.transpose(relaxed, (1, 0, 2))[None]


def solution(mesh):
    placed = (
        P("zone", "blk", None, None),
        P("zone", "blk", None, None),
        P("zone", "blk", None, None, None),
        P("zone", "blk", None, None),
        P(),
        P(("zone", "blk"), None),
        P(("zone", "blk")),
        P(("zone", "blk")),
        P(),
    )
    return jax.shard_map(
        body, mesh=mesh, in_specs=placed, out_specs=P("zone", "blk", None, None), check_vma=False
    )
```

```python
import jax
import jax.numpy as jnp
from jax import lax
from jax.experimental import pallas as pl
from jax.experimental.pallas import tpu as pltpu
from jax.sharding import PartitionSpec as P

NV = 7
LANES = 128
COLS = 2 * LANES
AXES = ("zone", "blk")
F32 = jnp.float32
BF16 = jnp.bfloat16
I32 = jnp.int32
VMEM = pltpu.VMEM
SMEM = pl.BlockSpec(memory_space=pltpu.SMEM)
MIB = 1 << 20
CHUNKS = 8


def params(mib):
    return pltpu.CompilerParams(vmem_limit_bytes=mib * MIB)


def cost(flops, bytes_accessed):
    return pl.CostEstimate(flops=flops, bytes_accessed=bytes_accessed, transcendentals=0)


def whole(space=VMEM):
    return pl.BlockSpec(memory_space=space)


def tables_kernel(owner_in, device_in, source_in, target_in, sent, asking, rows, sems):
    n = owner_in.shape[1]
    copies = [
        pltpu.make_async_copy(ref, rows.at[i], sems.at[i])
        for i, ref in enumerate((owner_in, device_in, source_in, target_in))
    ]
    for copy in copies:
        copy.start()
    for copy in copies:
        copy.wait()
    owner, block_device, source_row, target_row = (rows[i].astype(F32) for i in range(4))
    lane = lax.broadcasted_iota(I32, (n, n), 1)
    sub = lax.broadcasted_iota(I32, (n, n), 0)
    eye = lane == sub

    def column(row):
        return jnp.sum(jnp.where(eye, row, 0.0), axis=1, keepdims=True)

    number = lane.astype(F32)
    owner_col = column(owner)
    target = jnp.sum(jnp.where(owner_col == number, block_device, 0.0), axis=1, keepdims=True)
    hot = target == number
    earlier = jnp.where(lane < sub, 1.0, 0.0).astype(BF16)
    prior = jnp.dot(earlier, jnp.where(hot, 1.0, 0.0).astype(BF16), preferred_element_type=F32)
    source_col = column(source_row + 1.0)
    target_col = column(target_row + 1.0)
    picked = jnp.zeros((n, n), F32)
    for k in range(2):
        mine = hot & ((prior > 0.5) if k else (prior < 0.5))
        sent[k : k + 1, :] = jnp.sum(jnp.where(mine, source_col, 0.0), axis=0, keepdims=True).astype(I32)
        asked = column(jnp.sum(jnp.where(mine, target_col, 0.0), axis=0, keepdims=True))
        picked = jnp.where(lane == k, asked, picked)
    asking[...] = picked.astype(I32).reshape(asking.shape)


def slot_tables(owner, block_device, source_row, target_row):
    n = owner.shape[1]
    return pl.pallas_call(
        tables_kernel,
        in_specs=[whole(pltpu.HBM)] * 4,
        out_specs=[whole()] * 2,
        out_shape=[jax.ShapeDtypeStruct((2, n), I32), jax.ShapeDtypeStruct((n, 1, LANES), I32)],
        scratch_shapes=[VMEM((4, 1, n), I32), pltpu.SemaphoreType.DMA((4,))],
        compiler_params=params(61),
        cost_estimate=cost(4_000_000, 100_000),
        name="slot_tables",
    )(owner, block_device, source_row, target_row)


def begin(copies):
    for copy in copies:
        copy.start()


def finish(copies):
    for copy in copies:
        copy.wait()


def gather_kernel(sent_in, asked_in, flow_in, message_out, asked_out, sent, asked, flow, packed, message, sems, out_sems):
    n = message.shape[0]
    copies = [pltpu.make_async_copy(sent_in, sent, sems.at[0]), pltpu.make_async_copy(flow_in, flow, sems.at[1])]
    begin(copies)
    eye = lax.broadcasted_iota(I32, (n, n), 0) == lax.broadcasted_iota(I32, (n, n), 1)
    table = asked_in[...].reshape(n, LANES).astype(F32)
    for k in range(2):
        packed[k : k + 1, :] = jnp.sum(jnp.where(eye, table[:, k : k + 1], 0.0), axis=0, keepdims=True).astype(I32)
    tables = [pltpu.make_async_copy(packed, asked, sems.at[2]), pltpu.make_async_copy(packed, asked_out, sems.at[3])]
    begin(tables)
    finish(copies + tables)

    def step(d, carry):
        for part, rows in enumerate((sent, asked)):
            for k in range(2):
                row = jnp.maximum(rows[k, d] - 1, 0)
                for h in range(2):
                    start = 28 * part + 14 * k + NV * h
                    message[d, start : start + NV, :] = flow[row, :, LANES * h : LANES * (h + 1)]
        return carry

    size = n // CHUNKS
    stores = []
    for c in range(CHUNKS):
        lax.fori_loop(c * size, (c + 1) * size, step, 0, unroll=4)
        part = pl.ds(c * size, size)
        stores.append(pltpu.make_async_copy(message.at[part], message_out.at[part], out_sems.at[c]))
        stores[-1].start()
    finish(stores)


def gather(sent, asked, flow):
    devices = asked.shape[0]
    message = (devices, 8 * NV, LANES)
    return pl.pallas_call(
        gather_kernel,
        in_specs=[whole(pltpu.HBM), whole(), whole(pltpu.HBM)],
        out_specs=[whole(pltpu.HBM)] * 2,
        out_shape=[jax.ShapeDtypeStruct(message, F32), jax.ShapeDtypeStruct((2, devices), I32)],
        scratch_shapes=[
            pltpu.SMEM((2, devices), I32),
            pltpu.SMEM((2, devices), I32),
            VMEM(flow.shape, F32),
            VMEM((2, devices), I32),
            VMEM(message, F32),
            pltpu.SemaphoreType.DMA((4,)),
            pltpu.SemaphoreType.DMA((CHUNKS,)),
        ],
        compiler_params=params(58),
        cost_estimate=cost(1_000_000, 6_000_000),
        name="gather",
    )(sent, asked, flow)


def coupled(state, row, coef, mix):
    lane = lax.broadcasted_iota(I32, (8, LANES), 1)
    parts = []
    for direction in range(4):
        factor = coef(direction)
        for v in range(NV):
            if direction < 2:
                first = row + 2 * direction - 1
                pair = [state[2 * v + h, pl.ds(first, 8), :] for h in range(2)]
            else:
                mid = [state[2 * v + h, pl.ds(row, 8), :] for h in range(2)]
                if direction == 2:
                    left, right = (pltpu.roll(m, 1, 1) for m in mid)
                    pair = [jnp.where(lane == 0, 0.0, left), jnp.where(lane == 0, left, right)]
                else:
                    left, right = (pltpu.roll(m, LANES - 1, 1) for m in mid)
                    pair = [jnp.where(lane == LANES - 1, right, left), jnp.where(lane == LANES - 1, 0.0, right)]
            parts.append(factor * jnp.concatenate(pair, axis=1))
    cells = jnp.concatenate(parts, axis=0)
    high = cells.astype(BF16)
    low = (cells - high.astype(F32)).astype(BF16)
    dot = lambda a, b: jnp.dot(a, b, preferred_element_type=F32)
    return dot(mix[0], high) + dot(mix[1], high) + dot(mix[0], low)


def apply_inv(inv, cells):
    out = []
    for i in range(NV):
        total = None
        for j in range(NV):
            term = inv(i, j) * cells[j]
            total = term if j == 0 else total + term
        out.append(total)
    return out


def first_kernel(parity, flow, right, coef, mix, halo_a, halo_b, inv, start, start_edges, inv_edges, state, sems):
    tiles = right.shape[1] // 8
    copies = [
        pltpu.make_async_copy(inv.at[:, :, 8 * t : 8 * t + 8, :], inv_edges.at[g], sems.at[g])
        for g, t in enumerate((0, tiles - 1))
    ]
    for copy in copies:
        copy.start()
    even = parity[0] == 0
    for n in range(2 * NV):
        v, h = divmod(n, 2)
        a, b = halo_a[n : n + 1, :], halo_b[n : n + 1, :]
        state[n, 7:8, :] = jnp.where(even, b, a)
        state[n, 8 + 8 * tiles : 9 + 8 * tiles, :] = jnp.where(even, a, b)
        state[n, 8 : 8 + 8 * tiles, :] = flow[v, :, LANES * h : LANES * (h + 1)]

    def step(t, carry):
        row = pl.multiple_of(8 * t, 8)
        sums = coupled(state, row + 8, lambda d: coef[d, pl.ds(row, 8), :], mix)
        for v in range(NV):
            start[v, pl.ds(row, 8), :] = right[v, pl.ds(row, 8), :] - sums[8 * v : 8 * v + 8, :]
        return carry

    lax.fori_loop(0, tiles, step, 0)
    start_edges[0] = start[:, 0:8, :]
    start_edges[1] = start[:, 8 * tiles - 8 : 8 * tiles, :]
    for copy in copies:
        copy.wait()


def first_sum(parity, flow, right, coef, mix, halo_a, halo_b, inv):
    rows = flow.shape[1]
    shapes = (flow.shape, (2, NV, 8, COLS), (2, NV, NV, 8, COLS))
    return pl.pallas_call(
        first_kernel,
        in_specs=[SMEM] + [whole()] * 6 + [whole(pltpu.HBM)],
        out_specs=[whole()] * 3,
        out_shape=[jax.ShapeDtypeStruct(s, F32) for s in shapes],
        scratch_shapes=[VMEM((2 * NV, rows + 16, LANES), F32), pltpu.SemaphoreType.DMA((2,))],
        compiler_params=params(61),
        cost_estimate=cost(30_000_000, 8_000_000),
        name="first_sum",
    )(parity, flow, right, coef, mix, halo_a, halo_b, inv)


def added(sources, tile, v):
    return jnp.concatenate([ref[pl.ds(64 * tile + 8 + v, 8, stride=8), :] for ref in sources], axis=1)


def scatter_kernel(
    parity, sent, asked, message_in, start_edges, inv_edges, left, right, edge_a, edge_b, message, sems
):
    sources = (left, right)
    groups = left.shape[0] // 8
    size = message.shape[0] // CHUNKS
    loads = []
    for c in range(CHUNKS):
        part = pl.ds(c * size, size)
        loads.append(pltpu.make_async_copy(message_in.at[part], message.at[part], sems.at[c]))
    begin(loads)

    def clear(g, carry):
        for ref in sources:
            ref[pl.ds(pl.multiple_of(64 * g, 64), 64), :] = jnp.zeros((64, LANES), F32)
        return carry

    lax.fori_loop(0, groups // 8, clear, 0)

    def step(d, carry):
        for part, rows in enumerate((asked, sent)):
            for k in range(2):
                row = pl.multiple_of(8 * rows[k, d], 8)
                for h, ref in enumerate(sources):
                    start = 28 * part + 14 * k + NV * h
                    value = message[d, start : start + NV, :]
                    old = ref[pl.ds(row, NV), :]
                    ref[pl.ds(row, NV), :] = old - value if part else old + value
        return carry

    for c in range(CHUNKS):
        loads[c].wait()
        lax.fori_loop(c * size, (c + 1) * size, step, 0, unroll=4)
    even = parity[0] == 0
    edges = []
    for g, (tile, sub) in enumerate(((0, 0), (groups // 8 - 2, 7))):
        cells = [start_edges[g, v] + added(sources, tile, v) for v in range(NV)]
        relaxed = apply_inv(lambda i, j, g=g: inv_edges[g, i, j], cells)
        edges.append([r[sub : sub + 1, :] for r in relaxed])
    for v in range(NV):
        top, bottom = edges[0][v], edges[1][v]
        out_a, out_b = jnp.where(even, bottom, top), jnp.where(even, top, bottom)
        for h in range(2):
            n = 2 * v + h
            edge_a[n : n + 1, :] = out_a[:, LANES * h : LANES * (h + 1)]
            edge_b[n : n + 1, :] = out_b[:, LANES * h : LANES * (h + 1)]


def scatter(parity, sent, asked, message, start_edges, inv_edges, rows):
    shapes = [(8 * (rows + 8), LANES)] * 2 + [(2 * NV, LANES)] * 2
    return pl.pallas_call(
        scatter_kernel,
        in_specs=[SMEM] * 3 + [whole(pltpu.HBM)] + [whole()] * 2,
        out_specs=[whole()] * 4,
        out_shape=[jax.ShapeDtypeStruct(s, F32) for s in shapes],
        scratch_shapes=[VMEM(message.shape, F32), pltpu.SemaphoreType.DMA((CHUNKS,))],
        compiler_params=params(61),
        cost_estimate=cost(2_000_000, 7_000_000),
        name="scatter",
    )(parity, sent, asked, message, start_edges, inv_edges)


def sweeps_kernel(
    mix,
    left_in,
    other_in,
    start_in,
    right_in,
    coef_in,
    inv_in,
    out,
    state,
    done,
    left,
    other,
    start,
    right,
    coef,
    inv,
    sems,
    out_sems,
):
    sources = (left, other)
    tiles = start.shape[1] // 8
    size = tiles // CHUNKS

    def fetch(c):
        rows = pl.ds(pl.multiple_of(8 * size * c, 8), 8 * size)
        streams = ((start_in, start), (right_in, right), (coef_in, coef))
        copies = [
            pltpu.make_async_copy(ref.at[:, rows, :], part.at[:, rows, :], sems.at[n, c])
            for n, (ref, part) in enumerate(streams)
        ]
        groups = pl.ds(pl.multiple_of(64 * size * c + 8, 8), 64 * size)
        copies += [
            pltpu.make_async_copy(ref.at[groups, :], part.at[groups, :], sems.at[n, c])
            for n, (ref, part) in enumerate(((left_in, left), (other_in, other)), 3)
        ]
        return copies + [pltpu.make_async_copy(inv_in.at[:, :, rows, :], inv.at[:, :, rows, :], sems.at[5, c])]

    def store(c):
        rows = pl.ds(pl.multiple_of(8 * size * c, 8), 8 * size)
        return pltpu.make_async_copy(done.at[:, rows, :], out.at[:, rows, :], out_sems.at[c])

    for c in range(CHUNKS):
        begin(fetch(c))
    for n in range(2 * NV):
        state[n, 0:8, :] = jnp.zeros((8, LANES), F32)
        state[n, 8 + 8 * tiles : 16 + 8 * tiles, :] = jnp.zeros((8, LANES), F32)

    def sweep_one(t):
        rows = pl.ds(pl.multiple_of(8 * t, 8), 8)
        cells = [start[v, rows, :] + added(sources, t, v) for v in range(NV)]
        relaxed = apply_inv(lambda i, j: inv[i, j, rows, :], cells)
        for v in range(NV):
            for h in range(2):
                state[2 * v + h, pl.ds(8 * t + 8, 8), :] = relaxed[v][:, LANES * h : LANES * (h + 1)]

    def sweep_two(t):
        rows = pl.ds(pl.multiple_of(8 * t, 8), 8)
        sums = coupled(state, pl.multiple_of(8 * t + 8, 8), lambda d: coef[d, rows, :], mix)
        cells = [right[v, rows, :] + added(sources, t, v) - sums[8 * v : 8 * v + 8, :] for v in range(NV)]
        relaxed = apply_inv(lambda i, j: inv[i, j, rows, :], cells)
        for v in range(NV):
            done[v, rows, :] = relaxed[v]

    def step(c, carry):
        finish(fetch(c))
        for k in range(size):
            t = c * size + k
            sweep_one(t)
            sweep_two(jnp.maximum(t - 1, 0))

        @pl.when(c > 0)
        def _():
            store(c - 1).start()

        return carry

    lax.fori_loop(0, CHUNKS, step, 0)
    sweep_two(tiles - 1)
    store(CHUNKS - 1).start()
    for c in range(CHUNKS):
        store(c).wait()


def sweeps(left, other, mix, start, right, coef, inv):
    rows = start.shape[1]
    return pl.pallas_call(
        sweeps_kernel,
        in_specs=[whole()] + [whole(pltpu.HBM)] * 6,
        out_specs=whole(pltpu.HBM),
        out_shape=jax.ShapeDtypeStruct(start.shape, F32),
        scratch_shapes=[
            VMEM((2 * NV, rows + 16, LANES), F32),
            VMEM(start.shape, F32),
            VMEM(left.shape, F32),
            VMEM(left.shape, F32),
            VMEM(start.shape, F32),
            VMEM(start.shape, F32),
            VMEM(coef.shape, F32),
            VMEM(inv.shape, F32),
            pltpu.SemaphoreType.DMA((6, CHUNKS)),
            pltpu.SemaphoreType.DMA((CHUNKS,)),
        ],
        compiler_params=params(61),
        cost_estimate=cost(45_000_000, 24_000_000),
        name="sweeps",
    )(mix, left, other, start, right, coef, inv)


def edge_kernel(parity, relaxed, coef, mix, inv, halo_a, halo_b, out):
    low = pl.program_id(0) == 0
    use_a = (parity[0] == 0) != low
    place = lax.broadcasted_iota(I32, (8, COLS), 0) == jnp.where(low, 0, 7)
    factor = jnp.where(low, coef[0], coef[1])
    parts = []
    for v in range(NV):
        rows = [jnp.where(use_a, halo_a[n : n + 1, :], halo_b[n : n + 1, :]) for n in (2 * v, 2 * v + 1)]
        row = jnp.broadcast_to(jnp.concatenate(rows, axis=1), (8, COLS))
        parts.append(jnp.where(place, factor * row, 0.0))
    cells = jnp.concatenate(parts, axis=0)
    zero = jnp.zeros_like(cells)
    cells = jnp.concatenate([jnp.where(low, cells, zero), jnp.where(low, zero, cells), zero, zero], axis=0)
    high = cells.astype(BF16)
    rest = (cells - high.astype(F32)).astype(BF16)
    dot = lambda a, b: jnp.dot(a, b, preferred_element_type=F32)
    sums = dot(mix[0], high) + dot(mix[1], high) + dot(mix[0], rest)
    change = apply_inv(lambda i, j: inv[i, j], [sums[8 * v : 8 * v + 8, :] for v in range(NV)])
    for v in range(NV):
        out[v] = relaxed[v] - change[v]


def edge_rows(parity, relaxed, coef, mix, inv, halo_a, halo_b):
    last = relaxed.shape[1] // 8 - 1
    slab = pl.BlockSpec((NV, 8, COLS), lambda g: (0, g * last, 0))
    return pl.pallas_call(
        edge_kernel,
        grid=(2,),
        in_specs=[
            SMEM,
            slab,
            pl.BlockSpec((4, 8, COLS), lambda g: (0, g * last, 0)),
            pl.BlockSpec(mix.shape, lambda g: (0, 0, 0)),
            pl.BlockSpec((None, NV, NV, 8, COLS), lambda g: (g, 0, 0, 0, 0)),
            pl.BlockSpec((2 * NV, LANES), lambda g: (0, 0)),
            pl.BlockSpec((2 * NV, LANES), lambda g: (0, 0)),
        ],
        out_specs=slab,
        out_shape=jax.ShapeDtypeStruct(relaxed.shape, F32),
        input_output_aliases={1: 0},
        compiler_params=params(24),
        cost_estimate=cost(100_000, 900_000),
        name="edge_rows",
    )(parity, relaxed, coef, mix, inv, halo_a, halo_b)


def exchange(edge_a, edge_b):
    size = lax.axis_size("blk")
    pairs_a = [(i, i ^ 1) for i in range(size)]
    pairs_b = [(i, i - 1 if i % 2 == 0 else i + 1) for i in range(1, size - 1)]
    return lax.ppermute(edge_a, "blk", pairs_a), lax.ppermute(edge_b, "blk", pairs_b)


def mixing(face_jacobian):
    wide = jnp.transpose(face_jacobian, (1, 0, 2)).reshape(NV, 4 * NV)
    full = (wide[:, None, :, None] * jnp.eye(8, dtype=F32)[None, :, None, :]).reshape(8 * NV, 32 * NV)
    high = lax.reduce_precision(full, exponent_bits=8, mantissa_bits=7)
    return jnp.stack([high.astype(BF16), (full - high).astype(BF16)])


def body(flow_state, right_side, inv_diag, face_coef, face_jacobian, hole_owner, source_row, target_row, block_device):
    flow = jnp.transpose(flow_state[0], (1, 0, 2))
    right = jnp.transpose(right_side[0], (1, 0, 2))
    inv = jnp.transpose(inv_diag[0], (1, 2, 0, 3))
    rows = flow.shape[1]
    parity = (lax.axis_index("blk") % 2).astype(I32).reshape(1)
    as_row = lambda a: a.reshape(1, -1)
    sent, asking = slot_tables(as_row(hole_owner), as_row(block_device), as_row(source_row), as_row(target_row))
    asked = lax.all_to_all(asking, AXES, split_axis=0, concat_axis=0, tiled=True)
    top, bottom = flow[:, 0].reshape(2 * NV, LANES), flow[:, rows - 1].reshape(2 * NV, LANES)
    even = parity[0] == 0
    halo_a, halo_b = exchange(jnp.where(even, bottom, top), jnp.where(even, top, bottom))
    asked, halo_a, halo_b = lax.optimization_barrier((asked, halo_a, halo_b))
    message, asked = gather(sent, asked, flow_state[0])
    message = lax.all_to_all(message, AXES, split_axis=0, concat_axis=0, tiled=True)

    coef = jnp.transpose(face_coef[0], (1, 0, 2))
    mix = mixing(face_jacobian)
    start, start_edges, inv_edges = first_sum(parity, flow, right, coef, mix, halo_a, halo_b, inv)

    left, other, edge_a, edge_b = scatter(parity, sent, asked, message, start_edges, inv_edges, rows)
    halo_a, halo_b = exchange(edge_a, edge_b)
    relaxed = sweeps(left, other, mix, start, right, coef, inv)
    relaxed = edge_rows(parity, relaxed, coef, mix, inv_edges, halo_a, halo_b)
    return jnp.transpose(relaxed, (1, 0, 2))[None]


def solution(mesh):
    placed = (
        P("zone", "blk", None, None),
        P("zone", "blk", None, None),
        P("zone", "blk", None, None, None),
        P("zone", "blk", None, None),
        P(),
        P(("zone", "blk"), None),
        P(("zone", "blk")),
        P(("zone", "blk")),
        P(),
    )
    return jax.shard_map(
        body, mesh=mesh, in_specs=placed, out_specs=P("zone", "blk", None, None), check_vma=False
    )
```

```python
import jax
import jax.numpy as jnp
from jax import lax
from jax.experimental import pallas as pl
from jax.experimental.pallas import tpu as pltpu
from jax.sharding import PartitionSpec as P

NV = 7
LANES = 128
COLS = 2 * LANES
AXES = ("zone", "blk")
F32 = jnp.float32
BF16 = jnp.bfloat16
I32 = jnp.int32
VMEM = pltpu.VMEM
SMEM = pl.BlockSpec(memory_space=pltpu.SMEM)
MIB = 1 << 20
CHUNKS = 8


def params(mib):
    return pltpu.CompilerParams(vmem_limit_bytes=mib * MIB)


def cost(flops, bytes_accessed):
    return pl.CostEstimate(flops=flops, bytes_accessed=bytes_accessed, transcendentals=0)


def whole(space=VMEM):
    return pl.BlockSpec(memory_space=space)


def tables_kernel(owner_in, device_in, source_in, target_in, sent, asking, rows, sems):
    n = owner_in.shape[1]
    copies = [
        pltpu.make_async_copy(ref, rows.at[i], sems.at[i])
        for i, ref in enumerate((owner_in, device_in, source_in, target_in))
    ]
    for copy in copies:
        copy.start()
    for copy in copies:
        copy.wait()
    owner, block_device, source_row, target_row = (rows[i].astype(F32) for i in range(4))
    lane = lax.broadcasted_iota(I32, (n, n), 1)
    sub = lax.broadcasted_iota(I32, (n, n), 0)
    eye = lane == sub

    def column(row):
        return jnp.sum(jnp.where(eye, row, 0.0), axis=1, keepdims=True)

    number = lane.astype(F32)
    owner_col = column(owner)
    target = jnp.sum(jnp.where(owner_col == number, block_device, 0.0), axis=1, keepdims=True)
    hot = target == number
    earlier = jnp.where(lane < sub, 1.0, 0.0).astype(BF16)
    prior = jnp.dot(earlier, jnp.where(hot, 1.0, 0.0).astype(BF16), preferred_element_type=F32)
    source_col = column(source_row + 1.0)
    target_col = column(target_row + 1.0)
    picked = jnp.zeros((n, n), F32)
    for k in range(2):
        mine = hot & ((prior > 0.5) if k else (prior < 0.5))
        sent[k : k + 1, :] = jnp.sum(jnp.where(mine, source_col, 0.0), axis=0, keepdims=True).astype(I32)
        asked = column(jnp.sum(jnp.where(mine, target_col, 0.0), axis=0, keepdims=True))
        picked = jnp.where(lane == k, asked, picked)
    asking[...] = picked.astype(I32).reshape(asking.shape)


def slot_tables(owner, block_device, source_row, target_row):
    n = owner.shape[1]
    return pl.pallas_call(
        tables_kernel,
        in_specs=[whole(pltpu.HBM)] * 4,
        out_specs=[whole()] * 2,
        out_shape=[jax.ShapeDtypeStruct((2, n), I32), jax.ShapeDtypeStruct((n, 1, LANES), I32)],
        scratch_shapes=[VMEM((4, 1, n), I32), pltpu.SemaphoreType.DMA((4,))],
        compiler_params=params(61),
        cost_estimate=cost(4_000_000, 100_000),
        name="slot_tables",
    )(owner, block_device, source_row, target_row)


def begin(copies):
    for copy in copies:
        copy.start()


def finish(copies):
    for copy in copies:
        copy.wait()


def gather_kernel(sent_in, asked_in, flow_in, message_out, asked_out, sent, asked, flow, packed, message, sems, out_sems):
    n = message.shape[0]
    copies = [pltpu.make_async_copy(sent_in, sent, sems.at[0]), pltpu.make_async_copy(flow_in, flow, sems.at[1])]
    begin(copies)
    eye = lax.broadcasted_iota(I32, (n, n), 0) == lax.broadcasted_iota(I32, (n, n), 1)
    table = asked_in[...].reshape(n, LANES).astype(F32)
    for k in range(2):
        packed[k : k + 1, :] = jnp.sum(jnp.where(eye, table[:, k : k + 1], 0.0), axis=0, keepdims=True).astype(I32)
    tables = [pltpu.make_async_copy(packed, asked, sems.at[2]), pltpu.make_async_copy(packed, asked_out, sems.at[3])]
    begin(tables)
    finish(copies + tables)

    def step(d, carry):
        for part, rows in enumerate((sent, asked)):
            for k in range(2):
                row = jnp.maximum(rows[k, d] - 1, 0)
                for h in range(2):
                    start = 28 * part + 14 * k + NV * h
                    message[d, start : start + NV, :] = flow[row, :, LANES * h : LANES * (h + 1)]
        return carry

    size = n // CHUNKS
    stores = []
    for c in range(CHUNKS):
        lax.fori_loop(c * size, (c + 1) * size, step, 0, unroll=4)
        part = pl.ds(c * size, size)
        stores.append(pltpu.make_async_copy(message.at[part], message_out.at[part], out_sems.at[c]))
        stores[-1].start()
    finish(stores)


def gather(sent, asked, flow):
    devices = asked.shape[0]
    message = (devices, 8 * NV, LANES)
    return pl.pallas_call(
        gather_kernel,
        in_specs=[whole(pltpu.HBM), whole(), whole(pltpu.HBM)],
        out_specs=[whole(pltpu.HBM)] * 2,
        out_shape=[jax.ShapeDtypeStruct(message, F32), jax.ShapeDtypeStruct((2, devices), I32)],
        scratch_shapes=[
            pltpu.SMEM((2, devices), I32),
            pltpu.SMEM((2, devices), I32),
            VMEM(flow.shape, F32),
            VMEM((2, devices), I32),
            VMEM(message, F32),
            pltpu.SemaphoreType.DMA((4,)),
            pltpu.SemaphoreType.DMA((CHUNKS,)),
        ],
        compiler_params=params(58),
        cost_estimate=cost(1_000_000, 6_000_000),
        name="gather",
    )(sent, asked, flow)


def coupled(state, row, coef, mix):
    lane = lax.broadcasted_iota(I32, (8, LANES), 1)
    parts = []
    for direction in range(4):
        factor = coef(direction)
        for v in range(NV):
            if direction < 2:
                first = row + 2 * direction - 1
                pair = [state[2 * v + h, pl.ds(first, 8), :] for h in range(2)]
            else:
                mid = [state[2 * v + h, pl.ds(row, 8), :] for h in range(2)]
                if direction == 2:
                    left, right = (pltpu.roll(m, 1, 1) for m in mid)
                    pair = [jnp.where(lane == 0, 0.0, left), jnp.where(lane == 0, left, right)]
                else:
                    left, right = (pltpu.roll(m, LANES - 1, 1) for m in mid)
                    pair = [jnp.where(lane == LANES - 1, right, left), jnp.where(lane == LANES - 1, 0.0, right)]
            parts.append(factor * jnp.concatenate(pair, axis=1))
    cells = jnp.concatenate(parts, axis=0)
    high = cells.astype(BF16)
    low = (cells - high.astype(F32)).astype(BF16)
    dot = lambda a, b: jnp.dot(a, b, preferred_element_type=F32)
    return dot(mix[0], high) + dot(mix[1], high) + dot(mix[0], low)


def apply_inv(inv, cells):
    out = []
    for i in range(NV):
        total = None
        for j in range(NV):
            term = inv(i, j) * cells[j]
            total = term if j == 0 else total + term
        out.append(total)
    return out


def first_kernel(parity, flow, right, coef, mix, halo_a, halo_b, inv, start, inv_edges, state, sems):
    tiles = right.shape[1] // 8
    copies = [
        pltpu.make_async_copy(inv.at[:, :, 8 * t : 8 * t + 8, :], inv_edges.at[g], sems.at[g])
        for g, t in enumerate((0, tiles - 1))
    ]
    for copy in copies:
        copy.start()
    even = parity[0] == 0
    for n in range(2 * NV):
        v, h = divmod(n, 2)
        a, b = halo_a[n : n + 1, :], halo_b[n : n + 1, :]
        state[n, 7:8, :] = jnp.where(even, b, a)
        state[n, 8 + 8 * tiles : 9 + 8 * tiles, :] = jnp.where(even, a, b)
        state[n, 8 : 8 + 8 * tiles, :] = flow[v, :, LANES * h : LANES * (h + 1)]

    def step(t, carry):
        row = pl.multiple_of(8 * t, 8)
        sums = coupled(state, row + 8, lambda d: coef[d, pl.ds(row, 8), :], mix)
        for v in range(NV):
            start[v, pl.ds(row, 8), :] = right[v, pl.ds(row, 8), :] - sums[8 * v : 8 * v + 8, :]
        return carry

    lax.fori_loop(0, tiles, step, 0)
    for copy in copies:
        copy.wait()


def first_sum(parity, flow, right, coef, mix, halo_a, halo_b, inv):
    rows = flow.shape[1]
    shapes = (flow.shape, (2, NV, NV, 8, COLS))
    return pl.pallas_call(
        first_kernel,
        in_specs=[SMEM] + [whole()] * 6 + [whole(pltpu.HBM)],
        out_specs=[whole()] * 2,
        out_shape=[jax.ShapeDtypeStruct(s, F32) for s in shapes],
        scratch_shapes=[VMEM((2 * NV, rows + 16, LANES), F32), pltpu.SemaphoreType.DMA((2,))],
        compiler_params=params(61),
        cost_estimate=cost(30_000_000, 8_000_000),
        name="first_sum",
    )(parity, flow, right, coef, mix, halo_a, halo_b, inv)


def finish_kernel(
    parity,
    sent,
    asked,
    turn,
    message_in,
    start_in,
    right_in,
    coef_in,
    inv_in,
    out,
    edge_a,
    edge_b,
    message,
    add_left,
    add_right,
    sub_left,
    sub_right,
    start,
    right,
    coef,
    inv,
    above,
    below,
    ends,
    done,
    message_sems,
    sems,
    out_sems,
):
    tiles = start.shape[1] // 8
    size = tiles // CHUNKS
    count = message.shape[0] // CHUNKS
    plus, minus = (add_left, add_right), (sub_left, sub_right)

    def load(c):
        part = pl.ds(c * count, count)
        return pltpu.make_async_copy(message_in.at[part], message.at[part], message_sems.at[c])

    def fetch(c):
        rows = pl.ds(pl.multiple_of(8 * size * c, 8), 8 * size)
        streams = ((start_in, start), (right_in, right), (coef_in, coef))
        copies = [
            pltpu.make_async_copy(ref.at[:, rows, :], part.at[:, rows, :], sems.at[n, c])
            for n, (ref, part) in enumerate(streams)
        ]
        return copies + [pltpu.make_async_copy(inv_in.at[:, :, rows, :], inv.at[:, :, rows, :], sems.at[3, c])]

    def store(c):
        rows = pl.ds(pl.multiple_of(8 * size * c, 8), 8 * size)
        return pltpu.make_async_copy(done.at[:, rows, :], out.at[:, rows, :], out_sems.at[c])

    begin([load(c) for c in range(CHUNKS)])
    for c in range(CHUNKS):
        begin(fetch(c))

    def clear(g, carry):
        for ref in plus + minus:
            ref[pl.ds(pl.multiple_of(64 * g, 64), 64), :] = jnp.zeros((64, LANES), F32)
        return carry

    lax.fori_loop(0, add_left.shape[0] // 64, clear, 0)
    for n in range(2 * NV):
        above[n, 0:8, :] = jnp.zeros((8, LANES), F32)
        below[n, 8 + 8 * tiles : 16 + 8 * tiles, :] = jnp.zeros((8, LANES), F32)

    def scatter(d, carry):
        for k in range(2):
            for part, (rows, refs) in enumerate(((asked, plus), (sent, minus))):
                row = pl.multiple_of(8 * rows[k, d], 8)
                for h, ref in enumerate(refs):
                    first = 28 * part + 14 * k + NV * h
                    ref[pl.ds(row, NV), :] += message[d, first : first + NV, :]
        return carry

    for c in range(CHUNKS):
        load(c).wait()
        lax.fori_loop(c * count, (c + 1) * count, scatter, 0, unroll=4)

    lane = lax.broadcasted_iota(I32, (8, COLS), 1)

    def sweep_one(t):
        rows = pl.ds(pl.multiple_of(8 * t, 8), 8)
        groups = [pl.ds(64 * t + 8 + v, 8, stride=8) for v in range(NV)]
        source = [jnp.concatenate([p[g, :] - m[g, :] for p, m in zip(plus, minus)], axis=1) for g in groups]
        cells = [start[v, rows, :] + source[v] for v in range(NV)]
        relaxed = apply_inv(lambda i, j: inv[i, j, rows, :], cells)
        end = jnp.minimum(t, 1)
        for v in range(NV):
            ends[end, v] = relaxed[v]
        wide = jnp.concatenate(relaxed + [jnp.zeros((8, COLS), F32)], axis=0)
        high = wide.astype(BF16)
        low = (wide - high.astype(F32)).astype(BF16)
        mixed = jnp.dot(turn[...], jnp.concatenate([high, high, low], axis=0), preferred_element_type=F32)
        piece = lambda d, v: mixed[8 * (NV * d + v) : 8 * (NV * d + v) + 8, :]
        for v in range(NV):
            for h in range(2):
                half = slice(LANES * h, LANES * (h + 1))
                above[2 * v + h, pl.ds(8 * t + 8, 8), :] = piece(0, v)[:, half]
                below[2 * v + h, pl.ds(8 * t + 8, 8), :] = piece(1, v)[:, half]
            west = jnp.where(lane == 0, 0.0, pltpu.roll(piece(2, v), 1, 1))
            east = jnp.where(lane == COLS - 1, 0.0, pltpu.roll(piece(3, v), COLS - 1, 1))
            right[v, rows, :] = right[v, rows, :] + source[v] - coef[2, rows, :] * west - coef[3, rows, :] * east

    def sweep_two(t):
        rows = pl.ds(pl.multiple_of(8 * t, 8), 8)
        cells = []
        for v in range(NV):
            north, south = (
                jnp.concatenate([ref[2 * v + h, pl.ds(8 * t + 8 + shift, 8), :] for h in range(2)], axis=1)
                for ref, shift in ((above, -1), (below, 1))
            )
            cells.append(right[v, rows, :] - coef[0, rows, :] * north - coef[1, rows, :] * south)
        relaxed = apply_inv(lambda i, j: inv[i, j, rows, :], cells)
        for v in range(NV):
            done[v, rows, :] = relaxed[v]

    def step(c, carry):
        finish(fetch(c))
        for k in range(size):
            t = c * size + k
            sweep_one(t)
            sweep_two(jnp.maximum(t - 1, 0))

        @pl.when(c > 0)
        def _():
            store(c - 1).start()

        return carry

    lax.fori_loop(0, CHUNKS, step, 0)
    sweep_two(tiles - 1)
    store(CHUNKS - 1).start()
    even = parity[0] == 0
    for v in range(NV):
        top, bottom = ends[0, v][0:1, :], ends[1, v][7:8, :]
        out_a, out_b = jnp.where(even, bottom, top), jnp.where(even, top, bottom)
        for h in range(2):
            n = 2 * v + h
            edge_a[n : n + 1, :] = out_a[:, LANES * h : LANES * (h + 1)]
            edge_b[n : n + 1, :] = out_b[:, LANES * h : LANES * (h + 1)]
    for c in range(CHUNKS):
        store(c).wait()


def finish_sweeps(parity, sent, asked, turn, message, start, right, coef, inv):
    rows = start.shape[1]
    sums = VMEM((8 * (rows + 8), LANES), F32)
    padded = VMEM((2 * NV, rows + 16, LANES), F32)
    like = lambda a: VMEM(a.shape, F32)
    return pl.pallas_call(
        finish_kernel,
        in_specs=[SMEM] * 3 + [whole()] + [whole(pltpu.HBM)] * 5,
        out_specs=[whole(pltpu.HBM), whole(), whole()],
        out_shape=[jax.ShapeDtypeStruct(s, F32) for s in (start.shape, (2 * NV, LANES), (2 * NV, LANES))],
        scratch_shapes=[like(message)]
        + [sums] * 4
        + [like(a) for a in (start, right, coef, inv)]
        + [padded] * 2
        + [VMEM((2, NV, 8, COLS), F32), like(start)]
        + [pltpu.SemaphoreType.DMA(s) for s in ((CHUNKS,), (4, CHUNKS), (CHUNKS,))],
        compiler_params=params(61),
        cost_estimate=cost(45_000_000, 24_000_000),
        name="finish_sweeps",
    )(parity, sent, asked, turn, message, start, right, coef, inv)


def edge_kernel(parity, relaxed, coef, mix, inv, halo_a, halo_b, out):
    low = pl.program_id(0) == 0
    use_a = (parity[0] == 0) != low
    place = lax.broadcasted_iota(I32, (8, COLS), 0) == jnp.where(low, 0, 7)
    factor = jnp.where(low, coef[0], coef[1])
    parts = []
    for v in range(NV):
        rows = [jnp.where(use_a, halo_a[n : n + 1, :], halo_b[n : n + 1, :]) for n in (2 * v, 2 * v + 1)]
        row = jnp.broadcast_to(jnp.concatenate(rows, axis=1), (8, COLS))
        parts.append(jnp.where(place, factor * row, 0.0))
    cells = jnp.concatenate(parts, axis=0)
    zero = jnp.zeros_like(cells)
    cells = jnp.concatenate([jnp.where(low, cells, zero), jnp.where(low, zero, cells), zero, zero], axis=0)
    high = cells.astype(BF16)
    rest = (cells - high.astype(F32)).astype(BF16)
    dot = lambda a, b: jnp.dot(a, b, preferred_element_type=F32)
    sums = dot(mix[0], high) + dot(mix[1], high) + dot(mix[0], rest)
    change = apply_inv(lambda i, j: inv[i, j], [sums[8 * v : 8 * v + 8, :] for v in range(NV)])
    for v in range(NV):
        out[v] = relaxed[v] - change[v]


def edge_rows(parity, relaxed, coef, mix, inv, halo_a, halo_b):
    last = relaxed.shape[1] // 8 - 1
    slab = pl.BlockSpec((NV, 8, COLS), lambda g: (0, g * last, 0))
    return pl.pallas_call(
        edge_kernel,
        grid=(2,),
        in_specs=[
            SMEM,
            slab,
            pl.BlockSpec((4, 8, COLS), lambda g: (0, g * last, 0)),
            pl.BlockSpec(mix.shape, lambda g: (0, 0, 0)),
            pl.BlockSpec((None, NV, NV, 8, COLS), lambda g: (g, 0, 0, 0, 0)),
            pl.BlockSpec((2 * NV, LANES), lambda g: (0, 0)),
            pl.BlockSpec((2 * NV, LANES), lambda g: (0, 0)),
        ],
        out_specs=slab,
        out_shape=jax.ShapeDtypeStruct(relaxed.shape, F32),
        input_output_aliases={1: 0},
        compiler_params=params(24),
        cost_estimate=cost(100_000, 900_000),
        name="edge_rows",
    )(parity, relaxed, coef, mix, inv, halo_a, halo_b)


def exchange(edge_a, edge_b):
    size = lax.axis_size("blk")
    pairs_a = [(i, i ^ 1) for i in range(size)]
    pairs_b = [(i, i - 1 if i % 2 == 0 else i + 1) for i in range(1, size - 1)]
    return lax.ppermute(edge_a, "blk", pairs_a), lax.ppermute(edge_b, "blk", pairs_b)


def split(full):
    high = lax.reduce_precision(full, exponent_bits=8, mantissa_bits=7)
    return high.astype(BF16), (full - high).astype(BF16)


def mixing(face_jacobian):
    wide = jnp.transpose(face_jacobian, (1, 0, 2)).reshape(NV, 4 * NV)
    return jnp.stack(split((wide[:, None, :, None] * jnp.eye(8, dtype=F32)[None, :, None, :]).reshape(8 * NV, 32 * NV)))


def turning(face_jacobian):
    tall = jnp.pad(face_jacobian.reshape(4 * NV, NV), ((0, 0), (0, 1)))
    high, low = split((tall[:, None, :, None] * jnp.eye(8, dtype=F32)[None, :, None, :]).reshape(32 * NV, 64))
    return jnp.concatenate([high, low, high], axis=1)


def body(flow_state, right_side, inv_diag, face_coef, face_jacobian, hole_owner, source_row, target_row, block_device):
    flow = jnp.transpose(flow_state[0], (1, 0, 2))
    right = jnp.transpose(right_side[0], (1, 0, 2))
    inv = jnp.transpose(inv_diag[0], (1, 2, 0, 3))
    rows = flow.shape[1]
    parity = (lax.axis_index("blk") % 2).astype(I32).reshape(1)
    as_row = lambda a: a.reshape(1, -1)
    sent, asking = slot_tables(as_row(hole_owner), as_row(block_device), as_row(source_row), as_row(target_row))
    asked = lax.all_to_all(asking, AXES, split_axis=0, concat_axis=0, tiled=True)
    top, bottom = flow[:, 0].reshape(2 * NV, LANES), flow[:, rows - 1].reshape(2 * NV, LANES)
    even = parity[0] == 0
    halo_a, halo_b = exchange(jnp.where(even, bottom, top), jnp.where(even, top, bottom))
    asked, halo_a, halo_b = lax.optimization_barrier((asked, halo_a, halo_b))
    message, asked = gather(sent, asked, flow_state[0])
    message = lax.all_to_all(message, AXES, split_axis=0, concat_axis=0, tiled=True)

    coef = jnp.transpose(face_coef[0], (1, 0, 2))
    mix = mixing(face_jacobian)
    start, inv_edges = first_sum(parity, flow, right, coef, mix, halo_a, halo_b, inv)
    relaxed, edge_a, edge_b = finish_sweeps(
        parity, sent, asked, turning(face_jacobian), message, start, right, coef, inv
    )
    halo_a, halo_b = exchange(edge_a, edge_b)
    relaxed = edge_rows(parity, relaxed, coef, mix, inv_edges, halo_a, halo_b)
    return jnp.transpose(relaxed, (1, 0, 2))[None]


def solution(mesh):
    placed = (
        P("zone", "blk", None, None),
        P("zone", "blk", None, None),
        P("zone", "blk", None, None, None),
        P("zone", "blk", None, None),
        P(),
        P(("zone", "blk"), None),
        P(("zone", "blk")),
        P(("zone", "blk")),
        P(),
    )
    return jax.shard_map(
        body, mesh=mesh, in_specs=placed, out_specs=P("zone", "blk", None, None), check_vma=False
    )
```

```python
import jax
import jax.numpy as jnp
from jax import lax
from jax.experimental import pallas as pl
from jax.experimental.pallas import tpu as pltpu
from jax.sharding import PartitionSpec as P

NV = 7
LANES = 128
COLS = 2 * LANES
AXES = ("zone", "blk")
F32 = jnp.float32
BF16 = jnp.bfloat16
I32 = jnp.int32
VMEM = pltpu.VMEM
SMEM = pl.BlockSpec(memory_space=pltpu.SMEM)
MIB = 1 << 20
CHUNKS = 8
TILES = 4
PACKED = 2 * NV + 4


def params(mib):
    return pltpu.CompilerParams(vmem_limit_bytes=mib * MIB)


def cost(flops, bytes_accessed):
    return pl.CostEstimate(flops=flops, bytes_accessed=bytes_accessed, transcendentals=0)


def whole(space=VMEM):
    return pl.BlockSpec(memory_space=space)


def tables_kernel(owner_in, device_in, source_in, target_in, sent, asking, rows, sems):
    n = owner_in.shape[1]
    copies = [
        pltpu.make_async_copy(ref, rows.at[i], sems.at[i])
        for i, ref in enumerate((owner_in, device_in, source_in, target_in))
    ]
    for copy in copies:
        copy.start()
    for copy in copies:
        copy.wait()
    owner, block_device, source_row, target_row = (rows[i].astype(F32) for i in range(4))
    lane = lax.broadcasted_iota(I32, (n, n), 1)
    sub = lax.broadcasted_iota(I32, (n, n), 0)
    eye = lane == sub

    def column(row):
        return jnp.sum(jnp.where(eye, row, 0.0), axis=1, keepdims=True)

    number = lane.astype(F32)
    owner_col = column(owner)
    target = jnp.sum(jnp.where(owner_col == number, block_device, 0.0), axis=1, keepdims=True)
    hot = target == number
    earlier = jnp.where(lane < sub, 1.0, 0.0).astype(BF16)
    prior = jnp.dot(earlier, jnp.where(hot, 1.0, 0.0).astype(BF16), preferred_element_type=F32)
    source_col = column(source_row + 1.0)
    target_col = column(target_row + 1.0)
    picked = jnp.zeros((n, n), F32)
    for k in range(2):
        mine = hot & ((prior > 0.5) if k else (prior < 0.5))
        sent[k : k + 1, :] = jnp.sum(jnp.where(mine, source_col, 0.0), axis=0, keepdims=True).astype(I32)
        asked = column(jnp.sum(jnp.where(mine, target_col, 0.0), axis=0, keepdims=True))
        picked = jnp.where(lane == k, asked, picked)
    asking[...] = picked.astype(I32).reshape(asking.shape)


def slot_tables(owner, block_device, source_row, target_row):
    n = owner.shape[1]
    return pl.pallas_call(
        tables_kernel,
        in_specs=[whole(pltpu.HBM)] * 4,
        out_specs=[whole()] * 2,
        out_shape=[jax.ShapeDtypeStruct((2, n), I32), jax.ShapeDtypeStruct((n, 1, LANES), I32)],
        scratch_shapes=[VMEM((4, 1, n), I32), pltpu.SemaphoreType.DMA((4,))],
        compiler_params=params(61),
        cost_estimate=cost(4_000_000, 100_000),
        name="slot_tables",
    )(owner, block_device, source_row, target_row)


def begin(copies):
    for copy in copies:
        copy.start()


def finish(copies):
    for copy in copies:
        copy.wait()


def gather_kernel(
    parity, sent_in, asked_in, flow_in, message_out, tables_out, flow, sent, tables, table, message, sems, out_sems
):
    n = message.shape[0]
    copies = [pltpu.make_async_copy(sent_in, sent, sems.at[0]), pltpu.make_async_copy(flow_in, flow, sems.at[1])]
    begin(copies)
    eye = lax.broadcasted_iota(I32, (n, n), 0) == lax.broadcasted_iota(I32, (n, n), 1)
    columns = asked_in[...].reshape(n, LANES).astype(F32)
    for k in range(2):
        tables[k : k + 1, :] = jnp.sum(jnp.where(eye, columns[:, k : k + 1], 0.0), axis=0, keepdims=True).astype(I32)
    tables[4:8, :] = jnp.full((4, n), parity[0], I32)
    copies[0].wait()
    tables[2:4, :] = sent[...]
    shared = [pltpu.make_async_copy(tables, table, sems.at[2]), pltpu.make_async_copy(tables, tables_out, sems.at[3])]
    begin(shared)
    finish(shared + copies[1:])

    def step(d, carry):
        for part in range(2):
            for k in range(2):
                row = jnp.maximum(table[2 - 2 * part + k, d] - 1, 0)
                for h in range(2):
                    start = 28 * part + 14 * k + NV * h
                    message[d, start : start + NV, :] = flow[row, :, LANES * h : LANES * (h + 1)]
        return carry

    size = n // CHUNKS
    stores = []
    for c in range(CHUNKS):
        lax.fori_loop(c * size, (c + 1) * size, step, 0, unroll=4)
        part = pl.ds(c * size, size)
        stores.append(pltpu.make_async_copy(message.at[part], message_out.at[part], out_sems.at[c]))
        stores[-1].start()
    finish(stores)


def gather(parity, sent, asked, flow):
    devices = asked.shape[0]
    message = (devices, 8 * NV, LANES)
    return pl.pallas_call(
        gather_kernel,
        in_specs=[SMEM, whole(pltpu.HBM), whole(), whole(pltpu.HBM)],
        out_specs=[whole(pltpu.HBM)] * 2,
        out_shape=[jax.ShapeDtypeStruct(message, F32), jax.ShapeDtypeStruct((8, devices), I32)],
        scratch_shapes=[
            VMEM(flow.shape, F32),
            VMEM((2, devices), I32),
            VMEM((8, devices), I32),
            pltpu.SMEM((8, devices), I32),
            VMEM(message, F32),
            pltpu.SemaphoreType.DMA((4,)),
            pltpu.SemaphoreType.DMA((CHUNKS,)),
        ],
        compiler_params=params(58),
        cost_estimate=cost(1_000_000, 6_000_000),
        name="gather",
    )(parity, sent, asked, flow)


def coupled(state, row, coef, mix):
    lane = lax.broadcasted_iota(I32, (8, LANES), 1)
    parts = []
    for direction in range(4):
        factor = coef(direction)
        for v in range(NV):
            if direction < 2:
                first = row + 2 * direction - 1
                pair = [state[2 * v + h, pl.ds(first, 8), :] for h in range(2)]
            else:
                mid = [state[2 * v + h, pl.ds(row, 8), :] for h in range(2)]
                if direction == 2:
                    left, right = (pltpu.roll(m, 1, 1) for m in mid)
                    pair = [jnp.where(lane == 0, 0.0, left), jnp.where(lane == 0, left, right)]
                else:
                    left, right = (pltpu.roll(m, LANES - 1, 1) for m in mid)
                    pair = [jnp.where(lane == LANES - 1, right, left), jnp.where(lane == LANES - 1, 0.0, right)]
            parts.append(factor * jnp.concatenate(pair, axis=1))
    cells = jnp.concatenate(parts, axis=0)
    high = cells.astype(BF16)
    low = (cells - high.astype(F32)).astype(BF16)
    dot = lambda a, b: jnp.dot(a, b, preferred_element_type=F32)
    return dot(mix[0], high) + dot(mix[1], high) + dot(mix[0], low)


def apply_inv(inv, cells):
    out = []
    for i in range(NV):
        total = None
        for j in range(NV):
            term = inv(i, j) * cells[j]
            total = term if j == 0 else total + term
        out.append(total)
    return out


def first_kernel(
    parity, flow, mix, halo_a, halo_b, right, coef, inv, packed_out, inv_out, inv_edges, state, packed, blocks, sems
):
    rows = 8 * TILES
    steps = flow.shape[1] // rows
    even = parity[0] == 0
    reads, writes = [], []
    for c in range(steps):
        part = pl.ds(rows * c, rows)
        reads.append(
            [
                pltpu.make_async_copy(right.at[:, part, :], packed.at[c, NV : 2 * NV], sems.at[0, c]),
                pltpu.make_async_copy(coef.at[:, part, :], packed.at[c, 2 * NV : PACKED], sems.at[1, c]),
                pltpu.make_async_copy(inv.at[:, :, part, :], blocks.at[c], sems.at[2, c]),
            ]
        )
        begin(reads[c])
    for n in range(2 * NV):
        v, h = divmod(n, 2)
        a, b = halo_a[n : n + 1, :], halo_b[n : n + 1, :]
        state[n, 7:8, :] = jnp.where(even, b, a)
        state[n, 8 + rows * steps : 9 + rows * steps, :] = jnp.where(even, a, b)
        state[n, 8 : 8 + rows * steps, :] = flow[v, :, LANES * h : LANES * (h + 1)]

    for c in range(steps):
        finish(reads[c])

        def step(k, carry, c=c):
            here = pl.ds(pl.multiple_of(8 * k, 8), 8)
            row = pl.multiple_of(rows * c + 8 + 8 * k, 8)
            sums = coupled(state, row, lambda d: packed[c, 2 * NV + d, here, :], mix)
            for v in range(NV):
                packed[c, v, here, :] = packed[c, NV + v, here, :] - sums[8 * v : 8 * v + 8, :]
            return carry

        lax.fori_loop(0, TILES, step, 0)
        writes += [
            pltpu.make_async_copy(packed.at[c], packed_out.at[c], sems.at[3, c]),
            pltpu.make_async_copy(blocks.at[c], inv_out.at[c], sems.at[4, c]),
        ]
        begin(writes[-2:])
    inv_edges[0] = blocks[0, :, :, 0:8, :]
    inv_edges[1] = blocks[steps - 1, :, :, rows - 8 : rows, :]
    finish(writes)


def first_sum(parity, flow, right, coef, mix, halo_a, halo_b, inv):
    rows = flow.shape[1]
    steps = rows // (8 * TILES)
    packed = (steps, PACKED, 8 * TILES, COLS)
    blocks = (steps, NV, NV, 8 * TILES, COLS)
    return pl.pallas_call(
        first_kernel,
        in_specs=[SMEM] + [whole()] * 4 + [whole(pltpu.HBM)] * 3,
        out_specs=[whole(pltpu.HBM)] * 2 + [whole()],
        out_shape=[jax.ShapeDtypeStruct(s, F32) for s in (packed, blocks, (2, NV, NV, 8, COLS))],
        scratch_shapes=[
            VMEM((2 * NV, rows + 16, LANES), F32),
            VMEM(packed, F32),
            VMEM(blocks, F32),
            pltpu.SemaphoreType.DMA((5, steps)),
        ],
        compiler_params=params(61),
        cost_estimate=cost(30_000_000, 40_000_000),
        name="first_sum",
    )(parity, flow, mix, halo_a, halo_b, right, coef, inv)


def finish_kernel(
    table_in,
    turn_in,
    message_in,
    packed_in,
    inv_in,
    out,
    edge_a_out,
    edge_b_out,
    table,
    turn,
    message,
    add_left,
    add_right,
    sub_left,
    sub_right,
    packed,
    inv,
    above,
    below,
    ends,
    done,
    edge_a,
    edge_b,
    message_sems,
    sems,
    out_sems,
    small_sems,
):
    steps = packed_in.shape[0]
    rows = 8 * TILES
    count = message.shape[0] // CHUNKS
    plus, minus = (add_left, add_right), (sub_left, sub_right)

    def load(c):
        part = pl.ds(c * count, count)
        return pltpu.make_async_copy(message_in.at[part], message.at[part], message_sems.at[c])

    def fetch(c):
        return [
            pltpu.make_async_copy(packed_in.at[c], packed.at[c + 1], sems.at[0, c]),
            pltpu.make_async_copy(inv_in.at[c], inv.at[c + 1], sems.at[1, c]),
        ]

    def store(c):
        part = pl.ds(pl.multiple_of(rows * c, rows), rows)
        return pltpu.make_async_copy(done.at[c + 1], out.at[:, part, :], out_sems.at[c])

    small = [pltpu.make_async_copy(table_in, table, small_sems.at[0]), pltpu.make_async_copy(turn_in, turn, small_sems.at[1])]
    begin(small)
    begin([load(c) for c in range(CHUNKS)])
    begin(fetch(0))

    def clear(g, carry):
        for ref in plus + minus:
            ref[pl.ds(pl.multiple_of(64 * g, 64), 64), :] = jnp.zeros((64, LANES), F32)
        return carry

    lax.fori_loop(0, add_left.shape[0] // 64, clear, 0)
    for n in range(2 * NV):
        above[n, rows : rows + 8, :] = jnp.zeros((8, LANES), F32)
        below[n, 8 + rows * (steps + 1) : 16 + rows * (steps + 1), :] = jnp.zeros((8, LANES), F32)

    def scatter(d, carry):
        for k in range(2):
            for part, refs in enumerate((plus, minus)):
                row = pl.multiple_of(8 * table[2 * part + k, d], 8)
                for h, ref in enumerate(refs):
                    first = 28 * part + 14 * k + NV * h
                    ref[pl.ds(row, NV), :] += message[d, first : first + NV, :]
        return carry

    finish(small)
    for c in range(CHUNKS):
        load(c).wait()
        if c in (2, 6):
            begin(fetch(1 if c == 2 else 2))
        lax.fori_loop(c * count, (c + 1) * count, scatter, 0, unroll=4)

    lane = lax.broadcasted_iota(I32, (8, COLS), 1)

    def sweep_one(c, k):
        here = slice(8 * k, 8 * k + 8)
        base = pl.multiple_of(64 * TILES * c, 64)
        groups = [pl.ds(base + 64 * k + 8 + v, 8, stride=8) for v in range(NV)]
        source = [jnp.concatenate([p[g, :] - m[g, :] for p, m in zip(plus, minus)], axis=1) for g in groups]
        cells = [packed[c + 1, v, here, :] + source[v] for v in range(NV)]
        relaxed = apply_inv(lambda i, j: inv[c + 1, i, j, here, :], cells)
        if k in (0, TILES - 1):
            end = jnp.minimum(c, 1) if k == 0 else 2
            for v in range(NV):
                ends[end, v] = relaxed[v]
        wide = jnp.concatenate(relaxed + [jnp.zeros((8, COLS), F32)], axis=0)
        high = wide.astype(BF16)
        low = (wide - high.astype(F32)).astype(BF16)
        mixed = jnp.dot(turn[...], jnp.concatenate([high, high, low], axis=0), preferred_element_type=F32)
        piece = lambda d, v: mixed[8 * (NV * d + v) : 8 * (NV * d + v) + 8, :]
        first = pl.multiple_of(rows * (c + 1), rows)
        for v in range(NV):
            for h in range(2):
                half = slice(LANES * h, LANES * (h + 1))
                above[2 * v + h, pl.ds(first + 8 * k + 8, 8), :] = piece(0, v)[:, half]
                below[2 * v + h, pl.ds(first + 8 * k + 8, 8), :] = piece(1, v)[:, half]
            west = jnp.where(lane == 0, 0.0, pltpu.roll(piece(2, v), 1, 1))
            east = jnp.where(lane == COLS - 1, 0.0, pltpu.roll(piece(3, v), COLS - 1, 1))
            share = packed[c + 1, 2 * NV + 2, here, :] * west + packed[c + 1, 2 * NV + 3, here, :] * east
            packed[c + 1, NV + v, here, :] = packed[c + 1, NV + v, here, :] + source[v] - share

    def sweep_two(c, k):
        c, k = (c, k - 1) if k else (c - 1, TILES - 1)
        here = slice(8 * k, 8 * k + 8)
        first = rows * (c + 1)
        cells = []
        for v in range(NV):
            north, south = (
                jnp.concatenate([ref[2 * v + h, pl.ds(first + 8 * k + 8 + shift, 8), :] for h in range(2)], axis=1)
                for ref, shift in ((above, -1), (below, 1))
            )
            share = packed[c + 1, 2 * NV, here, :] * north + packed[c + 1, 2 * NV + 1, here, :] * south
            cells.append(packed[c + 1, NV + v, here, :] - share)
        relaxed = apply_inv(lambda i, j: inv[c + 1, i, j, here, :], cells)
        for v in range(NV):
            done[c + 1, v, here, :] = relaxed[v]

    def step(c, carry):
        finish(fetch(c))

        @pl.when(c + 3 < steps)
        def _():
            begin(fetch(c + 3))

        for k in range(0, TILES, 2):
            sweep_one(c, k)
            sweep_one(c, k + 1)
            sweep_two(c, k)
            sweep_two(c, k + 1)

        @pl.when(c > 0)
        def _():
            store(c - 1).start()

        return carry

    lax.fori_loop(0, steps, step, 0)
    sweep_two(steps, 0)
    store(steps - 1).start()
    even = table[4, 0] == 0
    for v in range(NV):
        top, bottom = ends[0, v][0:1, :], ends[2, v][7:8, :]
        out_a, out_b = jnp.where(even, bottom, top), jnp.where(even, top, bottom)
        for h in range(2):
            n = 2 * v + h
            edge_a[n : n + 1, :] = out_a[:, LANES * h : LANES * (h + 1)]
            edge_b[n : n + 1, :] = out_b[:, LANES * h : LANES * (h + 1)]
    edges = [
        pltpu.make_async_copy(edge_a, edge_a_out, small_sems.at[2]),
        pltpu.make_async_copy(edge_b, edge_b_out, small_sems.at[3]),
    ]
    begin(edges)
    for c in range(steps):
        store(c).wait()
    finish(edges)


def finish_sweeps(tables, turn, message, packed, inv):
    steps = packed.shape[0]
    rows = 8 * TILES * steps
    sums = VMEM((8 * (rows + 8), LANES), F32)
    padded = VMEM((2 * NV, rows + 8 * TILES + 16, LANES), F32)
    slab = (NV, rows, COLS)
    return pl.pallas_call(
        finish_kernel,
        in_specs=[whole(pltpu.HBM)] * 5,
        out_specs=[whole(pltpu.HBM)] * 3,
        out_shape=[jax.ShapeDtypeStruct(s, F32) for s in (slab, (2 * NV, LANES), (2 * NV, LANES))],
        scratch_shapes=[pltpu.SMEM(tables.shape, I32), VMEM(turn.shape, BF16), VMEM(message.shape, F32)]
        + [sums] * 4
        + [VMEM((steps + 1,) + a.shape[1:], F32) for a in (packed, inv)]
        + [padded] * 2
        + [VMEM((3, NV, 8, COLS), F32), VMEM((steps + 1, NV, 8 * TILES, COLS), F32)]
        + [VMEM((2 * NV, LANES), F32)] * 2
        + [pltpu.SemaphoreType.DMA(s) for s in ((CHUNKS,), (2, steps), (steps,), (4,))],
        compiler_params=params(61),
        cost_estimate=cost(45_000_000, 24_000_000),
        name="finish_sweeps",
    )(tables, turn, message, packed, inv)


def edge_kernel(parity, relaxed, coef, mix, inv, halo_a, halo_b, out):
    low = pl.program_id(0) == 0
    use_a = (parity[0] == 0) != low
    place = lax.broadcasted_iota(I32, (8, COLS), 0) == jnp.where(low, 0, 7)
    factor = jnp.where(low, coef[0], coef[1])
    parts = []
    for v in range(NV):
        rows = [jnp.where(use_a, halo_a[n : n + 1, :], halo_b[n : n + 1, :]) for n in (2 * v, 2 * v + 1)]
        row = jnp.broadcast_to(jnp.concatenate(rows, axis=1), (8, COLS))
        parts.append(jnp.where(place, factor * row, 0.0))
    cells = jnp.concatenate(parts, axis=0)
    zero = jnp.zeros_like(cells)
    cells = jnp.concatenate([jnp.where(low, cells, zero), jnp.where(low, zero, cells), zero, zero], axis=0)
    high = cells.astype(BF16)
    rest = (cells - high.astype(F32)).astype(BF16)
    dot = lambda a, b: jnp.dot(a, b, preferred_element_type=F32)
    sums = dot(mix[0], high) + dot(mix[1], high) + dot(mix[0], rest)
    change = apply_inv(lambda i, j: inv[i, j], [sums[8 * v : 8 * v + 8, :] for v in range(NV)])
    for v in range(NV):
        out[v] = relaxed[v] - change[v]


def edge_rows(parity, relaxed, coef, mix, inv, halo_a, halo_b):
    last = relaxed.shape[1] // 8 - 1
    slab = pl.BlockSpec((NV, 8, COLS), lambda g: (0, g * last, 0))
    return pl.pallas_call(
        edge_kernel,
        grid=(2,),
        in_specs=[
            SMEM,
            slab,
            pl.BlockSpec((4, 8, COLS), lambda g: (0, g * last, 0)),
            pl.BlockSpec(mix.shape, lambda g: (0, 0, 0)),
            pl.BlockSpec((None, NV, NV, 8, COLS), lambda g: (g, 0, 0, 0, 0)),
            pl.BlockSpec((2 * NV, LANES), lambda g: (0, 0)),
            pl.BlockSpec((2 * NV, LANES), lambda g: (0, 0)),
        ],
        out_specs=slab,
        out_shape=jax.ShapeDtypeStruct(relaxed.shape, F32),
        input_output_aliases={1: 0},
        compiler_params=params(24),
        cost_estimate=cost(100_000, 900_000),
        name="edge_rows",
    )(parity, relaxed, coef, mix, inv, halo_a, halo_b)


def exchange(edge_a, edge_b):
    size = lax.axis_size("blk")
    pairs_a = [(i, i ^ 1) for i in range(size)]
    pairs_b = [(i, i - 1 if i % 2 == 0 else i + 1) for i in range(1, size - 1)]
    return lax.ppermute(edge_a, "blk", pairs_a), lax.ppermute(edge_b, "blk", pairs_b)


def split(full):
    high = lax.reduce_precision(full, exponent_bits=8, mantissa_bits=7)
    return high.astype(BF16), (full - high).astype(BF16)


def mixing(face_jacobian):
    wide = jnp.transpose(face_jacobian, (1, 0, 2)).reshape(NV, 4 * NV)
    return jnp.stack(split((wide[:, None, :, None] * jnp.eye(8, dtype=F32)[None, :, None, :]).reshape(8 * NV, 32 * NV)))


def turning(face_jacobian):
    tall = jnp.pad(face_jacobian.reshape(4 * NV, NV), ((0, 0), (0, 1)))
    high, low = split((tall[:, None, :, None] * jnp.eye(8, dtype=F32)[None, :, None, :]).reshape(32 * NV, 64))
    return jnp.concatenate([high, low, high], axis=1)


def body(flow_state, right_side, inv_diag, face_coef, face_jacobian, hole_owner, source_row, target_row, block_device):
    flow = jnp.transpose(flow_state[0], (1, 0, 2))
    right = jnp.transpose(right_side[0], (1, 0, 2))
    inv = jnp.transpose(inv_diag[0], (1, 2, 0, 3))
    rows = flow.shape[1]
    parity = (lax.axis_index("blk") % 2).astype(I32).reshape(1)
    as_row = lambda a: a.reshape(1, -1)
    sent, asking = slot_tables(as_row(hole_owner), as_row(block_device), as_row(source_row), as_row(target_row))
    asked = lax.all_to_all(asking, AXES, split_axis=0, concat_axis=0, tiled=True)
    top, bottom = flow[:, 0].reshape(2 * NV, LANES), flow[:, rows - 1].reshape(2 * NV, LANES)
    even = parity[0] == 0
    halo_a, halo_b = exchange(jnp.where(even, bottom, top), jnp.where(even, top, bottom))
    asked, halo_a, halo_b = lax.optimization_barrier((asked, halo_a, halo_b))
    message, tables = gather(parity, sent, asked, flow_state[0])
    message = lax.all_to_all(message, AXES, split_axis=0, concat_axis=0, tiled=True)

    coef = jnp.transpose(face_coef[0], (1, 0, 2))
    mix = mixing(face_jacobian)
    packed, blocks, inv_edges = first_sum(parity, flow, right, coef, mix, halo_a, halo_b, inv)
    relaxed, edge_a, edge_b = finish_sweeps(
        tables, turning(face_jacobian), message, packed, blocks
    )
    halo_a, halo_b = exchange(edge_a, edge_b)
    relaxed = edge_rows(parity, relaxed, coef, mix, inv_edges, halo_a, halo_b)
    return jnp.transpose(relaxed, (1, 0, 2))[None]


def solution(mesh):
    placed = (
        P("zone", "blk", None, None),
        P("zone", "blk", None, None),
        P("zone", "blk", None, None, None),
        P("zone", "blk", None, None),
        P(),
        P(("zone", "blk"), None),
        P(("zone", "blk")),
        P(("zone", "blk")),
        P(),
    )
    return jax.shard_map(
        body, mesh=mesh, in_specs=placed, out_specs=P("zone", "blk", None, None), check_vma=False
    )
```

```python
import jax
import jax.numpy as jnp
from jax import lax
from jax.experimental import pallas as pl
from jax.experimental.pallas import tpu as pltpu
from jax.sharding import PartitionSpec as P

NV = 7
LANES = 128
COLS = 2 * LANES
AXES = ("zone", "blk")
F32 = jnp.float32
BF16 = jnp.bfloat16
I32 = jnp.int32
VMEM = pltpu.VMEM
SMEM = pl.BlockSpec(memory_space=pltpu.SMEM)
MIB = 1 << 20
CHUNKS = 8
TILES = 4
PACKED = 2 * NV + 4


def params(mib):
    return pltpu.CompilerParams(vmem_limit_bytes=mib * MIB)


def cost(flops, bytes_accessed):
    return pl.CostEstimate(flops=flops, bytes_accessed=bytes_accessed, transcendentals=0)


def whole(space=VMEM):
    return pl.BlockSpec(memory_space=space)


def tables_kernel(owner_in, device_in, source_in, target_in, sent, asking, rows, sems):
    n = owner_in.shape[1]
    copies = [
        pltpu.make_async_copy(ref, rows.at[i], sems.at[i])
        for i, ref in enumerate((owner_in, device_in, source_in, target_in))
    ]
    for copy in copies:
        copy.start()
    for copy in copies:
        copy.wait()
    owner, block_device, source_row, target_row = (rows[i].astype(F32) for i in range(4))
    lane = lax.broadcasted_iota(I32, (n, n), 1)
    sub = lax.broadcasted_iota(I32, (n, n), 0)
    eye = lane == sub

    def column(row):
        return jnp.sum(jnp.where(eye, row, 0.0), axis=1, keepdims=True)

    number = lane.astype(F32)
    owner_col = column(owner)
    target = jnp.sum(jnp.where(owner_col == number, block_device, 0.0), axis=1, keepdims=True)
    hot = target == number
    earlier = jnp.where(lane < sub, 1.0, 0.0).astype(BF16)
    prior = jnp.dot(earlier, jnp.where(hot, 1.0, 0.0).astype(BF16), preferred_element_type=F32)
    source_col = column(source_row + 1.0)
    target_col = column(target_row + 1.0)
    picked = jnp.zeros((n, n), F32)
    for k in range(2):
        mine = hot & ((prior > 0.5) if k else (prior < 0.5))
        sent[k : k + 1, :] = jnp.sum(jnp.where(mine, source_col, 0.0), axis=0, keepdims=True).astype(I32)
        asked = column(jnp.sum(jnp.where(mine, target_col, 0.0), axis=0, keepdims=True))
        picked = jnp.where(lane == k, asked, picked)
    asking[...] = picked.astype(I32).reshape(asking.shape)


def slot_tables(owner, block_device, source_row, target_row):
    n = owner.shape[1]
    return pl.pallas_call(
        tables_kernel,
        in_specs=[whole(pltpu.HBM)] * 4,
        out_specs=[whole()] * 2,
        out_shape=[jax.ShapeDtypeStruct((2, n), I32), jax.ShapeDtypeStruct((n, 1, LANES), I32)],
        scratch_shapes=[VMEM((4, 1, n), I32), pltpu.SemaphoreType.DMA((4,))],
        compiler_params=params(61),
        cost_estimate=cost(4_000_000, 100_000),
        name="slot_tables",
    )(owner, block_device, source_row, target_row)


def begin(copies):
    for copy in copies:
        copy.start()


def finish(copies):
    for copy in copies:
        copy.wait()


def gather_kernel(
    sent_in, asked_in, flow_in, message_out, tables_out, flow, sent, asked, tables, table, message, sems, out_sems
):
    n = message.shape[0]
    copies = [
        pltpu.make_async_copy(asked_in, asked, sems.at[4]),
        pltpu.make_async_copy(sent_in, sent, sems.at[0]),
        pltpu.make_async_copy(flow_in, flow, sems.at[1]),
    ]
    begin(copies)
    eye = lax.broadcasted_iota(I32, (n, n), 0) == lax.broadcasted_iota(I32, (n, n), 1)
    finish(copies[:2])
    columns = asked[...].reshape(n, LANES).astype(F32)
    for k in range(2):
        tables[k : k + 1, :] = jnp.sum(jnp.where(eye, columns[:, k : k + 1], 0.0), axis=0, keepdims=True).astype(I32)
    tables[2:4, :] = sent[...]
    shared = [pltpu.make_async_copy(tables, table, sems.at[2]), pltpu.make_async_copy(tables, tables_out, sems.at[3])]
    begin(shared)
    finish(shared + copies[2:])

    def step(d, carry):
        for part in range(2):
            for k in range(2):
                row = jnp.maximum(table[2 - 2 * part + k, d] - 1, 0)
                for h in range(2):
                    start = 28 * part + 14 * k + NV * h
                    message[d, start : start + NV, :] = flow[row, :, LANES * h : LANES * (h + 1)]
        return carry

    size = n // CHUNKS
    stores = []
    for c in range(CHUNKS):
        lax.fori_loop(c * size, (c + 1) * size, step, 0, unroll=4)
        part = pl.ds(c * size, size)
        stores.append(pltpu.make_async_copy(message.at[part], message_out.at[part], out_sems.at[c]))
        stores[-1].start()
    finish(stores)


def gather(sent, asked, flow):
    devices = asked.shape[0]
    message = (devices, 8 * NV, LANES)
    return pl.pallas_call(
        gather_kernel,
        in_specs=[whole(pltpu.HBM)] * 3,
        out_specs=[whole(pltpu.HBM)] * 2,
        out_shape=[jax.ShapeDtypeStruct(message, F32), jax.ShapeDtypeStruct((4, devices), I32)],
        scratch_shapes=[
            VMEM(flow.shape, F32),
            VMEM((2, devices), I32),
            VMEM(asked.shape, I32),
            VMEM((4, devices), I32),
            pltpu.SMEM((4, devices), I32),
            VMEM(message, F32),
            pltpu.SemaphoreType.DMA((5,)),
            pltpu.SemaphoreType.DMA((CHUNKS,)),
        ],
        compiler_params=params(58),
        cost_estimate=cost(1_000_000, 6_000_000),
        name="gather",
    )(sent, asked, flow)


def coupled(state, row, coef, mix):
    lane = lax.broadcasted_iota(I32, (8, LANES), 1)
    parts = []
    for direction in range(4):
        factor = coef(direction)
        for v in range(NV):
            if direction < 2:
                first = row + 2 * direction - 1
                pair = [state[2 * v + h, pl.ds(first, 8), :] for h in range(2)]
            else:
                mid = [state[2 * v + h, pl.ds(row, 8), :] for h in range(2)]
                if direction == 2:
                    left, right = (pltpu.roll(m, 1, 1) for m in mid)
                    pair = [jnp.where(lane == 0, 0.0, left), jnp.where(lane == 0, left, right)]
                else:
                    left, right = (pltpu.roll(m, LANES - 1, 1) for m in mid)
                    pair = [jnp.where(lane == LANES - 1, right, left), jnp.where(lane == LANES - 1, 0.0, right)]
            parts.append(factor * jnp.concatenate(pair, axis=1))
    cells = jnp.concatenate(parts, axis=0)
    high = cells.astype(BF16)
    low = (cells - high.astype(F32)).astype(BF16)
    dot = lambda a, b: jnp.dot(a, b, preferred_element_type=F32)
    return dot(mix[0], high) + dot(mix[1], high) + dot(mix[0], low)


def apply_inv(inv, cells):
    out = []
    for i in range(NV):
        total = None
        for j in range(NV):
            term = inv(i, j) * cells[j]
            total = term if j == 0 else total + term
        out.append(total)
    return out


def first_kernel(
    place, flow, mix, halo_a, halo_b, right, coef, inv, packed_out, inv_out, inv_edges, state, packed, blocks, sems
):
    rows = 8 * TILES
    steps = flow.shape[1] // rows
    even, ahead, behind = (place[i] == 1 for i in range(3))
    reads, writes = [], []
    for c in range(steps):
        part = pl.ds(rows * c, rows)
        reads.append(
            [
                pltpu.make_async_copy(right.at[:, part, :], packed.at[c, NV : 2 * NV], sems.at[0, c]),
                pltpu.make_async_copy(coef.at[:, part, :], packed.at[c, 2 * NV : PACKED], sems.at[1, c]),
                pltpu.make_async_copy(inv.at[:, :, part, :], blocks.at[c], sems.at[2, c]),
            ]
        )
        begin(reads[c])
    for n in range(2 * NV):
        v, h = divmod(n, 2)
        a, b = halo_a[n : n + 1, :], halo_b[n : n + 1, :]
        state[n, 7:8, :] = jnp.where(ahead, jnp.where(even, b, a), 0.0)
        state[n, 8 + rows * steps : 9 + rows * steps, :] = jnp.where(behind, jnp.where(even, a, b), 0.0)
        state[n, 8 : 8 + rows * steps, :] = flow[v, :, LANES * h : LANES * (h + 1)]

    for c in range(steps):
        finish(reads[c])

        def step(k, carry, c=c):
            here = pl.ds(pl.multiple_of(8 * k, 8), 8)
            row = pl.multiple_of(rows * c + 8 + 8 * k, 8)
            sums = coupled(state, row, lambda d: packed[c, 2 * NV + d, here, :], mix)
            for v in range(NV):
                packed[c, v, here, :] = packed[c, NV + v, here, :] - sums[8 * v : 8 * v + 8, :]
            return carry

        lax.fori_loop(0, TILES, step, 0)
        writes += [
            pltpu.make_async_copy(packed.at[c], packed_out.at[c], sems.at[3, c]),
            pltpu.make_async_copy(blocks.at[c], inv_out.at[c], sems.at[4, c]),
        ]
        begin(writes[-2:])
    inv_edges[0] = blocks[0, :, :, 0:8, :]
    inv_edges[1] = blocks[steps - 1, :, :, rows - 8 : rows, :]
    finish(writes)


def first_sum(place, flow, right, coef, mix, halo_a, halo_b, inv):
    rows = flow.shape[1]
    steps = rows // (8 * TILES)
    packed = (steps, PACKED, 8 * TILES, COLS)
    blocks = (steps, NV, NV, 8 * TILES, COLS)
    return pl.pallas_call(
        first_kernel,
        in_specs=[SMEM] + [whole()] * 4 + [whole(pltpu.HBM)] * 3,
        out_specs=[whole(pltpu.HBM)] * 2 + [whole()],
        out_shape=[jax.ShapeDtypeStruct(s, F32) for s in (packed, blocks, (2, NV, NV, 8, COLS))],
        scratch_shapes=[
            VMEM((2 * NV, rows + 16, LANES), F32),
            VMEM(packed, F32),
            VMEM(blocks, F32),
            pltpu.SemaphoreType.DMA((5, steps)),
        ],
        compiler_params=params(61),
        cost_estimate=cost(30_000_000, 40_000_000),
        name="first_sum",
    )(place, flow, mix, halo_a, halo_b, right, coef, inv)


def finish_kernel(
    table_in,
    turn_in,
    message_in,
    packed_in,
    inv_in,
    out,
    top_out,
    bottom_out,
    table,
    turn,
    message,
    add_left,
    add_right,
    sub_left,
    sub_right,
    packed,
    inv,
    above,
    below,
    ends,
    done,
    top,
    bottom,
    message_sems,
    sems,
    out_sems,
    small_sems,
):
    steps = packed_in.shape[0]
    rows = 8 * TILES
    count = message.shape[0] // CHUNKS
    plus, minus = (add_left, add_right), (sub_left, sub_right)

    def load(c):
        part = pl.ds(c * count, count)
        return pltpu.make_async_copy(message_in.at[part], message.at[part], message_sems.at[c])

    def fetch(c):
        return [
            pltpu.make_async_copy(packed_in.at[c], packed.at[c + 1], sems.at[0, c]),
            pltpu.make_async_copy(inv_in.at[c], inv.at[c + 1], sems.at[1, c]),
        ]

    def store(c):
        part = pl.ds(pl.multiple_of(rows * c, rows), rows)
        return pltpu.make_async_copy(done.at[c + 1], out.at[:, part, :], out_sems.at[c])

    small = [pltpu.make_async_copy(table_in, table, small_sems.at[0]), pltpu.make_async_copy(turn_in, turn, small_sems.at[1])]
    begin(small)
    begin([load(c) for c in range(CHUNKS)])
    begin(fetch(0))

    def clear(g, carry):
        for ref in plus + minus:
            ref[pl.ds(pl.multiple_of(64 * g, 64), 64), :] = jnp.zeros((64, LANES), F32)
        return carry

    lax.fori_loop(0, add_left.shape[0] // 64, clear, 0)
    for n in range(2 * NV):
        above[n, rows : rows + 8, :] = jnp.zeros((8, LANES), F32)
        below[n, 8 + rows * (steps + 1) : 16 + rows * (steps + 1), :] = jnp.zeros((8, LANES), F32)

    def scatter(d, carry):
        for k in range(2):
            for part, refs in enumerate((plus, minus)):
                row = pl.multiple_of(8 * table[2 * part + k, d], 8)
                for h, ref in enumerate(refs):
                    first = 28 * part + 14 * k + NV * h
                    ref[pl.ds(row, NV), :] += message[d, first : first + NV, :]
        return carry

    finish(small)
    for c in range(CHUNKS):
        load(c).wait()
        if c in (2, 6):
            begin(fetch(1 if c == 2 else 2))
        lax.fori_loop(c * count, (c + 1) * count, scatter, 0, unroll=4)

    lane = lax.broadcasted_iota(I32, (8, COLS), 1)

    def sweep_one(c, k):
        here = slice(8 * k, 8 * k + 8)
        base = pl.multiple_of(64 * TILES * c, 64)
        groups = [pl.ds(base + 64 * k + 8 + v, 8, stride=8) for v in range(NV)]
        source = [jnp.concatenate([p[g, :] - m[g, :] for p, m in zip(plus, minus)], axis=1) for g in groups]
        cells = [packed[c + 1, v, here, :] + source[v] for v in range(NV)]
        relaxed = apply_inv(lambda i, j: inv[c + 1, i, j, here, :], cells)
        if k in (0, TILES - 1):
            end = jnp.minimum(c, 1) if k == 0 else 2
            for v in range(NV):
                ends[end, v] = relaxed[v]
        wide = jnp.concatenate(relaxed + [jnp.zeros((8, COLS), F32)], axis=0)
        high = wide.astype(BF16)
        low = (wide - high.astype(F32)).astype(BF16)
        mixed = jnp.dot(turn[...], jnp.concatenate([high, high, low], axis=0), preferred_element_type=F32)
        piece = lambda d, v: mixed[8 * (NV * d + v) : 8 * (NV * d + v) + 8, :]
        first = pl.multiple_of(rows * (c + 1), rows)
        for v in range(NV):
            for h in range(2):
                half = slice(LANES * h, LANES * (h + 1))
                above[2 * v + h, pl.ds(first + 8 * k + 8, 8), :] = piece(0, v)[:, half]
                below[2 * v + h, pl.ds(first + 8 * k + 8, 8), :] = piece(1, v)[:, half]
            west = jnp.where(lane == 0, 0.0, pltpu.roll(piece(2, v), 1, 1))
            east = jnp.where(lane == COLS - 1, 0.0, pltpu.roll(piece(3, v), COLS - 1, 1))
            share = packed[c + 1, 2 * NV + 2, here, :] * west + packed[c + 1, 2 * NV + 3, here, :] * east
            packed[c + 1, NV + v, here, :] = packed[c + 1, NV + v, here, :] + source[v] - share

    def sweep_two(c, k):
        c, k = (c, k - 1) if k else (c - 1, TILES - 1)
        here = slice(8 * k, 8 * k + 8)
        first = rows * (c + 1)
        cells = []
        for v in range(NV):
            north, south = (
                jnp.concatenate([ref[2 * v + h, pl.ds(first + 8 * k + 8 + shift, 8), :] for h in range(2)], axis=1)
                for ref, shift in ((above, -1), (below, 1))
            )
            share = packed[c + 1, 2 * NV, here, :] * north + packed[c + 1, 2 * NV + 1, here, :] * south
            cells.append(packed[c + 1, NV + v, here, :] - share)
        relaxed = apply_inv(lambda i, j: inv[c + 1, i, j, here, :], cells)
        for v in range(NV):
            done[c + 1, v, here, :] = relaxed[v]

    def step(c, carry):
        finish(fetch(c))

        @pl.when(c + 3 < steps)
        def _():
            begin(fetch(c + 3))

        for k in range(0, TILES, 2):
            sweep_one(c, k)
            sweep_one(c, k + 1)
            sweep_two(c, k)
            sweep_two(c, k + 1)

        @pl.when(c > 0)
        def _():
            store(c - 1).start()

        return carry

    lax.fori_loop(0, steps, step, 0)
    sweep_two(steps, 0)
    store(steps - 1).start()
    for v in range(NV):
        for h in range(2):
            n = 2 * v + h
            top[n : n + 1, :] = ends[0, v, 0:1, LANES * h : LANES * (h + 1)]
            bottom[n : n + 1, :] = ends[2, v, 7:8, LANES * h : LANES * (h + 1)]
    edges = [
        pltpu.make_async_copy(top, top_out, small_sems.at[2]),
        pltpu.make_async_copy(bottom, bottom_out, small_sems.at[3]),
    ]
    begin(edges)
    for c in range(steps):
        store(c).wait()
    finish(edges)


def finish_sweeps(tables, turn, message, packed, inv):
    steps = packed.shape[0]
    rows = 8 * TILES * steps
    sums = VMEM((8 * (rows + 8), LANES), F32)
    padded = VMEM((2 * NV, rows + 8 * TILES + 16, LANES), F32)
    slab = (NV, rows, COLS)
    return pl.pallas_call(
        finish_kernel,
        in_specs=[whole(pltpu.HBM)] * 5,
        out_specs=[whole(pltpu.HBM)] * 3,
        out_shape=[jax.ShapeDtypeStruct(s, F32) for s in (slab, (2 * NV, LANES), (2 * NV, LANES))],
        scratch_shapes=[pltpu.SMEM(tables.shape, I32), VMEM(turn.shape, BF16), VMEM(message.shape, F32)]
        + [sums] * 4
        + [VMEM((steps + 1,) + a.shape[1:], F32) for a in (packed, inv)]
        + [padded] * 2
        + [VMEM((3, NV, 8, COLS), F32), VMEM((steps + 1, NV, 8 * TILES, COLS), F32)]
        + [VMEM((2 * NV, LANES), F32)] * 2
        + [pltpu.SemaphoreType.DMA(s) for s in ((CHUNKS,), (2, steps), (steps,), (4,))],
        compiler_params=params(61),
        cost_estimate=cost(45_000_000, 24_000_000),
        name="finish_sweeps",
    )(tables, turn, message, packed, inv)


def edge_kernel(
    place, relaxed_in, coef_in, mix_in, inv_in, halo_a_in, halo_b_in, out, ends, coef, mix, inv, halo_a, halo_b, sems
):
    even = place[0] == 1
    tiles = (pl.ds(0, 8), pl.ds(out.shape[1] - 8, 8))
    copies = [
        pltpu.make_async_copy(src, dst, sems.at[i])
        for i, (src, dst) in enumerate(
            [(mix_in, mix), (inv_in, inv), (halo_a_in, halo_a), (halo_b_in, halo_b)]
            + [(relaxed_in.at[:, tile, :], ends.at[g]) for g, tile in enumerate(tiles)]
            + [(coef_in.at[:, tile, :], coef.at[g]) for g, tile in enumerate(tiles)]
        )
    ]
    begin(copies)
    finish(copies)
    sub = lax.broadcasted_iota(I32, (8, COLS), 0)
    zero = jnp.zeros((8 * NV, COLS), F32)
    dot = lambda a, b: jnp.dot(a, b, preferred_element_type=F32)
    for g in range(2):
        use_a = even if g else jnp.logical_not(even)
        mine = (sub == (7 if g else 0)) & (place[1 + g] == 1)
        parts = []
        for v in range(NV):
            rows = [jnp.where(use_a, halo_a[n : n + 1, :], halo_b[n : n + 1, :]) for n in (2 * v, 2 * v + 1)]
            row = jnp.broadcast_to(jnp.concatenate(rows, axis=1), (8, COLS))
            parts.append(jnp.where(mine, coef[g, g] * row, 0.0))
        cells = jnp.concatenate([zero] * g + parts + [zero] * (3 - g), axis=0)
        high = cells.astype(BF16)
        low = (cells - high.astype(F32)).astype(BF16)
        sums = dot(mix[0], high) + dot(mix[1], high) + dot(mix[0], low)
        change = apply_inv(lambda i, j, g=g: inv[g, i, j], [sums[8 * v : 8 * v + 8, :] for v in range(NV)])
        for v in range(NV):
            ends[g, v] = ends[g, v] - change[v]
    writes = [pltpu.make_async_copy(ends.at[g], out.at[:, tile, :], sems.at[g]) for g, tile in enumerate(tiles)]
    begin(writes)
    finish(writes)


def edge_rows(place, relaxed, coef, mix, inv, halo_a, halo_b):
    return pl.pallas_call(
        edge_kernel,
        in_specs=[SMEM] + [whole(pltpu.HBM)] * 6,
        out_specs=whole(pltpu.HBM),
        out_shape=jax.ShapeDtypeStruct(relaxed.shape, F32),
        scratch_shapes=[
            VMEM((2, NV, 8, COLS), F32),
            VMEM((2, 4, 8, COLS), F32),
            VMEM(mix.shape, BF16),
            VMEM(inv.shape, F32),
            VMEM(halo_a.shape, F32),
            VMEM(halo_b.shape, F32),
            pltpu.SemaphoreType.DMA((8,)),
        ],
        input_output_aliases={1: 0},
        compiler_params=params(40),
        cost_estimate=cost(100_000, 900_000),
        name="edge_rows",
    )(place, relaxed, coef, mix, inv, halo_a, halo_b)


def exchange(top, bottom, even):
    zones, size = lax.axis_size("zone"), lax.axis_size("blk")
    pairs_a = [(i, i ^ 1) for i in range(size)]
    pairs_b = []
    for z in range(zones):
        for i in range(size):
            other, j = z, i - 1 if i % 2 == 0 else i + 1
            if not 0 <= j < size:
                other, j = z ^ 1, i
            pairs_b.append((z * size + i, other * size + j))
    edge_a, edge_b = jnp.where(even, bottom, top), jnp.where(even, top, bottom)
    return lax.ppermute(edge_a, "blk", pairs_a), lax.ppermute(edge_b, AXES, pairs_b)


def split(full):
    high = lax.reduce_precision(full, exponent_bits=8, mantissa_bits=7)
    return high.astype(BF16), (full - high).astype(BF16)


def mixing(face_jacobian):
    wide = jnp.transpose(face_jacobian, (1, 0, 2)).reshape(NV, 4 * NV)
    return jnp.stack(split((wide[:, None, :, None] * jnp.eye(8, dtype=F32)[None, :, None, :]).reshape(8 * NV, 32 * NV)))


def turning(face_jacobian):
    tall = jnp.pad(face_jacobian.reshape(4 * NV, NV), ((0, 0), (0, 1)))
    high, low = split((tall[:, None, :, None] * jnp.eye(8, dtype=F32)[None, :, None, :]).reshape(32 * NV, 64))
    return jnp.concatenate([high, low, high], axis=1)


def body(flow_state, right_side, inv_diag, face_coef, face_jacobian, hole_owner, source_row, target_row, block_device):
    flow = jnp.transpose(flow_state[0], (1, 0, 2))
    right = jnp.transpose(right_side[0], (1, 0, 2))
    inv = jnp.transpose(inv_diag[0], (1, 2, 0, 3))
    rows = flow.shape[1]
    slab = lax.axis_index("blk")
    even = slab % 2 == 0
    place = jnp.stack([even, slab > 0, slab < lax.axis_size("blk") - 1]).astype(I32)
    as_row = lambda a: a.reshape(1, -1)
    sent, asking = slot_tables(as_row(hole_owner), as_row(block_device), as_row(source_row), as_row(target_row))
    asked = lax.all_to_all(asking, AXES, split_axis=0, concat_axis=0, tiled=True)
    top, bottom = flow[:, 0].reshape(2 * NV, LANES), flow[:, rows - 1].reshape(2 * NV, LANES)
    halo_a, halo_b = exchange(top, bottom, even)
    asked, halo_a, halo_b = lax.optimization_barrier((asked, halo_a, halo_b))
    message, tables = gather(sent, asked, flow_state[0])
    message = lax.all_to_all(message, AXES, split_axis=0, concat_axis=0, tiled=True)

    coef = jnp.transpose(face_coef[0], (1, 0, 2))
    mix = mixing(face_jacobian)
    packed, blocks, inv_edges = first_sum(place, flow, right, coef, mix, halo_a, halo_b, inv)
    relaxed, top, bottom = finish_sweeps(
        tables, turning(face_jacobian), message, packed, blocks
    )
    halo_a, halo_b = exchange(top, bottom, even)
    relaxed = edge_rows(place, relaxed, coef, mix, inv_edges, halo_a, halo_b)
    return jnp.transpose(relaxed, (1, 0, 2))[None]


def solution(mesh):
    placed = (
        P("zone", "blk", None, None),
        P("zone", "blk", None, None),
        P("zone", "blk", None, None, None),
        P("zone", "blk", None, None),
        P(),
        P(("zone", "blk"), None),
        P(("zone", "blk")),
        P(("zone", "blk")),
        P(),
    )
    return jax.shard_map(
        body, mesh=mesh, in_specs=placed, out_specs=P("zone", "blk", None, None), check_vma=False
    )
```

```python
import jax
import jax.numpy as jnp
from jax import lax
from jax.experimental import pallas as pl
from jax.experimental.pallas import tpu as pltpu
from jax.sharding import PartitionSpec as P

NV = 7
LANES = 128
COLS = 2 * LANES
AXES = ("zone", "blk")
F32 = jnp.float32
BF16 = jnp.bfloat16
I32 = jnp.int32
VMEM = pltpu.VMEM
SMEM = pl.BlockSpec(memory_space=pltpu.SMEM)
MIB = 1 << 20
CHUNKS = 8
TILES = 4
PACKED = 2 * NV + 4


def params(mib):
    return pltpu.CompilerParams(vmem_limit_bytes=mib * MIB)


def cost(flops, bytes_accessed):
    return pl.CostEstimate(flops=flops, bytes_accessed=bytes_accessed, transcendentals=0)


def whole(space=VMEM):
    return pl.BlockSpec(memory_space=space)


def tables_kernel(owner_in, device_in, source_in, target_in, sent, asking, rows, sems):
    n = owner_in.shape[1]
    copies = [
        pltpu.make_async_copy(ref, rows.at[i], sems.at[i])
        for i, ref in enumerate((owner_in, device_in, source_in, target_in))
    ]
    for copy in copies:
        copy.start()
    for copy in copies:
        copy.wait()
    owner, block_device, source_row, target_row = (rows[i].astype(F32) for i in range(4))
    lane = lax.broadcasted_iota(I32, (n, n), 1)
    sub = lax.broadcasted_iota(I32, (n, n), 0)
    eye = lane == sub

    def column(row):
        return jnp.sum(jnp.where(eye, row, 0.0), axis=1, keepdims=True)

    number = lane.astype(F32)
    owner_col = column(owner)
    target = jnp.sum(jnp.where(owner_col == number, block_device, 0.0), axis=1, keepdims=True)
    hot = target == number
    earlier = jnp.where(lane < sub, 1.0, 0.0).astype(BF16)
    prior = jnp.dot(earlier, jnp.where(hot, 1.0, 0.0).astype(BF16), preferred_element_type=F32)
    source_col = column(source_row + 1.0)
    target_col = column(target_row + 1.0)
    picked = jnp.zeros((n, n), F32)
    for k in range(2):
        mine = hot & ((prior > 0.5) if k else (prior < 0.5))
        sent[k : k + 1, :] = jnp.sum(jnp.where(mine, source_col, 0.0), axis=0, keepdims=True).astype(I32)
        asked = column(jnp.sum(jnp.where(mine, target_col, 0.0), axis=0, keepdims=True))
        picked = jnp.where(lane == k, asked, picked)
    asking[...] = picked.astype(I32).reshape(asking.shape)


def slot_tables(owner, block_device, source_row, target_row):
    n = owner.shape[1]
    return pl.pallas_call(
        tables_kernel,
        in_specs=[whole(pltpu.HBM)] * 4,
        out_specs=[whole()] * 2,
        out_shape=[jax.ShapeDtypeStruct((2, n), I32), jax.ShapeDtypeStruct((n, 1, LANES), I32)],
        scratch_shapes=[VMEM((4, 1, n), I32), pltpu.SemaphoreType.DMA((4,))],
        compiler_params=params(61),
        cost_estimate=cost(4_000_000, 100_000),
        name="slot_tables",
    )(owner, block_device, source_row, target_row)


def begin(copies):
    for copy in copies:
        copy.start()


def finish(copies):
    for copy in copies:
        copy.wait()


def gather_kernel(
    sent_in, asked_in, flow_in, message_out, tables_out, flow, sent, asked, tables, table, message, sems, out_sems
):
    n = message.shape[0]
    copies = [
        pltpu.make_async_copy(asked_in, asked, sems.at[4]),
        pltpu.make_async_copy(sent_in, sent, sems.at[0]),
        pltpu.make_async_copy(flow_in, flow, sems.at[1]),
    ]
    begin(copies)
    eye = lax.broadcasted_iota(I32, (n, n), 0) == lax.broadcasted_iota(I32, (n, n), 1)
    copies[0].wait()
    columns = asked[...].reshape(n, LANES).astype(F32)
    for k in range(2):
        tables[k : k + 1, :] = jnp.sum(jnp.where(eye, columns[:, k : k + 1], 0.0), axis=0, keepdims=True).astype(I32)
    to_scalar = pltpu.make_async_copy(tables, table, sems.at[2])
    to_scalar.start()
    finish(copies[1:])

    def rows_of(source, part):
        def step(d, carry):
            for k in range(2):
                row = jnp.maximum(source[k, d] - 1, 0)
                for h in range(2):
                    start = 28 * part + 14 * k + NV * h
                    message[d, start : start + NV, :] = flow[row, :, LANES * h : LANES * (h + 1)]
            return carry

        return step

    lax.fori_loop(0, n, rows_of(sent, 0), 0, unroll=8)
    to_scalar.wait()
    stores = [pltpu.make_async_copy(tables, tables_out, sems.at[3])]
    stores[0].start()
    size = n // CHUNKS
    for c in range(CHUNKS):
        lax.fori_loop(c * size, (c + 1) * size, rows_of(table, 1), 0, unroll=8)
        part = pl.ds(c * size, size)
        stores.append(pltpu.make_async_copy(message.at[part], message_out.at[part], out_sems.at[c]))
        stores[-1].start()
    finish(stores)


def gather(sent, asked, flow):
    devices = asked.shape[0]
    message = (devices, 8 * NV, LANES)
    return pl.pallas_call(
        gather_kernel,
        in_specs=[whole(pltpu.HBM)] * 3,
        out_specs=[whole(pltpu.HBM)] * 2,
        out_shape=[jax.ShapeDtypeStruct(message, F32), jax.ShapeDtypeStruct((2, devices), I32)],
        scratch_shapes=[
            VMEM(flow.shape, F32),
            pltpu.SMEM((2, devices), I32),
            VMEM(asked.shape, I32),
            VMEM((2, devices), I32),
            pltpu.SMEM((2, devices), I32),
            VMEM(message, F32),
            pltpu.SemaphoreType.DMA((5,)),
            pltpu.SemaphoreType.DMA((CHUNKS,)),
        ],
        compiler_params=params(58),
        cost_estimate=cost(1_000_000, 6_000_000),
        name="gather",
    )(sent, asked, flow)


def coupled(state, row, coef, mix):
    lane = lax.broadcasted_iota(I32, (8, LANES), 1)
    parts = []
    for direction in range(4):
        factor = coef(direction)
        for v in range(NV):
            if direction < 2:
                first = row + 2 * direction - 1
                pair = [state[2 * v + h, pl.ds(first, 8), :] for h in range(2)]
            else:
                mid = [state[2 * v + h, pl.ds(row, 8), :] for h in range(2)]
                if direction == 2:
                    left, right = (pltpu.roll(m, 1, 1) for m in mid)
                    pair = [jnp.where(lane == 0, 0.0, left), jnp.where(lane == 0, left, right)]
                else:
                    left, right = (pltpu.roll(m, LANES - 1, 1) for m in mid)
                    pair = [jnp.where(lane == LANES - 1, right, left), jnp.where(lane == LANES - 1, 0.0, right)]
            parts.append(factor * jnp.concatenate(pair, axis=1))
    cells = jnp.concatenate(parts, axis=0)
    high = cells.astype(BF16)
    low = (cells - high.astype(F32)).astype(BF16)
    dot = lambda a, b: jnp.dot(a, b, preferred_element_type=F32)
    return dot(mix[0], high) + dot(mix[1], high) + dot(mix[0], low)


def apply_inv(inv, cells):
    out = []
    for i in range(NV):
        total = None
        for j in range(NV):
            term = inv(i, j) * cells[j]
            total = term if j == 0 else total + term
        out.append(total)
    return out


def first_kernel(
    place, jac, flow, mix, halo_a, halo_b, right, coef, inv, packed_out, inv_out, operators, state, packed, blocks, sems
):
    rows = 8 * TILES
    steps = flow.shape[1] // rows
    even, ahead, behind = (place[0, i] == 1 for i in range(3))
    reads, writes = [], []
    for c in range(steps):
        part = pl.ds(rows * c, rows)
        reads.append(
            [
                pltpu.make_async_copy(right.at[:, part, :], packed.at[c, NV : 2 * NV], sems.at[0, c]),
                pltpu.make_async_copy(coef.at[:, part, :], packed.at[c, 2 * NV : PACKED], sems.at[1, c]),
                pltpu.make_async_copy(inv.at[:, :, part, :], blocks.at[c], sems.at[2, c]),
            ]
        )
        begin(reads[c])
    for n in range(2 * NV):
        v, h = divmod(n, 2)
        a, b = halo_a[n : n + 1, :], halo_b[n : n + 1, :]
        state[n, 7:8, :] = jnp.where(ahead, jnp.where(even, b, a), 0.0)
        state[n, 8 + rows * steps : 9 + rows * steps, :] = jnp.where(behind, jnp.where(even, a, b), 0.0)
        state[n, 8 : 8 + rows * steps, :] = flow[v, :, LANES * h : LANES * (h + 1)]

    for c in range(steps):
        finish(reads[c])

        def step(k, carry, c=c):
            here = pl.ds(pl.multiple_of(8 * k, 8), 8)
            row = pl.multiple_of(rows * c + 8 + 8 * k, 8)
            sums = coupled(state, row, lambda d: packed[c, 2 * NV + d, here, :], mix)
            for v in range(NV):
                packed[c, v, here, :] = packed[c, NV + v, here, :] - sums[8 * v : 8 * v + 8, :]
            return carry

        lax.fori_loop(0, TILES, step, 0)
        writes += [
            pltpu.make_async_copy(packed.at[c], packed_out.at[c], sems.at[3, c]),
            pltpu.make_async_copy(blocks.at[c], inv_out.at[c], sems.at[4, c]),
        ]
        begin(writes[-2:])
    for g, (there, c, row) in enumerate(((ahead, 0, 0), (behind, steps - 1, rows - 1))):
        factor = jnp.where(there, packed[c, 2 * NV + g, row : row + 1, :], 0.0)
        for i in range(NV):
            weights = [factor * blocks[c, i, k, row : row + 1, :] for k in range(NV)]
            for j in range(NV):
                total = jac[NV * NV * g + j] * weights[0]
                for k in range(1, NV):
                    total = total + jac[NV * (NV * g + k) + j] * weights[k]
                operators[g, j, i : i + 1, :] = total
    finish(writes)


def first_sum(place, jac, flow, right, coef, mix, halo_a, halo_b, inv):
    rows = flow.shape[1]
    steps = rows // (8 * TILES)
    packed = (steps, PACKED, 8 * TILES, COLS)
    blocks = (steps, NV, NV, 8 * TILES, COLS)
    return pl.pallas_call(
        first_kernel,
        in_specs=[SMEM] * 2 + [whole()] * 4 + [whole(pltpu.HBM)] * 3,
        out_specs=[whole(pltpu.HBM)] * 2 + [whole()],
        out_shape=[jax.ShapeDtypeStruct(s, F32) for s in (packed, blocks, (2, NV, 8, COLS))],
        scratch_shapes=[
            VMEM((2 * NV, rows + 16, LANES), F32),
            VMEM(packed, F32),
            VMEM(blocks, F32),
            pltpu.SemaphoreType.DMA((5, steps)),
        ],
        compiler_params=params(61),
        cost_estimate=cost(30_000_000, 40_000_000),
        name="first_sum",
    )(place, jac, flow, mix, halo_a, halo_b, right, coef, inv)


def finish_kernel(
    asked_in,
    sent_in,
    place_in,
    turn_in,
    message_in,
    packed_in,
    inv_in,
    out,
    edge_a_out,
    edge_b_out,
    asked,
    sent,
    place,
    turn,
    message,
    add_left,
    add_right,
    sub_left,
    sub_right,
    packed,
    inv,
    above,
    below,
    ends,
    done,
    edge_a,
    edge_b,
    message_sems,
    sems,
    out_sems,
    small_sems,
):
    steps = packed_in.shape[0]
    rows = 8 * TILES
    count = message.shape[0] // CHUNKS
    plus, minus = (add_left, add_right), (sub_left, sub_right)

    def load(c):
        part = pl.ds(c * count, count)
        return pltpu.make_async_copy(message_in.at[part], message.at[part], message_sems.at[c])

    def fetch(c):
        return [
            pltpu.make_async_copy(packed_in.at[c], packed.at[c + 1], sems.at[0, c]),
            pltpu.make_async_copy(inv_in.at[c], inv.at[c + 1], sems.at[1, c]),
        ]

    def store(c):
        part = pl.ds(pl.multiple_of(rows * c, rows), rows)
        return pltpu.make_async_copy(done.at[c + 1], out.at[:, part, :], out_sems.at[c])

    pairs = ((asked_in, asked), (sent_in, sent), (place_in, place), (turn_in, turn))
    small = [pltpu.make_async_copy(src, dst, small_sems.at[i]) for i, (src, dst) in enumerate(pairs)]
    begin(small)
    begin([load(c) for c in range(CHUNKS)])
    begin(fetch(0))

    def clear(g, carry):
        for ref in plus + minus:
            ref[pl.ds(pl.multiple_of(64 * g, 64), 64), :] = jnp.zeros((64, LANES), F32)
        return carry

    lax.fori_loop(0, add_left.shape[0] // 64, clear, 0)
    for n in range(2 * NV):
        above[n, rows : rows + 8, :] = jnp.zeros((8, LANES), F32)
        below[n, 8 + rows * (steps + 1) : 16 + rows * (steps + 1), :] = jnp.zeros((8, LANES), F32)

    def scatter(d, carry):
        for k in range(2):
            for part, (table, refs) in enumerate(((asked, plus), (sent, minus))):
                row = pl.multiple_of(8 * table[k, d], 8)
                for h, ref in enumerate(refs):
                    first = 28 * part + 14 * k + NV * h
                    ref[pl.ds(row, NV), :] += message[d, first : first + NV, :]
        return carry

    finish(small)
    for c in range(CHUNKS):
        load(c).wait()
        if c in (2, 6):
            begin(fetch(1 if c == 2 else 2))
        lax.fori_loop(c * count, (c + 1) * count, scatter, 0, unroll=4)

    lane = lax.broadcasted_iota(I32, (8, COLS), 1)

    def sweep_one(c, k):
        here = slice(8 * k, 8 * k + 8)
        base = pl.multiple_of(64 * TILES * c, 64)
        groups = [pl.ds(base + 64 * k + 8 + v, 8, stride=8) for v in range(NV)]
        source = [jnp.concatenate([p[g, :] - m[g, :] for p, m in zip(plus, minus)], axis=1) for g in groups]
        cells = [packed[c + 1, v, here, :] + source[v] for v in range(NV)]
        relaxed = apply_inv(lambda i, j: inv[c + 1, i, j, here, :], cells)
        if k in (0, TILES - 1):
            end = jnp.minimum(c, 1) if k == 0 else 2
            for v in range(NV):
                ends[end, v] = relaxed[v]
        wide = jnp.concatenate(relaxed + [jnp.zeros((8, COLS), F32)], axis=0)
        high = wide.astype(BF16)
        low = (wide - high.astype(F32)).astype(BF16)
        mixed = jnp.dot(turn[...], jnp.concatenate([high, high, low], axis=0), preferred_element_type=F32)
        piece = lambda d, v: mixed[8 * (NV * d + v) : 8 * (NV * d + v) + 8, :]
        first = pl.multiple_of(rows * (c + 1), rows)
        for v in range(NV):
            for h in range(2):
                half = slice(LANES * h, LANES * (h + 1))
                above[2 * v + h, pl.ds(first + 8 * k + 8, 8), :] = piece(0, v)[:, half]
                below[2 * v + h, pl.ds(first + 8 * k + 8, 8), :] = piece(1, v)[:, half]
            west = jnp.where(lane == 0, 0.0, pltpu.roll(piece(2, v), 1, 1))
            east = jnp.where(lane == COLS - 1, 0.0, pltpu.roll(piece(3, v), COLS - 1, 1))
            share = packed[c + 1, 2 * NV + 2, here, :] * west + packed[c + 1, 2 * NV + 3, here, :] * east
            packed[c + 1, NV + v, here, :] = packed[c + 1, NV + v, here, :] + source[v] - share

    def sweep_two(c, k):
        c, k = (c, k - 1) if k else (c - 1, TILES - 1)
        here = slice(8 * k, 8 * k + 8)
        first = rows * (c + 1)
        cells = []
        for v in range(NV):
            north, south = (
                jnp.concatenate([ref[2 * v + h, pl.ds(first + 8 * k + 8 + shift, 8), :] for h in range(2)], axis=1)
                for ref, shift in ((above, -1), (below, 1))
            )
            share = packed[c + 1, 2 * NV, here, :] * north + packed[c + 1, 2 * NV + 1, here, :] * south
            cells.append(packed[c + 1, NV + v, here, :] - share)
        relaxed = apply_inv(lambda i, j: inv[c + 1, i, j, here, :], cells)
        for v in range(NV):
            done[c + 1, v, here, :] = relaxed[v]

    def step(c, carry):
        finish(fetch(c))

        @pl.when(c + 3 < steps)
        def _():
            begin(fetch(c + 3))

        for k in range(0, TILES, 2):
            sweep_one(c, k)
            sweep_one(c, k + 1)
            sweep_two(c, k)
            sweep_two(c, k + 1)

        @pl.when(c > 0)
        def _():
            store(c - 1).start()

        return carry

    lax.fori_loop(0, steps, step, 0)
    sweep_two(steps, 0)
    store(steps - 1).start()
    even = place[0, 0] == 1
    for v in range(NV):
        top, bottom = ends[0, v, 0:1, :], ends[2, v, 7:8, :]
        out_a, out_b = jnp.where(even, bottom, top), jnp.where(even, top, bottom)
        for h in range(2):
            n = 2 * v + h
            edge_a[n : n + 1, :] = out_a[:, LANES * h : LANES * (h + 1)]
            edge_b[n : n + 1, :] = out_b[:, LANES * h : LANES * (h + 1)]
    edges = [
        pltpu.make_async_copy(edge_a, edge_a_out, small_sems.at[4]),
        pltpu.make_async_copy(edge_b, edge_b_out, small_sems.at[5]),
    ]
    begin(edges)
    for c in range(steps):
        store(c).wait()
    finish(edges)


def finish_sweeps(asked, sent, place, turn, message, packed, inv):
    steps = packed.shape[0]
    rows = 8 * TILES * steps
    sums = VMEM((8 * (rows + 8), LANES), F32)
    padded = VMEM((2 * NV, rows + 8 * TILES + 16, LANES), F32)
    slab = (NV, rows, COLS)
    return pl.pallas_call(
        finish_kernel,
        in_specs=[whole(pltpu.HBM)] * 7,
        out_specs=[whole(pltpu.HBM)] * 3,
        out_shape=[jax.ShapeDtypeStruct(s, F32) for s in (slab, (2 * NV, LANES), (2 * NV, LANES))],
        scratch_shapes=[pltpu.SMEM(a.shape, I32) for a in (asked, sent, place)]
        + [VMEM(turn.shape, BF16), VMEM(message.shape, F32)]
        + [sums] * 4
        + [VMEM((steps + 1,) + a.shape[1:], F32) for a in (packed, inv)]
        + [padded] * 2
        + [VMEM((3, NV, 8, COLS), F32), VMEM((steps + 1, NV, 8 * TILES, COLS), F32)]
        + [VMEM((2 * NV, LANES), F32)] * 2
        + [pltpu.SemaphoreType.DMA(s) for s in ((CHUNKS,), (2, steps), (steps,), (6,))],
        compiler_params=params(61),
        cost_estimate=cost(45_000_000, 24_000_000),
        name="finish_sweeps",
    )(asked, sent, place, turn, message, packed, inv)


def edge_kernel(place, relaxed, operators, halo_a, halo_b, out, ends, sems):
    even = place[0, 0] == 1
    tiles = (pl.ds(0, 8), pl.ds(out.shape[1] - 8, 8))
    reads = [pltpu.make_async_copy(relaxed.at[:, tile, :], ends.at[g], sems.at[g]) for g, tile in enumerate(tiles)]
    begin(reads)
    changes = []
    for g in range(2):
        use_a = even if g else jnp.logical_not(even)
        total = None
        for j in range(NV):
            halves = [jnp.where(use_a, halo_a[n : n + 1, :], halo_b[n : n + 1, :]) for n in (2 * j, 2 * j + 1)]
            term = operators[g, j] * jnp.concatenate(halves, axis=1)
            total = term if j == 0 else total + term
        changes.append(total)
    finish(reads)
    for g, row in enumerate((0, 7)):
        for v in range(NV):
            ends[g, v, row : row + 1, :] = ends[g, v, row : row + 1, :] - changes[g][v : v + 1, :]
    writes = [pltpu.make_async_copy(ends.at[g], out.at[:, tile, :], sems.at[g]) for g, tile in enumerate(tiles)]
    begin(writes)
    finish(writes)


def edge_rows(place, relaxed, operators, halo_a, halo_b):
    return pl.pallas_call(
        edge_kernel,
        in_specs=[SMEM, whole(pltpu.HBM)] + [whole()] * 3,
        out_specs=whole(pltpu.HBM),
        out_shape=jax.ShapeDtypeStruct(relaxed.shape, F32),
        scratch_shapes=[VMEM((2, NV, 8, COLS), F32), pltpu.SemaphoreType.DMA((2,))],
        input_output_aliases={1: 0},
        compiler_params=params(24),
        cost_estimate=cost(100_000, 400_000),
        name="edge_rows",
    )(place, relaxed, operators, halo_a, halo_b)


def exchange(edge_a, edge_b):
    zones, size = lax.axis_size("zone"), lax.axis_size("blk")
    pairs_a = [(i, i ^ 1) for i in range(size)]
    pairs_b = []
    for z in range(zones):
        for i in range(size):
            other, j = z, i - 1 if i % 2 == 0 else i + 1
            if not 0 <= j < size:
                other, j = z ^ 1, i
            pairs_b.append((z * size + i, other * size + j))
    return lax.ppermute(edge_a, "blk", pairs_a), lax.ppermute(edge_b, AXES, pairs_b)


def split(full):
    high = lax.reduce_precision(full, exponent_bits=8, mantissa_bits=7)
    return high.astype(BF16), (full - high).astype(BF16)


def mixing(face_jacobian):
    wide = jnp.transpose(face_jacobian, (1, 0, 2)).reshape(NV, 4 * NV)
    return jnp.stack(split((wide[:, None, :, None] * jnp.eye(8, dtype=F32)[None, :, None, :]).reshape(8 * NV, 32 * NV)))


def turning(face_jacobian):
    tall = jnp.pad(face_jacobian.reshape(4 * NV, NV), ((0, 0), (0, 1)))
    high, low = split((tall[:, None, :, None] * jnp.eye(8, dtype=F32)[None, :, None, :]).reshape(32 * NV, 64))
    return jnp.concatenate([high, low, high], axis=1)


def body(flow_state, right_side, inv_diag, face_coef, face_jacobian, hole_owner, source_row, target_row, block_device):
    flow = jnp.transpose(flow_state[0], (1, 0, 2))
    right = jnp.transpose(right_side[0], (1, 0, 2))
    inv = jnp.transpose(inv_diag[0], (1, 2, 0, 3))
    rows = flow.shape[1]
    slab = lax.axis_index("blk")
    even = slab % 2 == 0
    flags = jnp.stack([even, slab > 0, slab < lax.axis_size("blk") - 1]).astype(I32)
    place = jnp.pad(flags, (0, LANES - 3)).reshape(1, LANES)
    as_row = lambda a: a.reshape(1, -1)
    sent, asking = slot_tables(as_row(hole_owner), as_row(block_device), as_row(source_row), as_row(target_row))
    asked = lax.all_to_all(asking, AXES, split_axis=0, concat_axis=0, tiled=True)
    top, bottom = flow[:, 0].reshape(2 * NV, LANES), flow[:, rows - 1].reshape(2 * NV, LANES)
    halo_a, halo_b = exchange(jnp.where(even, bottom, top), jnp.where(even, top, bottom))
    asked, halo_a, halo_b = lax.optimization_barrier((asked, halo_a, halo_b))
    message, asked = gather(sent, asked, flow_state[0])
    message = lax.all_to_all(message, AXES, split_axis=0, concat_axis=0, tiled=True)

    coef = jnp.transpose(face_coef[0], (1, 0, 2))
    mix = mixing(face_jacobian)
    jac = face_jacobian.reshape(-1)
    packed, blocks, operators = first_sum(place, jac, flow, right, coef, mix, halo_a, halo_b, inv)
    relaxed, edge_a, edge_b = finish_sweeps(
        asked, sent, place, turning(face_jacobian), message, packed, blocks
    )
    halo_a, halo_b = exchange(edge_a, edge_b)
    relaxed = edge_rows(place, relaxed, operators, halo_a, halo_b)
    return jnp.transpose(relaxed, (1, 0, 2))[None]


def solution(mesh):
    placed = (
        P("zone", "blk", None, None),
        P("zone", "blk", None, None),
        P("zone", "blk", None, None, None),
        P("zone", "blk", None, None),
        P(),
        P(("zone", "blk"), None),
        P(("zone", "blk")),
        P(("zone", "blk")),
        P(),
    )
    return jax.shard_map(
        body, mesh=mesh, in_specs=placed, out_specs=P("zone", "blk", None, None), check_vma=False
    )
```

```python
import jax
import jax.numpy as jnp
from jax import lax
from jax.experimental import pallas as pl
from jax.experimental.pallas import tpu as pltpu
from jax.sharding import PartitionSpec as P

NV = 7
LANES = 128
COLS = 2 * LANES
AXES = ("zone", "blk")
F32 = jnp.float32
BF16 = jnp.bfloat16
I32 = jnp.int32
VMEM = pltpu.VMEM
SMEM = pl.BlockSpec(memory_space=pltpu.SMEM)
MIB = 1 << 20
CHUNKS = 8
TILES = 4
PACKED = 2 * NV + 4


def params(mib):
    return pltpu.CompilerParams(vmem_limit_bytes=mib * MIB)


def cost(flops, bytes_accessed):
    return pl.CostEstimate(flops=flops, bytes_accessed=bytes_accessed, transcendentals=0)


def whole(space=VMEM):
    return pl.BlockSpec(memory_space=space)


def tables_kernel(owner_in, device_in, source_in, target_in, sent, asking, rows, sems):
    n = owner_in.shape[1]
    copies = [
        pltpu.make_async_copy(ref, rows.at[i], sems.at[i])
        for i, ref in enumerate((owner_in, device_in, source_in, target_in))
    ]
    for copy in copies:
        copy.start()
    for copy in copies:
        copy.wait()
    owner, block_device, source_row, target_row = (rows[i].astype(F32) for i in range(4))
    lane = lax.broadcasted_iota(I32, (n, n), 1)
    sub = lax.broadcasted_iota(I32, (n, n), 0)
    eye = lane == sub

    def column(row):
        return jnp.sum(jnp.where(eye, row, 0.0), axis=1, keepdims=True)

    number = lane.astype(F32)
    owner_col = column(owner)
    target = jnp.sum(jnp.where(owner_col == number, block_device, 0.0), axis=1, keepdims=True)
    hot = target == number
    earlier = jnp.where(lane < sub, 1.0, 0.0).astype(BF16)
    prior = jnp.dot(earlier, jnp.where(hot, 1.0, 0.0).astype(BF16), preferred_element_type=F32)
    source_col = column(source_row + 1.0)
    target_col = column(target_row + 1.0)
    picked = jnp.zeros((n, n), F32)
    for k in range(2):
        mine = hot & ((prior > 0.5) if k else (prior < 0.5))
        sent[k : k + 1, :] = jnp.sum(jnp.where(mine, source_col, 0.0), axis=0, keepdims=True).astype(I32)
        asked = column(jnp.sum(jnp.where(mine, target_col, 0.0), axis=0, keepdims=True))
        picked = jnp.where(lane == k, asked, picked)
    asking[...] = picked.astype(I32).reshape(asking.shape)


def slot_tables(owner, block_device, source_row, target_row):
    n = owner.shape[1]
    return pl.pallas_call(
        tables_kernel,
        in_specs=[whole(pltpu.HBM)] * 4,
        out_specs=[whole()] * 2,
        out_shape=[jax.ShapeDtypeStruct((2, n), I32), jax.ShapeDtypeStruct((n, 1, LANES), I32)],
        scratch_shapes=[VMEM((4, 1, n), I32), pltpu.SemaphoreType.DMA((4,))],
        compiler_params=params(61),
        cost_estimate=cost(4_000_000, 100_000),
        name="slot_tables",
    )(owner, block_device, source_row, target_row)


def begin(copies):
    for copy in copies:
        copy.start()


def finish(copies):
    for copy in copies:
        copy.wait()


def gather_kernel(
    sent_in, asked_in, flow_in, message_out, tables_out, flow, sent, asked, tables, table, message, sems, out_sems
):
    n = message.shape[0]
    copies = [
        pltpu.make_async_copy(asked_in, asked, sems.at[4]),
        pltpu.make_async_copy(sent_in, sent, sems.at[0]),
        pltpu.make_async_copy(flow_in, flow, sems.at[1]),
    ]
    begin(copies)
    eye = lax.broadcasted_iota(I32, (n, n), 0) == lax.broadcasted_iota(I32, (n, n), 1)
    copies[0].wait()
    columns = asked[...].reshape(n, LANES).astype(F32)
    for k in range(2):
        tables[k : k + 1, :] = jnp.sum(jnp.where(eye, columns[:, k : k + 1], 0.0), axis=0, keepdims=True).astype(I32)
    to_scalar = pltpu.make_async_copy(tables, table, sems.at[2])
    to_scalar.start()
    finish(copies[1:])

    stores = [pltpu.make_async_copy(tables, tables_out, sems.at[3])]
    stores[0].start()
    to_scalar.wait()

    def step(d, carry):
        for part, source in enumerate((sent, table)):
            for k in range(2):
                row = jnp.maximum(source[k, d] - 1, 0)
                for h in range(2):
                    start = 28 * part + 14 * k + NV * h
                    message[d, start : start + NV, :] = flow[row, :, LANES * h : LANES * (h + 1)]
        return carry

    size = n // CHUNKS
    for c in range(CHUNKS):
        lax.fori_loop(c * size, (c + 1) * size, step, 0, unroll=4)
        part = pl.ds(c * size, size)
        stores.append(pltpu.make_async_copy(message.at[part], message_out.at[part], out_sems.at[c]))
        stores[-1].start()
    finish(stores)


def gather(sent, asked, flow):
    devices = asked.shape[0]
    message = (devices, 8 * NV, LANES)
    return pl.pallas_call(
        gather_kernel,
        in_specs=[whole(pltpu.HBM)] * 3,
        out_specs=[whole(pltpu.HBM)] * 2,
        out_shape=[jax.ShapeDtypeStruct(message, F32), jax.ShapeDtypeStruct((2, devices), I32)],
        scratch_shapes=[
            VMEM(flow.shape, F32),
            pltpu.SMEM((2, devices), I32),
            VMEM(asked.shape, I32),
            VMEM((2, devices), I32),
            pltpu.SMEM((2, devices), I32),
            VMEM(message, F32),
            pltpu.SemaphoreType.DMA((5,)),
            pltpu.SemaphoreType.DMA((CHUNKS,)),
        ],
        compiler_params=params(58),
        cost_estimate=cost(1_000_000, 6_000_000),
        name="gather",
    )(sent, asked, flow)


def coupled(state, row, coef, mix):
    lane = lax.broadcasted_iota(I32, (8, LANES), 1)
    parts = []
    for direction in range(4):
        factor = coef(direction)
        for v in range(NV):
            if direction < 2:
                first = row + 2 * direction - 1
                pair = [state[2 * v + h, pl.ds(first, 8), :] for h in range(2)]
            else:
                mid = [state[2 * v + h, pl.ds(row, 8), :] for h in range(2)]
                if direction == 2:
                    left, right = (pltpu.roll(m, 1, 1) for m in mid)
                    pair = [jnp.where(lane == 0, 0.0, left), jnp.where(lane == 0, left, right)]
                else:
                    left, right = (pltpu.roll(m, LANES - 1, 1) for m in mid)
                    pair = [jnp.where(lane == LANES - 1, right, left), jnp.where(lane == LANES - 1, 0.0, right)]
            parts.append(factor * jnp.concatenate(pair, axis=1))
    cells = jnp.concatenate(parts, axis=0)
    high = cells.astype(BF16)
    low = (cells - high.astype(F32)).astype(BF16)
    dot = lambda a, b: jnp.dot(a, b, preferred_element_type=F32)
    return dot(mix[0], high) + dot(mix[1], high) + dot(mix[0], low)


def apply_inv(inv, cells):
    out = []
    for i in range(NV):
        total = None
        for j in range(NV):
            term = inv(i, j) * cells[j]
            total = term if j == 0 else total + term
        out.append(total)
    return out


def first_kernel(
    place, jac, flow, mix, halo_a, halo_b, right, coef, inv, packed_out, inv_out, operators, state, packed, blocks, sems
):
    rows = 8 * TILES
    steps = flow.shape[1] // rows
    even, ahead, behind = (place[0, i] == 1 for i in range(3))
    reads, writes = [], []
    for c in range(steps):
        part = pl.ds(rows * c, rows)
        reads.append(
            [
                pltpu.make_async_copy(right.at[:, part, :], packed.at[c, NV : 2 * NV], sems.at[0, c]),
                pltpu.make_async_copy(coef.at[:, part, :], packed.at[c, 2 * NV : PACKED], sems.at[1, c]),
                pltpu.make_async_copy(inv.at[:, :, part, :], blocks.at[c], sems.at[2, c]),
            ]
        )
        begin(reads[c])
    for n in range(2 * NV):
        v, h = divmod(n, 2)
        a, b = halo_a[n : n + 1, :], halo_b[n : n + 1, :]
        state[n, 7:8, :] = jnp.where(ahead, jnp.where(even, b, a), 0.0)
        state[n, 8 + rows * steps : 9 + rows * steps, :] = jnp.where(behind, jnp.where(even, a, b), 0.0)
        state[n, 8 : 8 + rows * steps, :] = flow[v, :, LANES * h : LANES * (h + 1)]

    for c in range(steps):
        finish(reads[c])

        def step(k, carry, c=c):
            here = pl.ds(pl.multiple_of(8 * k, 8), 8)
            row = pl.multiple_of(rows * c + 8 + 8 * k, 8)
            sums = coupled(state, row, lambda d: packed[c, 2 * NV + d, here, :], mix)
            for v in range(NV):
                packed[c, v, here, :] = packed[c, NV + v, here, :] - sums[8 * v : 8 * v + 8, :]
            return carry

        lax.fori_loop(0, TILES, step, 0)
        writes += [
            pltpu.make_async_copy(packed.at[c], packed_out.at[c], sems.at[3, c]),
            pltpu.make_async_copy(blocks.at[c], inv_out.at[c], sems.at[4, c]),
        ]
        begin(writes[-2:])
    for g, (there, c, row) in enumerate(((ahead, 0, 0), (behind, steps - 1, rows - 1))):
        factor = jnp.where(there, packed[c, 2 * NV + g, row : row + 1, :], 0.0)
        for i in range(NV):
            weights = [factor * blocks[c, i, k, row : row + 1, :] for k in range(NV)]
            for j in range(NV):
                total = jac[NV * NV * g + j] * weights[0]
                for k in range(1, NV):
                    total = total + jac[NV * (NV * g + k) + j] * weights[k]
                operators[g, j, i : i + 1, :] = total
    finish(writes)


def first_sum(place, jac, flow, right, coef, mix, halo_a, halo_b, inv):
    rows = flow.shape[1]
    steps = rows // (8 * TILES)
    packed = (steps, PACKED, 8 * TILES, COLS)
    blocks = (steps, NV, NV, 8 * TILES, COLS)
    return pl.pallas_call(
        first_kernel,
        in_specs=[SMEM] * 2 + [whole()] * 4 + [whole(pltpu.HBM)] * 3,
        out_specs=[whole(pltpu.HBM)] * 2 + [whole()],
        out_shape=[jax.ShapeDtypeStruct(s, F32) for s in (packed, blocks, (2, NV, 8, COLS))],
        scratch_shapes=[
            VMEM((2 * NV, rows + 16, LANES), F32),
            VMEM(packed, F32),
            VMEM(blocks, F32),
            pltpu.SemaphoreType.DMA((5, steps)),
        ],
        compiler_params=params(61),
        cost_estimate=cost(30_000_000, 40_000_000),
        name="first_sum",
    )(place, jac, flow, mix, halo_a, halo_b, right, coef, inv)


def finish_kernel(
    asked_in,
    sent_in,
    place_in,
    turn_in,
    message_in,
    packed_in,
    inv_in,
    out,
    edge_a_out,
    edge_b_out,
    rims_out,
    asked,
    sent,
    place,
    turn,
    message,
    add_left,
    add_right,
    sub_left,
    sub_right,
    packed,
    inv,
    above,
    below,
    ends,
    done,
    edge_a,
    edge_b,
    message_sems,
    sems,
    out_sems,
    small_sems,
):
    steps = packed_in.shape[0]
    rows = 8 * TILES
    count = message.shape[0] // CHUNKS
    plus, minus = (add_left, add_right), (sub_left, sub_right)

    def load(c):
        part = pl.ds(c * count, count)
        return pltpu.make_async_copy(message_in.at[part], message.at[part], message_sems.at[c])

    def fetch(c):
        return [
            pltpu.make_async_copy(packed_in.at[c], packed.at[c + 1], sems.at[0, c]),
            pltpu.make_async_copy(inv_in.at[c], inv.at[c + 1], sems.at[1, c]),
        ]

    def store(c):
        part = pl.ds(pl.multiple_of(rows * c, rows), rows)
        return pltpu.make_async_copy(done.at[c + 1], out.at[:, part, :], out_sems.at[c])

    pairs = ((asked_in, asked), (sent_in, sent), (place_in, place), (turn_in, turn))
    small = [pltpu.make_async_copy(src, dst, small_sems.at[i]) for i, (src, dst) in enumerate(pairs)]
    begin(small)
    begin([load(c) for c in range(CHUNKS)])
    begin(fetch(0))

    def clear(g, carry):
        for ref in plus + minus:
            ref[pl.ds(pl.multiple_of(64 * g, 64), 64), :] = jnp.zeros((64, LANES), F32)
        return carry

    lax.fori_loop(0, add_left.shape[0] // 64, clear, 0)
    for n in range(2 * NV):
        above[n, rows : rows + 8, :] = jnp.zeros((8, LANES), F32)
        below[n, 8 + rows * (steps + 1) : 16 + rows * (steps + 1), :] = jnp.zeros((8, LANES), F32)

    def scatter(d, carry):
        for k in range(2):
            for part, (table, refs) in enumerate(((asked, plus), (sent, minus))):
                row = pl.multiple_of(8 * table[k, d], 8)
                for h, ref in enumerate(refs):
                    first = 28 * part + 14 * k + NV * h
                    ref[pl.ds(row, NV), :] += message[d, first : first + NV, :]
        return carry

    finish(small)
    for c in range(CHUNKS):
        load(c).wait()
        if c in (2, 6):
            begin(fetch(1 if c == 2 else 2))
        lax.fori_loop(c * count, (c + 1) * count, scatter, 0, unroll=4)

    lane = lax.broadcasted_iota(I32, (8, COLS), 1)

    def sweep_one(c, k):
        here = slice(8 * k, 8 * k + 8)
        base = pl.multiple_of(64 * TILES * c, 64)
        groups = [pl.ds(base + 64 * k + 8 + v, 8, stride=8) for v in range(NV)]
        source = [jnp.concatenate([p[g, :] - m[g, :] for p, m in zip(plus, minus)], axis=1) for g in groups]
        cells = [packed[c + 1, v, here, :] + source[v] for v in range(NV)]
        relaxed = apply_inv(lambda i, j: inv[c + 1, i, j, here, :], cells)
        if k in (0, TILES - 1):
            end = jnp.minimum(c, 1) if k == 0 else 2
            for v in range(NV):
                ends[end, v] = relaxed[v]
        wide = jnp.concatenate(relaxed + [jnp.zeros((8, COLS), F32)], axis=0)
        high = wide.astype(BF16)
        low = (wide - high.astype(F32)).astype(BF16)
        mixed = jnp.dot(turn[...], jnp.concatenate([high, high, low], axis=0), preferred_element_type=F32)
        piece = lambda d, v: mixed[8 * (NV * d + v) : 8 * (NV * d + v) + 8, :]
        first = pl.multiple_of(rows * (c + 1), rows)
        for v in range(NV):
            for h in range(2):
                half = slice(LANES * h, LANES * (h + 1))
                above[2 * v + h, pl.ds(first + 8 * k + 8, 8), :] = piece(0, v)[:, half]
                below[2 * v + h, pl.ds(first + 8 * k + 8, 8), :] = piece(1, v)[:, half]
            west = jnp.where(lane == 0, 0.0, pltpu.roll(piece(2, v), 1, 1))
            east = jnp.where(lane == COLS - 1, 0.0, pltpu.roll(piece(3, v), COLS - 1, 1))
            share = packed[c + 1, 2 * NV + 2, here, :] * west + packed[c + 1, 2 * NV + 3, here, :] * east
            packed[c + 1, NV + v, here, :] = packed[c + 1, NV + v, here, :] + source[v] - share

    def sweep_two(c, k):
        c, k = (c, k - 1) if k else (c - 1, TILES - 1)
        here = slice(8 * k, 8 * k + 8)
        first = rows * (c + 1)
        cells = []
        for v in range(NV):
            north, south = (
                jnp.concatenate([ref[2 * v + h, pl.ds(first + 8 * k + 8 + shift, 8), :] for h in range(2)], axis=1)
                for ref, shift in ((above, -1), (below, 1))
            )
            share = packed[c + 1, 2 * NV, here, :] * north + packed[c + 1, 2 * NV + 1, here, :] * south
            cells.append(packed[c + 1, NV + v, here, :] - share)
        relaxed = apply_inv(lambda i, j: inv[c + 1, i, j, here, :], cells)
        for v in range(NV):
            done[c + 1, v, here, :] = relaxed[v]

    def step(c, carry):
        finish(fetch(c))

        @pl.when(c + 3 < steps)
        def _():
            begin(fetch(c + 3))

        for k in range(0, TILES, 2):
            sweep_one(c, k)
            sweep_one(c, k + 1)
            sweep_two(c, k)
            sweep_two(c, k + 1)

        @pl.when(c > 0)
        def _():
            store(c - 1).start()

        return carry

    lax.fori_loop(0, steps, step, 0)
    sweep_two(steps, 0)
    store(steps - 1).start()
    even = place[0, 0] == 1
    for v in range(NV):
        top, bottom = ends[0, v, 0:1, :], ends[2, v, 7:8, :]
        out_a, out_b = jnp.where(even, bottom, top), jnp.where(even, top, bottom)
        for h in range(2):
            n = 2 * v + h
            edge_a[n : n + 1, :] = out_a[:, LANES * h : LANES * (h + 1)]
            edge_b[n : n + 1, :] = out_b[:, LANES * h : LANES * (h + 1)]
    edges = [
        pltpu.make_async_copy(edge_a, edge_a_out, small_sems.at[4]),
        pltpu.make_async_copy(edge_b, edge_b_out, small_sems.at[5]),
        pltpu.make_async_copy(done.at[1, :, 0:8, :], rims_out.at[0], small_sems.at[6]),
        pltpu.make_async_copy(done.at[steps, :, rows - 8 : rows, :], rims_out.at[1], small_sems.at[7]),
    ]
    begin(edges)
    for c in range(steps):
        store(c).wait()
    finish(edges)


def finish_sweeps(asked, sent, place, turn, message, packed, inv):
    steps = packed.shape[0]
    rows = 8 * TILES * steps
    sums = VMEM((8 * (rows + 8), LANES), F32)
    padded = VMEM((2 * NV, rows + 8 * TILES + 16, LANES), F32)
    slab = (NV, rows, COLS)
    edge = (2 * NV, LANES)
    return pl.pallas_call(
        finish_kernel,
        in_specs=[whole(pltpu.HBM)] * 7,
        out_specs=[whole(pltpu.HBM)] * 4,
        out_shape=[jax.ShapeDtypeStruct(s, F32) for s in (slab, edge, edge, (2, NV, 8, COLS))],
        scratch_shapes=[pltpu.SMEM(a.shape, I32) for a in (asked, sent, place)]
        + [VMEM(turn.shape, BF16), VMEM(message.shape, F32)]
        + [sums] * 4
        + [VMEM((steps + 1,) + a.shape[1:], F32) for a in (packed, inv)]
        + [padded] * 2
        + [VMEM((3, NV, 8, COLS), F32), VMEM((steps + 1, NV, 8 * TILES, COLS), F32)]
        + [VMEM((2 * NV, LANES), F32)] * 2
        + [pltpu.SemaphoreType.DMA(s) for s in ((CHUNKS,), (2, steps), (steps,), (8,))],
        compiler_params=params(61),
        cost_estimate=cost(45_000_000, 24_000_000),
        name="finish_sweeps",
    )(asked, sent, place, turn, message, packed, inv)


def edge_kernel(place, relaxed, rims, operators, halo_a, halo_b, out, ends, sems):
    even = place[0, 0] == 1
    writes = []
    for g, (first, row) in enumerate(((0, 0), (out.shape[1] - 8, 7))):
        use_a = even if g else jnp.logical_not(even)
        change = None
        for j in range(NV):
            halves = [jnp.where(use_a, halo_a[n : n + 1, :], halo_b[n : n + 1, :]) for n in (2 * j, 2 * j + 1)]
            term = operators[g, j] * jnp.concatenate(halves, axis=1)
            change = term if j == 0 else change + term
        ends[g] = rims[g]
        for v in range(NV):
            ends[g, v, row : row + 1, :] = rims[g, v, row : row + 1, :] - change[v : v + 1, :]
        writes.append(pltpu.make_async_copy(ends.at[g], out.at[:, pl.ds(first, 8), :], sems.at[g]))
        writes[g].start()
    finish(writes)


def edge_rows(place, relaxed, rims, operators, halo_a, halo_b):
    return pl.pallas_call(
        edge_kernel,
        in_specs=[SMEM, whole(pltpu.HBM)] + [whole()] * 4,
        out_specs=whole(pltpu.HBM),
        out_shape=jax.ShapeDtypeStruct(relaxed.shape, F32),
        scratch_shapes=[VMEM((2, NV, 8, COLS), F32), pltpu.SemaphoreType.DMA((2,))],
        input_output_aliases={1: 0},
        compiler_params=params(24),
        cost_estimate=cost(100_000, 400_000),
        name="edge_rows",
    )(place, relaxed, rims, operators, halo_a, halo_b)


def hold_kernel(rims_in, rims):
    rims[...] = rims_in[...]


def hold(rims):
    return pl.pallas_call(
        hold_kernel,
        in_specs=[whole()],
        out_specs=whole(),
        out_shape=jax.ShapeDtypeStruct(rims.shape, F32),
        compiler_params=params(24),
        cost_estimate=cost(100_000, 8_000_000),
        name="hold",
    )(rims)


def exchange(edge_a, edge_b):
    zones, size = lax.axis_size("zone"), lax.axis_size("blk")
    pairs_a = [(i, i ^ 1) for i in range(size)]
    pairs_b = []
    for z in range(zones):
        for i in range(size):
            other, j = z, i - 1 if i % 2 == 0 else i + 1
            if not 0 <= j < size:
                other, j = z ^ 1, i
            pairs_b.append((z * size + i, other * size + j))
    return lax.ppermute(edge_a, "blk", pairs_a), lax.ppermute(edge_b, AXES, pairs_b)


def split(full):
    high = lax.reduce_precision(full, exponent_bits=8, mantissa_bits=7)
    return high.astype(BF16), (full - high).astype(BF16)


def mixing(face_jacobian):
    wide = jnp.transpose(face_jacobian, (1, 0, 2)).reshape(NV, 4 * NV)
    return jnp.stack(split((wide[:, None, :, None] * jnp.eye(8, dtype=F32)[None, :, None, :]).reshape(8 * NV, 32 * NV)))


def turning(face_jacobian):
    tall = jnp.pad(face_jacobian.reshape(4 * NV, NV), ((0, 0), (0, 1)))
    high, low = split((tall[:, None, :, None] * jnp.eye(8, dtype=F32)[None, :, None, :]).reshape(32 * NV, 64))
    return jnp.concatenate([high, low, high], axis=1)


def body(flow_state, right_side, inv_diag, face_coef, face_jacobian, hole_owner, source_row, target_row, block_device):
    flow = jnp.transpose(flow_state[0], (1, 0, 2))
    right = jnp.transpose(right_side[0], (1, 0, 2))
    inv = jnp.transpose(inv_diag[0], (1, 2, 0, 3))
    rows = flow.shape[1]
    slab = lax.axis_index("blk")
    even = slab % 2 == 0
    flags = jnp.stack([even, slab > 0, slab < lax.axis_size("blk") - 1]).astype(I32)
    place = jnp.pad(flags, (0, LANES - 3)).reshape(1, LANES)
    as_row = lambda a: a.reshape(1, -1)
    sent, asking = slot_tables(as_row(hole_owner), as_row(block_device), as_row(source_row), as_row(target_row))
    asked = lax.all_to_all(asking, AXES, split_axis=0, concat_axis=0, tiled=True)
    top, bottom = flow[:, 0].reshape(2 * NV, LANES), flow[:, rows - 1].reshape(2 * NV, LANES)
    halo_a, halo_b = exchange(jnp.where(even, bottom, top), jnp.where(even, top, bottom))
    asked, halo_a, halo_b = lax.optimization_barrier((asked, halo_a, halo_b))
    message, asked = gather(sent, asked, flow_state[0])
    message = lax.all_to_all(message, AXES, split_axis=0, concat_axis=0, tiled=True)

    coef = jnp.transpose(face_coef[0], (1, 0, 2))
    mix = mixing(face_jacobian)
    jac = face_jacobian.reshape(-1)
    packed, blocks, operators = first_sum(place, jac, flow, right, coef, mix, halo_a, halo_b, inv)
    relaxed, edge_a, edge_b, rims = finish_sweeps(
        asked, sent, place, turning(face_jacobian), message, packed, blocks
    )
    halo_a, halo_b = exchange(edge_a, edge_b)
    relaxed = edge_rows(place, relaxed, hold(rims), operators, halo_a, halo_b)
    return jnp.transpose(relaxed, (1, 0, 2))[None]


def solution(mesh):
    placed = (
        P("zone", "blk", None, None),
        P("zone", "blk", None, None),
        P("zone", "blk", None, None, None),
        P("zone", "blk", None, None),
        P(),
        P(("zone", "blk"), None),
        P(("zone", "blk")),
        P(("zone", "blk")),
        P(),
    )
    return jax.shard_map(
        body, mesh=mesh, in_specs=placed, out_specs=P("zone", "blk", None, None), check_vma=False
    )
```

```python
import jax
import jax.numpy as jnp
from jax import lax
from jax.experimental import pallas as pl
from jax.experimental.pallas import tpu as pltpu
from jax.sharding import PartitionSpec as P

NV = 7
LANES = 128
COLS = 2 * LANES
AXES = ("zone", "blk")
F32 = jnp.float32
BF16 = jnp.bfloat16
I32 = jnp.int32
VMEM = pltpu.VMEM
SMEM = pl.BlockSpec(memory_space=pltpu.SMEM)
MIB = 1 << 20
CHUNKS = 8
TILES = 4
PACKED = 2 * NV + 4


def params(mib):
    return pltpu.CompilerParams(vmem_limit_bytes=mib * MIB)


def cost(flops, bytes_accessed):
    return pl.CostEstimate(flops=flops, bytes_accessed=bytes_accessed, transcendentals=0)


def whole(space=VMEM):
    return pl.BlockSpec(memory_space=space)


def tables_kernel(owner_in, device_in, source_in, target_in, sent, asking, rows, sems):
    n = owner_in.shape[1]
    copies = [
        pltpu.make_async_copy(ref, rows.at[i], sems.at[i])
        for i, ref in enumerate((owner_in, device_in, source_in, target_in))
    ]
    for copy in copies:
        copy.start()
    for copy in copies:
        copy.wait()
    owner, block_device, source_row, target_row = (rows[i].astype(F32) for i in range(4))
    lane = lax.broadcasted_iota(I32, (n, n), 1)
    sub = lax.broadcasted_iota(I32, (n, n), 0)
    eye = lane == sub

    def column(row):
        return jnp.sum(jnp.where(eye, row, 0.0), axis=1, keepdims=True)

    number = lane.astype(F32)
    owner_col = column(owner)
    target = jnp.sum(jnp.where(owner_col == number, block_device, 0.0), axis=1, keepdims=True)
    hot = target == number
    earlier = jnp.where(lane < sub, 1.0, 0.0).astype(BF16)
    prior = jnp.dot(earlier, jnp.where(hot, 1.0, 0.0).astype(BF16), preferred_element_type=F32)
    source_col = column(source_row + 1.0)
    target_col = column(target_row + 1.0)
    picked = jnp.zeros((n, n), F32)
    for k in range(2):
        mine = hot & ((prior > 0.5) if k else (prior < 0.5))
        sent[k : k + 1, :] = jnp.sum(jnp.where(mine, source_col, 0.0), axis=0, keepdims=True).astype(I32)
        asked = column(jnp.sum(jnp.where(mine, target_col, 0.0), axis=0, keepdims=True))
        picked = jnp.where(lane == k, asked, picked)
    asking[...] = picked.astype(I32).reshape(asking.shape)


def slot_tables(owner, block_device, source_row, target_row):
    n = owner.shape[1]
    return pl.pallas_call(
        tables_kernel,
        in_specs=[whole(pltpu.HBM)] * 4,
        out_specs=[whole()] * 2,
        out_shape=[jax.ShapeDtypeStruct((2, n), I32), jax.ShapeDtypeStruct((n, 1, LANES), I32)],
        scratch_shapes=[VMEM((4, 1, n), I32), pltpu.SemaphoreType.DMA((4,))],
        compiler_params=params(61),
        cost_estimate=cost(4_000_000, 100_000),
        name="slot_tables",
    )(owner, block_device, source_row, target_row)


def begin(copies):
    for copy in copies:
        copy.start()


def finish(copies):
    for copy in copies:
        copy.wait()


def gather_kernel(
    sent_in, asked_in, flow_in, message_out, tables_out, flow, sent, asked, tables, table, message, sems, out_sems
):
    n = message.shape[0]
    copies = [
        pltpu.make_async_copy(asked_in, asked, sems.at[4]),
        pltpu.make_async_copy(sent_in, sent, sems.at[0]),
        pltpu.make_async_copy(flow_in, flow, sems.at[1]),
    ]
    begin(copies)
    eye = lax.broadcasted_iota(I32, (n, n), 0) == lax.broadcasted_iota(I32, (n, n), 1)
    copies[0].wait()
    columns = asked[...].reshape(n, LANES).astype(F32)
    for k in range(2):
        tables[k : k + 1, :] = jnp.sum(jnp.where(eye, columns[:, k : k + 1], 0.0), axis=0, keepdims=True).astype(I32)
    to_scalar = pltpu.make_async_copy(tables, table, sems.at[2])
    to_scalar.start()
    finish(copies[1:])

    stores = [pltpu.make_async_copy(tables, tables_out, sems.at[3])]
    stores[0].start()
    to_scalar.wait()

    def step(d, carry):
        for part, source in enumerate((sent, table)):
            for k in range(2):
                row = jnp.maximum(source[k, d] - 1, 0)
                for h in range(2):
                    start = 28 * part + 14 * k + NV * h
                    message[d, start : start + NV, :] = flow[row, :, LANES * h : LANES * (h + 1)]
        return carry

    size = n // CHUNKS
    for c in range(CHUNKS):
        lax.fori_loop(c * size, (c + 1) * size, step, 0, unroll=4)
        part = pl.ds(c * size, size)
        stores.append(pltpu.make_async_copy(message.at[part], message_out.at[part], out_sems.at[c]))
        stores[-1].start()
    finish(stores)


def gather(sent, asked, flow):
    devices = asked.shape[0]
    message = (devices, 8 * NV, LANES)
    return pl.pallas_call(
        gather_kernel,
        in_specs=[whole(pltpu.HBM)] * 3,
        out_specs=[whole(pltpu.HBM)] * 2,
        out_shape=[jax.ShapeDtypeStruct(message, F32), jax.ShapeDtypeStruct((2, devices), I32)],
        scratch_shapes=[
            VMEM(flow.shape, F32),
            pltpu.SMEM((2, devices), I32),
            VMEM(asked.shape, I32),
            VMEM((2, devices), I32),
            pltpu.SMEM((2, devices), I32),
            VMEM(message, F32),
            pltpu.SemaphoreType.DMA((5,)),
            pltpu.SemaphoreType.DMA((CHUNKS,)),
        ],
        compiler_params=params(58),
        cost_estimate=cost(1_000_000, 6_000_000),
        name="gather",
    )(sent, asked, flow)


def coupled(state, row, coef, mix):
    lane = lax.broadcasted_iota(I32, (8, LANES), 1)
    parts = []
    for direction in range(4):
        factor = coef(direction)
        for v in range(NV):
            if direction < 2:
                first = row + 2 * direction - 1
                pair = [state[2 * v + h, pl.ds(first, 8), :] for h in range(2)]
            else:
                mid = [state[2 * v + h, pl.ds(row, 8), :] for h in range(2)]
                if direction == 2:
                    left, right = (pltpu.roll(m, 1, 1) for m in mid)
                    pair = [jnp.where(lane == 0, 0.0, left), jnp.where(lane == 0, left, right)]
                else:
                    left, right = (pltpu.roll(m, LANES - 1, 1) for m in mid)
                    pair = [jnp.where(lane == LANES - 1, right, left), jnp.where(lane == LANES - 1, 0.0, right)]
            parts.append(factor * jnp.concatenate(pair, axis=1))
    cells = jnp.concatenate(parts, axis=0)
    high = cells.astype(BF16)
    low = (cells - high.astype(F32)).astype(BF16)
    dot = lambda a, b: jnp.dot(a, b, preferred_element_type=F32)
    return dot(mix[0], high) + dot(mix[1], high) + dot(mix[0], low)


def apply_inv(inv, cells):
    out = []
    for i in range(NV):
        total = None
        for j in range(NV):
            term = inv(i, j) * cells[j]
            total = term if j == 0 else total + term
        out.append(total)
    return out


def first_kernel(
    place, jac, flow, mix, halo_a, halo_b, right, coef, inv, packed_out, inv_out, operators, state, packed, blocks, sems
):
    rows = 8 * TILES
    steps = flow.shape[1] // rows
    even, ahead, behind = (place[0, i] == 1 for i in range(3))
    reads, writes = [], []
    for c in range(steps):
        part = pl.ds(rows * c, rows)
        reads.append(
            [
                pltpu.make_async_copy(right.at[:, part, :], packed.at[c, NV : 2 * NV], sems.at[0, c]),
                pltpu.make_async_copy(coef.at[:, part, :], packed.at[c, 2 * NV : PACKED], sems.at[1, c]),
                pltpu.make_async_copy(inv.at[:, :, part, :], blocks.at[c], sems.at[2, c]),
            ]
        )
        begin(reads[c])
    for n in range(2 * NV):
        v, h = divmod(n, 2)
        a, b = halo_a[n : n + 1, :], halo_b[n : n + 1, :]
        state[n, 7:8, :] = jnp.where(ahead, jnp.where(even, b, a), 0.0)
        state[n, 8 + rows * steps : 9 + rows * steps, :] = jnp.where(behind, jnp.where(even, a, b), 0.0)
        state[n, 8 : 8 + rows * steps, :] = flow[v, :, LANES * h : LANES * (h + 1)]

    for c in range(steps):
        finish(reads[c])

        def step(k, carry, c=c):
            here = pl.ds(pl.multiple_of(8 * k, 8), 8)
            row = pl.multiple_of(rows * c + 8 + 8 * k, 8)
            sums = coupled(state, row, lambda d: packed[c, 2 * NV + d, here, :], mix)
            for v in range(NV):
                packed[c, v, here, :] = packed[c, NV + v, here, :] - sums[8 * v : 8 * v + 8, :]
            return carry

        lax.fori_loop(0, TILES, step, 0)
        writes += [
            pltpu.make_async_copy(packed.at[c], packed_out.at[c], sems.at[3, c]),
            pltpu.make_async_copy(blocks.at[c], inv_out.at[c], sems.at[4, c]),
        ]
        begin(writes[-2:])
    for g, (there, c, row) in enumerate(((ahead, 0, 0), (behind, steps - 1, rows - 1))):
        factor = jnp.where(there, packed[c, 2 * NV + g, row : row + 1, :], 0.0)
        for i in range(NV):
            weights = [factor * blocks[c, i, k, row : row + 1, :] for k in range(NV)]
            for j in range(NV):
                total = jac[NV * NV * g + j] * weights[0]
                for k in range(1, NV):
                    total = total + jac[NV * (NV * g + k) + j] * weights[k]
                operators[g, j, i : i + 1, :] = total
    finish(writes)


def first_sum(place, jac, flow, right, coef, mix, halo_a, halo_b, inv):
    rows = flow.shape[1]
    steps = rows // (8 * TILES)
    packed = (steps, PACKED, 8 * TILES, COLS)
    blocks = (steps, NV, NV, 8 * TILES, COLS)
    return pl.pallas_call(
        first_kernel,
        in_specs=[SMEM] * 2 + [whole()] * 4 + [whole(pltpu.HBM)] * 3,
        out_specs=[whole(pltpu.HBM)] * 2 + [whole()],
        out_shape=[jax.ShapeDtypeStruct(s, F32) for s in (packed, blocks, (2, NV, 8, COLS))],
        scratch_shapes=[
            VMEM((2 * NV, rows + 16, LANES), F32),
            VMEM(packed, F32),
            VMEM(blocks, F32),
            pltpu.SemaphoreType.DMA((5, steps)),
        ],
        compiler_params=params(61),
        cost_estimate=cost(30_000_000, 40_000_000),
        name="first_sum",
    )(place, jac, flow, mix, halo_a, halo_b, right, coef, inv)


def finish_kernel(
    asked_in,
    sent_in,
    place_in,
    turn_in,
    message_in,
    packed_in,
    inv_in,
    out,
    edge_a_out,
    edge_b_out,
    rims_out,
    asked,
    sent,
    place,
    turn,
    message,
    add_left,
    add_right,
    sub_left,
    sub_right,
    packed,
    inv,
    above,
    below,
    ends,
    done,
    edge_a,
    edge_b,
    message_sems,
    sems,
    out_sems,
    small_sems,
):
    steps = packed_in.shape[0]
    rows = 8 * TILES
    count = message.shape[0] // CHUNKS
    plus, minus = (add_left, add_right), (sub_left, sub_right)

    def load(c):
        part = pl.ds(c * count, count)
        return pltpu.make_async_copy(message_in.at[part], message.at[part], message_sems.at[c])

    def fetch(c):
        return [
            pltpu.make_async_copy(packed_in.at[c], packed.at[c + 1], sems.at[0, c]),
            pltpu.make_async_copy(inv_in.at[c], inv.at[c + 1], sems.at[1, c]),
        ]

    def store(c):
        part = pl.ds(pl.multiple_of(rows * c, rows), rows)
        return pltpu.make_async_copy(done.at[c + 1], out.at[:, part, :], out_sems.at[c])

    pairs = ((asked_in, asked), (sent_in, sent), (place_in, place), (turn_in, turn))
    small = [pltpu.make_async_copy(src, dst, small_sems.at[i]) for i, (src, dst) in enumerate(pairs)]
    begin(small)
    begin([load(c) for c in range(CHUNKS)])
    begin(fetch(0))

    def clear(g, carry):
        for ref in plus + minus:
            ref[pl.ds(pl.multiple_of(64 * g, 64), 64), :] = jnp.zeros((64, LANES), F32)
        return carry

    lax.fori_loop(0, add_left.shape[0] // 64, clear, 0)
    for n in range(2 * NV):
        above[n, rows : rows + 8, :] = jnp.zeros((8, LANES), F32)
        below[n, 8 + rows * (steps + 1) : 16 + rows * (steps + 1), :] = jnp.zeros((8, LANES), F32)

    def scatter(d, carry):
        for k in range(2):
            for part, (table, refs) in enumerate(((asked, plus), (sent, minus))):
                row = pl.multiple_of(8 * table[k, d], 8)
                for h, ref in enumerate(refs):
                    first = 28 * part + 14 * k + NV * h
                    ref[pl.ds(row, NV), :] += message[d, first : first + NV, :]
        return carry

    finish(small)
    for c in range(CHUNKS):
        load(c).wait()
        if c in (0, 4):
            begin(fetch(1 if c == 0 else 2))
        lax.fori_loop(c * count, (c + 1) * count, scatter, 0, unroll=4)

    lane = lax.broadcasted_iota(I32, (8, COLS), 1)

    def sweep_one(c, k):
        here = slice(8 * k, 8 * k + 8)
        base = pl.multiple_of(64 * TILES * c, 64)
        groups = [pl.ds(base + 64 * k + 8 + v, 8, stride=8) for v in range(NV)]
        source = [jnp.concatenate([p[g, :] - m[g, :] for p, m in zip(plus, minus)], axis=1) for g in groups]
        cells = [packed[c + 1, v, here, :] + source[v] for v in range(NV)]
        relaxed = apply_inv(lambda i, j: inv[c + 1, i, j, here, :], cells)
        if k in (0, TILES - 1):
            end = jnp.minimum(c, 1) if k == 0 else 2
            for v in range(NV):
                ends[end, v] = relaxed[v]
        wide = jnp.concatenate(relaxed + [jnp.zeros((8, COLS), F32)], axis=0)
        high = wide.astype(BF16)
        low = (wide - high.astype(F32)).astype(BF16)
        mixed = jnp.dot(turn[...], jnp.concatenate([high, high, low], axis=0), preferred_element_type=F32)
        piece = lambda d, v: mixed[8 * (NV * d + v) : 8 * (NV * d + v) + 8, :]
        first = pl.multiple_of(rows * (c + 1), rows)
        for v in range(NV):
            for h in range(2):
                half = slice(LANES * h, LANES * (h + 1))
                above[2 * v + h, pl.ds(first + 8 * k + 8, 8), :] = piece(0, v)[:, half]
                below[2 * v + h, pl.ds(first + 8 * k + 8, 8), :] = piece(1, v)[:, half]
            west = jnp.where(lane == 0, 0.0, pltpu.roll(piece(2, v), 1, 1))
            east = jnp.where(lane == COLS - 1, 0.0, pltpu.roll(piece(3, v), COLS - 1, 1))
            share = packed[c + 1, 2 * NV + 2, here, :] * west + packed[c + 1, 2 * NV + 3, here, :] * east
            packed[c + 1, NV + v, here, :] = packed[c + 1, NV + v, here, :] + source[v] - share

    def sweep_two(c, k):
        c, k = (c, k - 1) if k else (c - 1, TILES - 1)
        here = slice(8 * k, 8 * k + 8)
        first = rows * (c + 1)
        cells = []
        for v in range(NV):
            north, south = (
                jnp.concatenate([ref[2 * v + h, pl.ds(first + 8 * k + 8 + shift, 8), :] for h in range(2)], axis=1)
                for ref, shift in ((above, -1), (below, 1))
            )
            share = packed[c + 1, 2 * NV, here, :] * north + packed[c + 1, 2 * NV + 1, here, :] * south
            cells.append(packed[c + 1, NV + v, here, :] - share)
        relaxed = apply_inv(lambda i, j: inv[c + 1, i, j, here, :], cells)
        for v in range(NV):
            done[c + 1, v, here, :] = relaxed[v]

    def step(c, carry):
        finish(fetch(c))

        @pl.when(c + 3 < steps)
        def _():
            begin(fetch(c + 3))

        for k in range(0, TILES, 2):
            sweep_one(c, k)
            sweep_one(c, k + 1)
            sweep_two(c, k)
            sweep_two(c, k + 1)

        @pl.when(c > 0)
        def _():
            store(c - 1).start()

        return carry

    lax.fori_loop(0, steps, step, 0)
    sweep_two(steps, 0)
    store(steps - 1).start()
    even = place[0, 0] == 1
    for v in range(NV):
        top, bottom = ends[0, v, 0:1, :], ends[2, v, 7:8, :]
        out_a, out_b = jnp.where(even, bottom, top), jnp.where(even, top, bottom)
        for h in range(2):
            n = 2 * v + h
            edge_a[n : n + 1, :] = out_a[:, LANES * h : LANES * (h + 1)]
            edge_b[n : n + 1, :] = out_b[:, LANES * h : LANES * (h + 1)]
    edges = [
        pltpu.make_async_copy(edge_a, edge_a_out, small_sems.at[4]),
        pltpu.make_async_copy(edge_b, edge_b_out, small_sems.at[5]),
        pltpu.make_async_copy(done.at[1, :, 0:8, :], rims_out.at[0], small_sems.at[6]),
        pltpu.make_async_copy(done.at[steps, :, rows - 8 : rows, :], rims_out.at[1], small_sems.at[7]),
    ]
    begin(edges)
    for c in range(steps):
        store(c).wait()
    finish(edges)


def finish_sweeps(asked, sent, place, turn, message, packed, inv):
    steps = packed.shape[0]
    rows = 8 * TILES * steps
    sums = VMEM((8 * (rows + 8), LANES), F32)
    padded = VMEM((2 * NV, rows + 8 * TILES + 16, LANES), F32)
    slab = (NV, rows, COLS)
    edge = (2 * NV, LANES)
    return pl.pallas_call(
        finish_kernel,
        in_specs=[whole(pltpu.HBM)] * 7,
        out_specs=[whole(pltpu.HBM)] * 4,
        out_shape=[jax.ShapeDtypeStruct(s, F32) for s in (slab, edge, edge, (2, NV, 8, COLS))],
        scratch_shapes=[pltpu.SMEM(a.shape, I32) for a in (asked, sent, place)]
        + [VMEM(turn.shape, BF16), VMEM(message.shape, F32)]
        + [sums] * 4
        + [VMEM((steps + 1,) + a.shape[1:], F32) for a in (packed, inv)]
        + [padded] * 2
        + [VMEM((3, NV, 8, COLS), F32), VMEM((steps + 1, NV, 8 * TILES, COLS), F32)]
        + [VMEM((2 * NV, LANES), F32)] * 2
        + [pltpu.SemaphoreType.DMA(s) for s in ((CHUNKS,), (2, steps), (steps,), (8,))],
        compiler_params=params(61),
        cost_estimate=cost(45_000_000, 24_000_000),
        name="finish_sweeps",
    )(asked, sent, place, turn, message, packed, inv)


def edge_kernel(place, relaxed, rims, operators, halo_a, halo_b, out, ends, sems):
    even = place[0, 0] == 1
    writes = []
    for g, (first, row) in enumerate(((0, 0), (out.shape[1] - 8, 7))):
        use_a = even if g else jnp.logical_not(even)
        change = None
        for j in range(NV):
            halves = [jnp.where(use_a, halo_a[n : n + 1, :], halo_b[n : n + 1, :]) for n in (2 * j, 2 * j + 1)]
            term = operators[g, j] * jnp.concatenate(halves, axis=1)
            change = term if j == 0 else change + term
        ends[g] = rims[g]
        for v in range(NV):
            ends[g, v, row : row + 1, :] = rims[g, v, row : row + 1, :] - change[v : v + 1, :]
        writes.append(pltpu.make_async_copy(ends.at[g], out.at[:, pl.ds(first, 8), :], sems.at[g]))
        writes[g].start()
    finish(writes)


def edge_rows(place, relaxed, rims, operators, halo_a, halo_b):
    return pl.pallas_call(
        edge_kernel,
        in_specs=[SMEM, whole(pltpu.HBM)] + [whole()] * 4,
        out_specs=whole(pltpu.HBM),
        out_shape=jax.ShapeDtypeStruct(relaxed.shape, F32),
        scratch_shapes=[VMEM((2, NV, 8, COLS), F32), pltpu.SemaphoreType.DMA((2,))],
        input_output_aliases={1: 0},
        compiler_params=params(24),
        cost_estimate=cost(100_000, 400_000),
        name="edge_rows",
    )(place, relaxed, rims, operators, halo_a, halo_b)


def hold_kernel(rims_in, rims):
    rims[...] = rims_in[...]


def hold(rims):
    return pl.pallas_call(
        hold_kernel,
        in_specs=[whole()],
        out_specs=whole(),
        out_shape=jax.ShapeDtypeStruct(rims.shape, F32),
        compiler_params=params(24),
        cost_estimate=cost(100_000, 8_000_000),
        name="hold",
    )(rims)


def exchange(edge_a, edge_b):
    zones, size = lax.axis_size("zone"), lax.axis_size("blk")
    pairs_a = [(i, i ^ 1) for i in range(size)]
    pairs_b = []
    for z in range(zones):
        for i in range(size):
            other, j = z, i - 1 if i % 2 == 0 else i + 1
            if not 0 <= j < size:
                other, j = z ^ 1, i
            pairs_b.append((z * size + i, other * size + j))
    return lax.ppermute(edge_a, "blk", pairs_a), lax.ppermute(edge_b, AXES, pairs_b)


def split(full):
    high = lax.reduce_precision(full, exponent_bits=8, mantissa_bits=7)
    return high.astype(BF16), (full - high).astype(BF16)


def mixing(face_jacobian):
    wide = jnp.transpose(face_jacobian, (1, 0, 2)).reshape(NV, 4 * NV)
    return jnp.stack(split((wide[:, None, :, None] * jnp.eye(8, dtype=F32)[None, :, None, :]).reshape(8 * NV, 32 * NV)))


def turning(face_jacobian):
    tall = jnp.pad(face_jacobian.reshape(4 * NV, NV), ((0, 0), (0, 1)))
    high, low = split((tall[:, None, :, None] * jnp.eye(8, dtype=F32)[None, :, None, :]).reshape(32 * NV, 64))
    return jnp.concatenate([high, low, high], axis=1)


def body(flow_state, right_side, inv_diag, face_coef, face_jacobian, hole_owner, source_row, target_row, block_device):
    flow = jnp.transpose(flow_state[0], (1, 0, 2))
    right = jnp.transpose(right_side[0], (1, 0, 2))
    inv = jnp.transpose(inv_diag[0], (1, 2, 0, 3))
    rows = flow.shape[1]
    slab = lax.axis_index("blk")
    even = slab % 2 == 0
    flags = jnp.stack([even, slab > 0, slab < lax.axis_size("blk") - 1]).astype(I32)
    place = jnp.pad(flags, (0, LANES - 3)).reshape(1, LANES)
    as_row = lambda a: a.reshape(1, -1)
    sent, asking = slot_tables(as_row(hole_owner), as_row(block_device), as_row(source_row), as_row(target_row))
    asked = lax.all_to_all(asking, AXES, split_axis=0, concat_axis=0, tiled=True)
    top, bottom = flow[:, 0].reshape(2 * NV, LANES), flow[:, rows - 1].reshape(2 * NV, LANES)
    halo_a, halo_b = exchange(jnp.where(even, bottom, top), jnp.where(even, top, bottom))
    asked, halo_a, halo_b = lax.optimization_barrier((asked, halo_a, halo_b))
    message, asked = gather(sent, asked, flow_state[0])
    message = lax.all_to_all(message, AXES, split_axis=0, concat_axis=0, tiled=True)

    coef = jnp.transpose(face_coef[0], (1, 0, 2))
    mix = mixing(face_jacobian)
    jac = face_jacobian.reshape(-1)
    packed, blocks, operators = first_sum(place, jac, flow, right, coef, mix, halo_a, halo_b, inv)
    relaxed, edge_a, edge_b, rims = finish_sweeps(
        asked, sent, place, turning(face_jacobian), message, packed, blocks
    )
    halo_a, halo_b = exchange(edge_a, edge_b)
    relaxed = edge_rows(place, relaxed, hold(rims), operators, halo_a, halo_b)
    return jnp.transpose(relaxed, (1, 0, 2))[None]


def solution(mesh):
    placed = (
        P("zone", "blk", None, None),
        P("zone", "blk", None, None),
        P("zone", "blk", None, None, None),
        P("zone", "blk", None, None),
        P(),
        P(("zone", "blk"), None),
        P(("zone", "blk")),
        P(("zone", "blk")),
        P(),
    )
    return jax.shard_map(
        body, mesh=mesh, in_specs=placed, out_specs=P("zone", "blk", None, None), check_vma=False
    )
```
